32 devices in a mesh: group: 4 (over y, x), ctx: 8 (over z, core).
Axes of the slice: x: 2, y: 2, z: 4, core: 2. Of those that a mesh axis runs over, the one named last changes fastest.
Arguments:
- tokens: bfloat16 [4, 1024, 2048], P('group', 'ctx'), may hold values from -8 to 8
- positions: int32 [4, 1024], P('group', 'ctx'), may hold values from 0 to 1023, as said below
- expert_ids: int32 [4, 1024, 8], P('group', 'ctx'), may hold values from 0 to 15, all different within a row; in each aligned block of 128 rows (0 to 127, 128 to 255, ..., all dimensions but the last counted through in order) at most 96 rows name the same one
- cotangent: bfloat16 [4, 1024, 2048], P('group', 'ctx'), may hold values from -6 to 6
- attention_gain: bfloat16 [2048], P('group'), may hold values from 0.5 to 1.5
- query_weight: bfloat16 [2048, 4096], P('group'), may hold values from -0.125 to 0.125
- key_weight: bfloat16 [2048, 512], P('group'), may hold values from -0.125 to 0.125
- value_weight: bfloat16 [2048, 512], P('group'), may hold values from -0.125 to 0.125
- output_weight: bfloat16 [2048, 4096], P('group'), may hold values from -2 to 2
- query_gain: bfloat16 [128], P('group'), may hold values from 0.099609375 to 1.8984375
- key_gain: bfloat16 [128], P('group'), may hold values from 0.099609375 to 1.8984375
- mixture_gain: bfloat16 [2048], P('group'), may hold values from 0.5 to 1.5
- router_weight: bfloat16 [2048, 16], P('group'), may hold values from -1 to 1
- gate_weight: bfloat16 [16, 2048, 768], P(None, 'group'), may hold values from -0.125 to 0.125
- up_weight: bfloat16 [16, 2048, 768], P(None, 'group'), may hold values from -0.125 to 0.125
- down_weight: bfloat16 [16, 2048, 768], P(None, 'group'), may hold values from -30 to 30
Outputs:
- layer_out: bfloat16 [4, 1024, 2048], P('group', 'ctx')
- tokens_grad: bfloat16 [4, 1024, 2048], P('group', 'ctx')
- attention_gain_grad: float32 [2048], P('group')
- query_weight_grad: float32 [2048, 4096], P('group')
- key_weight_grad: float32 [2048, 512], P('group')
- value_weight_grad: float32 [2048, 512], P('group')
- output_weight_grad: float32 [2048, 4096], P('group')
- query_gain_grad: float32 [128], P('group')
- key_gain_grad: float32 [128], P('group')
- mixture_gain_grad: float32 [2048], P('group')
- router_weight_grad: float32 [2048, 16], P('group')
- gate_weight_grad: float32 [16, 2048, 768], P(None, 'group')
- up_weight_grad: float32 [16, 2048, 768], P(None, 'group')
- down_weight_grad: float32 [16, 2048, 768], P(None, 'group')
The draws below stay inside these ranges and needn't reach their ends.
Inputs may be any that keep to these rules, and one draw needn't show every extreme that they name: positions restart at 0 where a document begins and rise by one from token to token inside it; every sequence begins a document at its first token and holds one to four documents. `expert_ids`: each token names 8 different experts; among the 128 tokens of one device (aligned blocks of rows) no expert is named by more than 96 tokens, a bound that some block reaches.
All inputs are finite; a program needn't handle non-finite values.
Results may differ from the reference program's by a relative error of at most 0.03.
Values may be sent and summed in bfloat16 or wider, within the bound.
A program may use at most 576 MiB of HBM per device.

```python
import math
import jax
import jax.numpy as jnp
import numpy as np
from jax import lax

D = 2048
HQ = 32
HK = 4
HD = 128
F = 768
TOPK = 8
EXPERTS = 16
TOK_DEV = 128
CAP = 96
SEQS = 4
LENGTH = 1024


def offset_vector(key):
    return 0.7 * jax.random.truncated_normal(jax.random.fold_in(key, 21), -3.0, 3.0, (D,), jnp.float32)


def quiet_experts(key):
    order = jax.random.permutation(jax.random.fold_in(key, 31), EXPERTS)
    return (order < max(EXPERTS // 4, 1)).astype(jnp.float32)


def draw_tokens(key, part):
    shift = offset_vector(key)
    noise = jax.random.truncated_normal(jax.random.fold_in(key, 22), -5.0, 5.0, (SEQS, LENGTH, D), jnp.float32)
    return (noise + shift[None, None, :]).astype(jnp.bfloat16)


def draw_router_weight(key, part):
    shift = offset_vector(key)
    quiet = quiet_experts(key)
    noise = 0.7 / D ** 0.5 * jax.random.truncated_normal(jax.random.fold_in(key, 23), -4.0, 4.0, (D, EXPERTS), jnp.float32)
    lean = -12.0 / D * shift[:, None] * quiet[None, :]
    return (noise + lean).astype(jnp.bfloat16)


def draw_down_weight(key, part):
    quiet = quiet_experts(key)
    scale = (1.0 + 39.0 * quiet) * (2.0 / F ** 0.5)
    values = jax.random.truncated_normal(jax.random.fold_in(key, 24), -4.0, 4.0, (EXPERTS, D, F), jnp.float32)
    return (values * scale[:, None, None]).astype(jnp.bfloat16)


def draw_positions(key, part):
    index_row = jnp.arange(LENGTH, dtype=jnp.int32)
    boundary = jax.random.randint(jax.random.fold_in(key, 11), (SEQS, 3), 1, LENGTH)
    single_seq = jax.random.randint(jax.random.fold_in(key, 12), (), 0, SEQS)
    seq_index = jnp.arange(SEQS, dtype=jnp.int32)[:, None]
    boundary = jnp.where(seq_index == single_seq, 0, boundary).astype(jnp.int32)
    begins = jnp.max(jnp.where(boundary[:, :, None] <= index_row[None, None, :], boundary[:, :, None], 0), axis=1)
    return (index_row[None, :] - begins).astype(jnp.int32)


def block_scale(rng, extent, pieces, least, top_value):
    loudness, own = 1.0, jax.random.fold_in(rng, 6)
    for axis_at, shards_of in pieces:
        steps = jnp.exp(jax.random.uniform(jax.random.fold_in(own, axis_at), (shards_of,), jnp.float32, least / len(pieces), top_value / len(pieces)))
        loudness = loudness * jnp.repeat(steps, extent[axis_at] // shards_of).reshape([-1 if axis == axis_at else 1 for axis in range(len(extent))])
    return loudness


def routed_block(key, own, number, rows, count, top, bound, slope):
    order = jax.random.permutation(key, count)
    packed, common = shares(count, rows * top, bound, slope, True), shares(count, rows * top, bound, slope, False)
    places = jnp.arange(count)

    def named(tallies, turn):
        used = int((tallies > 0).sum())
        fixed = max(1, used // 4)
        moved = fixed + (places - fixed + turn * (used - fixed)) % max(1, count - fixed)
        return jnp.zeros((count,), jnp.int32).at[order[jnp.where(places < fixed, places, moved)]].set(jnp.asarray(tallies, jnp.int32))

    tallies = jnp.where(number % 4 == 0, named(packed, number // 4), named(common, number - number // 4 - 1))
    mixed = jax.random.permutation(jax.random.fold_in(own, 3), count)
    giver, sink = mixed[0:count // 2 * 2:2], mixed[1:count // 2 * 2:2]
    slack = jnp.minimum(tallies[giver] - 1, bound - tallies[sink]) // 2
    slack = jnp.where((giver == order[0]) | (sink == order[0]) | (tallies[sink] == 0), 0, jnp.maximum(slack, 0))
    moved = jax.random.randint(jax.random.fold_in(own, 4), (count // 2,), 0, 1 << 20) % (slack + 1)
    tallies = tallies.at[giver].add(-moved).at[sink].add(moved)
    items = jnp.searchsorted(jnp.cumsum(tallies), jnp.arange(rows * top), side="right").astype(jnp.int32)
    listing = items.reshape(top, rows).T
    listing = listing[jax.random.permutation(jax.random.fold_in(own, 1), rows)]
    turn = jax.random.randint(jax.random.fold_in(own, 2), (rows, 1), 0, top)
    return jnp.take_along_axis(listing, (jnp.arange(top)[None, :] + turn) % top, axis=1)


def shares(amount, total, limit, slope, full):
    loads = [(1 << 20) // math.isqrt(rank ** slope) + 1 for rank in range(1, amount + 1)]
    largest = limit if full else min(limit, max(-(-total // amount), total * loads[0] // sum(loads)))
    least = 1 if total - largest >= amount - 1 else 0
    given, spare = [largest] + [least] * (amount - 1), total - largest - least * (amount - 1)
    while spare > 0:
        free = [i for i in range(1, amount) if given[i] < largest] or [i for i in range(1, amount) if given[i] < limit]
        whole, left = sum([loads[i] for i in free]), spare
        for i in free:
            addition = min(limit - given[i], max(1, left * loads[i] // whole), spare)
            given[i] = given[i] + addition
            spare = spare - addition
    return np.array(given)


def gaussian(rng, shape, spread, most, split=(), held_as=jnp.bfloat16):
    array = jax.random.normal(rng, shape, jnp.float32) * spread
    if len(split) > 0:
        array = block_scale(rng, shape, split, -0.22, 0.18) * array
    return jnp.clip(array, min=-most, max=most).astype(held_as)


def setup_inputs(seed: int = 0) -> dict:
    key_of = jax.random.split(jax.random.key(seed), 17)
    tokens = draw_tokens(jax.random.fold_in(key_of[16], 71), 0)
    positions = draw_positions(jax.random.fold_in(key_of[16], 71), 0)
    expert_ids_keys = jax.random.split(jax.random.fold_in(key_of[2], 1), SEQS * LENGTH // TOK_DEV)
    expert_ids_turns = jax.random.permutation(jax.random.fold_in(key_of[2], 3), SEQS * LENGTH // TOK_DEV)
    expert_ids = jax.vmap(lambda own, number: routed_block(jax.random.fold_in(key_of[2], 2), own, number, TOK_DEV, EXPERTS, TOPK, CAP, 1))(expert_ids_keys, expert_ids_turns).reshape((SEQS, LENGTH, TOPK))
    cotangent = gaussian(key_of[3], (SEQS, LENGTH, D), 1.0, 6.0, ((0, 4), (1, 8)))
    attention_gain = jnp.clip(1.0 + 0.1 * jax.random.normal(key_of[4], (D,), jnp.float32), 0.5, 1.5).astype(jnp.bfloat16)
    query_weight = gaussian(key_of[5], (D, HQ * HD), D ** -0.5, 0.125, ((0, 4),))
    key_weight = gaussian(key_of[6], (D, HK * HD), D ** -0.5, 0.125, ((0, 4),))
    value_weight = gaussian(key_of[7], (D, HK * HD), D ** -0.5, 0.125, ((0, 4),))
    output_weight = gaussian(key_of[8], (D, HQ * HD), 8 ** -0.5, 2.0, ((0, 4),))
    query_gain = jnp.clip(1.0 + 0.18 * jax.random.normal(key_of[9], (HD,), jnp.float32), 0.099609375, 1.8984375).astype(jnp.bfloat16)
    key_gain = jnp.clip(1.0 + 0.18 * jax.random.normal(key_of[10], (HD,), jnp.float32), 0.099609375, 1.8984375).astype(jnp.bfloat16)
    mixture_gain = jnp.clip(1.0 + 0.1 * jax.random.normal(key_of[11], (D,), jnp.float32), 0.5, 1.5).astype(jnp.bfloat16)
    router_weight = draw_router_weight(jax.random.fold_in(key_of[16], 71), 0)
    gate_weight = gaussian(key_of[13], (EXPERTS, D, F), D ** -0.5, 0.125, ((1, 4),))
    up_weight = gaussian(key_of[14], (EXPERTS, D, F), D ** -0.5, 0.125, ((1, 4),))
    down_weight = draw_down_weight(jax.random.fold_in(key_of[16], 71), 0)
    return {"tokens": tokens, "positions": positions, "expert_ids": expert_ids, "cotangent": cotangent, "attention_gain": attention_gain, "query_weight": query_weight, "key_weight": key_weight, "value_weight": value_weight, "output_weight": output_weight, "query_gain": query_gain, "key_gain": key_gain, "mixture_gain": mixture_gain, "router_weight": router_weight, "gate_weight": gate_weight, "up_weight": up_weight, "down_weight": down_weight}


EPS = 1e-06
ROPE_BASE = 1000000.0
FLOOR = -1e+30

@jax.custom_vjp
def low(v):
    return lax.optimization_barrier(v.astype(jnp.bfloat16)).astype(jnp.float32)

@jax.custom_vjp
def low_back(v):
    return v

def low_keep(v):
    return (low(v), None)

def low_pass(kept, grad):
    return (grad,)

def back_keep(v):
    return (v, None)

def back_low(kept, grad):
    return (low(grad),)
low.defvjp(low_keep, low_pass)
low_back.defvjp(back_keep, back_low)

def matmul(left, right):
    return jnp.dot(left, right, precision=lax.Precision.HIGHEST, preferred_element_type=jnp.float32)

def rms_norm(values, gains):
    return values * lax.rsqrt(lax.optimization_barrier(jnp.mean(values * values, axis=-1, keepdims=True)) + EPS) * gains

def rope_tables(position_row):
    frequency = ROPE_BASE ** (-2.0 * jnp.arange(HD // 2, dtype=jnp.float32) / HD)
    angles = position_row.astype(jnp.float32)[:, None] * frequency[None, :]
    angles = jnp.concatenate([angles, angles], axis=-1)[:, None, :]
    return (jnp.cos(angles), jnp.sin(angles))

def rotate(values, cosine, sine):
    middle = values.shape[-1] // 2
    turned = jnp.concatenate([-values[..., middle:], values[..., :middle]], axis=-1)
    return values * cosine + turned * sine

def attend(query, key_heads, value_heads, position_row):
    length = query.shape[0]
    block_size = 256 if length % 256 == 0 else length
    key_rep = jnp.repeat(key_heads, HQ // HK, axis=1)
    value_rep = jnp.repeat(value_heads, HQ // HK, axis=1)
    key_index = jnp.arange(length, dtype=jnp.int32)
    scaling = HD ** (-0.5)

    def one_block(number):
        block_start = (number * block_size).astype(jnp.int32)
        query_rows = lax.dynamic_slice_in_dim(query, block_start, block_size, 0)
        row_pos = lax.dynamic_slice_in_dim(position_row, block_start, block_size, 0)
        row_index = block_start + jnp.arange(block_size, dtype=jnp.int32)
        scores = low_back(jnp.einsum('qhd,khd->hqk', query_rows, key_rep, precision=lax.Precision.HIGHEST) * scaling)
        allowed = (key_index[None, :] <= row_index[:, None]) & (key_index[None, :] >= (row_index - row_pos)[:, None])
        masked = jnp.where(allowed[None], scores, FLOOR)
        highest = lax.optimization_barrier(jnp.max(masked, axis=-1, keepdims=True))
        expo = jnp.where(allowed[None], jnp.exp(masked - highest), 0.0)
        probs = expo / lax.optimization_barrier(jnp.sum(expo, axis=-1, keepdims=True))
        return jnp.einsum('hqk,khd->qhd', low(probs), value_rep, precision=lax.Precision.HIGHEST)
    result = lax.map(jax.checkpoint(one_block), jnp.arange(length // block_size, dtype=jnp.int32))
    return result.reshape(length, HQ, HD)

def forward(params, inputs, position_row, chosen_ids):
    attention_gain, query_weight, key_weight, value_weight, output_weight, query_gain, key_gain, mixture_gain, router_weight, gate_weight, up_weight, down_weight = params
    length = inputs.shape[0]
    normed = low(rms_norm(inputs, attention_gain))
    query_raw = low_back(matmul(normed, query_weight)).reshape(length, HQ, HD)
    key_raw = low_back(matmul(normed, key_weight)).reshape(length, HK, HD)
    value_raw = low_back(matmul(normed, value_weight)).reshape(length, HK, HD)
    cosine, sine = rope_tables(position_row)
    query = low(rotate(rms_norm(query_raw, query_gain), cosine, sine))
    key_heads = low(rotate(rms_norm(key_raw, key_gain), cosine, sine))
    value_heads = low(value_raw)
    mixed = attend(query, key_heads, value_heads, position_row).reshape(length, HQ * HD)
    mixed = low(low_back(mixed))
    attn_out = low_back(matmul(mixed, output_weight.T))
    hidden = inputs + attn_out
    moe_in = low(rms_norm(hidden, mixture_gain))
    logits = low_back(matmul(moe_in, router_weight))
    onehot = (chosen_ids[:, :, None] == jnp.arange(EXPERTS, dtype=jnp.int32)[None, None, :]).astype(jnp.float32)
    chosen = lax.optimization_barrier(jnp.sum(onehot * logits[:, None, :], axis=-1))
    expo = jnp.exp(chosen - lax.optimization_barrier(jnp.max(chosen, axis=-1, keepdims=True)))
    gates = expo / lax.optimization_barrier(jnp.sum(expo, axis=-1, keepdims=True))
    combine = lax.optimization_barrier(jnp.sum(gates[:, :, None] * onehot, axis=1))

    def expert(running, number):
        gate_val = low_back(matmul(moe_in, gate_weight[number]))
        up_val = low_back(matmul(moe_in, up_weight[number]))
        act = low(gate_val * lax.logistic(gate_val) * up_val)
        out_val = low_back(matmul(act, down_weight[number].T))
        weight_col = lax.dynamic_slice_in_dim(combine, number, 1, 1)
        return (running + weight_col * out_val, None)
    mixture, unused = lax.scan(jax.checkpoint(expert), jnp.zeros_like(hidden), jnp.arange(EXPERTS, dtype=jnp.int32))
    return hidden + mixture

def reference(tokens, positions, expert_ids, cotangent, attention_gain, query_weight, key_weight, value_weight, output_weight, query_gain, key_gain, mixture_gain, router_weight, gate_weight, up_weight, down_weight):
    params = tuple((w.astype(jnp.float32) for w in (attention_gain, query_weight, key_weight, value_weight, output_weight, query_gain, key_gain, mixture_gain, router_weight, gate_weight, up_weight, down_weight)))

    def one_sequence(running, item):
        seq_tokens, seq_pos, seq_ids, seq_cot = item

        def run(weights, inputs):
            return forward(weights, inputs, seq_pos, seq_ids)
        result, pull = jax.vjp(run, params, seq_tokens.astype(jnp.float32))
        weight_grads, input_grad = pull(seq_cot.astype(jnp.float32))
        running = jax.tree.map(lambda a, b: a + b, running, weight_grads)
        return (running, (result.astype(jnp.bfloat16), input_grad.astype(jnp.bfloat16)))
    zeros = jax.tree.map(jnp.zeros_like, params)
    grads, (layer_out, tokens_grad) = lax.scan(one_sequence, zeros, (tokens, positions, expert_ids, cotangent))
    return (layer_out, tokens_grad, grads[0], grads[1], grads[2], grads[3], grads[4], grads[5], grads[6], grads[7], grads[8], grads[9], grads[10], grads[11])
```

```python
import functools

import jax
import jax.numpy as jnp
from jax import lax
from jax.experimental import pallas as pl
from jax.experimental.pallas import tpu as pltpu
from jax.sharding import PartitionSpec as P

D = 2048
HQ = 32
HK = 4
HD = 128
F = 768
TOPK = 8
EXPERTS = 16
PAD = 128

EPS = 1e-06
ROPE_BASE = 1000000.0
FLOOR = -1e30
F32 = jnp.float32
BF16 = jnp.bfloat16


def rms_parts(values, gains):
    factor = lax.rsqrt(jnp.mean(values * values, axis=-1, keepdims=True) + EPS)
    return (values * factor * gains, factor)


def rms_back(values, factor, gains, gradient):
    weighted = gradient * gains
    inner = jnp.mean(weighted * values, axis=-1, keepdims=True)
    grad_values = factor * weighted - values * (factor * factor * factor) * inner
    return (grad_values, gradient * values * factor)


def dot(left, right):
    return jnp.dot(left, right, preferred_element_type=F32)


def dot_nt(left, right):
    return lax.dot_general(left, right, (((1,), (1,)), ((), ())), preferred_element_type=F32)


def dot_tn(left, right):
    return lax.dot_general(left, right, (((0,), (0,)), ((), ())), preferred_element_type=F32)


def rope_tables(position_row):
    frequency = ROPE_BASE ** (-2.0 * jnp.arange(HD // 2, dtype=F32) / HD)
    angles = position_row.astype(F32)[:, None] * frequency[None, :]
    cosine, sine = jnp.cos(angles), jnp.sin(angles)
    return (
        jnp.concatenate([cosine, cosine], axis=-1),
        jnp.concatenate([-sine, sine], axis=-1),
    )


def turn(values):
    return pltpu.roll(values, HD // 2, 1)


def normed_rope(raw, gains, cosine, sine):
    normed, factor = rms_parts(raw, gains)
    return (normed * cosine + turn(normed) * sine, factor)


def masked_scores(query, key, doc_start, first_row, columns):
    scores = dot_nt(query, key) * (HD**-0.5)
    rows = query.shape[0]
    row_index = first_row + lax.broadcasted_iota(jnp.int32, (rows, columns), 0)
    key_index = lax.broadcasted_iota(jnp.int32, (rows, columns), 1)
    allowed = (key_index <= row_index) & (key_index >= doc_start)
    return jnp.where(allowed, scores, FLOOR)


def attend_kernel(
    block, q_ref, kv_ref, doc_ref, cos_ref, sin_ref, qg_ref, kg_ref, out_ref, key_ref, val_ref
):
    length = kv_ref.shape[0]
    head, part = pl.program_id(0), pl.program_id(1)

    @pl.when((head == 0) & (part == 0))
    def _():
        key, unused = normed_rope(kv_ref[:, :HD], kg_ref[...], cos_ref[...], sin_ref[...])
        key_ref[...] = key.astype(BF16)
        val_ref[...] = kv_ref[:, HD:].astype(BF16)

    for number in range(length // block):

        @pl.when(part == number)
        def _():
            rows = pl.ds(number * block, block)
            columns = (number + 1) * block
            query, unused = normed_rope(q_ref[...], qg_ref[...], cos_ref[rows, :], sin_ref[rows, :])
            masked = masked_scores(
                query.astype(BF16), key_ref[:columns, :], doc_ref[...], number * block, columns
            )
            weights = jnp.exp(masked - jnp.max(masked, axis=-1, keepdims=True))
            total = jnp.sum(weights, axis=-1, keepdims=True)
            mixed = dot(weights.astype(BF16), val_ref[:columns, :])
            out_ref[...] = (mixed / total).astype(BF16)


def attend_back_kernel(
    block,
    q_ref,
    kv_ref,
    doc_ref,
    cos_ref,
    sin_ref,
    qg_ref,
    kg_ref,
    dm_ref,
    dq_ref,
    dkv_ref,
    qt_ref,
    kt_ref,
    key_ref,
    val_ref,
    dk_ref,
    dv_ref,
):
    length = kv_ref.shape[0]
    head, part = pl.program_id(0), pl.program_id(1)
    scaling = HD**-0.5

    @pl.when((head == 0) & (part == 0))
    def _():
        key, unused = normed_rope(kv_ref[:, :HD], kg_ref[...], cos_ref[...], sin_ref[...])
        key_ref[...] = key.astype(BF16)
        val_ref[...] = kv_ref[:, HD:].astype(BF16)
        dk_ref[...] = jnp.zeros_like(dk_ref)
        dv_ref[...] = jnp.zeros_like(dv_ref)
        qt_ref[...] = jnp.zeros_like(qt_ref)

    for number in range(length // block):

        @pl.when(part == number)
        def _():
            rows = pl.ds(number * block, block)
            columns = (number + 1) * block
            cosine, sine = cos_ref[rows, :], sin_ref[rows, :]
            raw = q_ref[...]
            query, factor = normed_rope(raw, qg_ref[...], cosine, sine)
            query = query.astype(BF16)
            key, value = key_ref[:columns, :], val_ref[:columns, :]
            upstream = dm_ref[...]
            masked = masked_scores(query, key, doc_ref[...], number * block, columns)
            weights = jnp.exp(masked - jnp.max(masked, axis=-1, keepdims=True))
            probs = weights / jnp.sum(weights, axis=-1, keepdims=True)
            prob_grad = dot_nt(upstream, value)
            delta = jnp.sum(probs * prob_grad, axis=-1, keepdims=True)
            score_grad = (probs * (prob_grad - delta)).astype(BF16)
            dk_ref[:columns, :] += dot_tn(score_grad, query)
            dv_ref[:columns, :] += dot_tn(probs.astype(BF16), upstream)
            rotated = dot(score_grad, key) * scaling
            query_grad = rotated * cosine - turn(rotated) * sine
            raw_grad, terms = rms_back(raw, factor, qg_ref[...], query_grad)
            dq_ref[...] = raw_grad.astype(BF16)
            qt_ref[...] += jnp.sum(terms, axis=0, keepdims=True)

    @pl.when((head == pl.num_programs(0) - 1) & (part == pl.num_programs(1) - 1))
    def _():
        raw = kv_ref[:, :HD]
        cosine, sine = cos_ref[...], sin_ref[...]
        unused, factor = rms_parts(raw, kg_ref[...])
        rotated = dk_ref[...] * scaling
        key_grad = rotated * cosine - turn(rotated) * sine
        raw_grad, terms = rms_back(raw, factor, kg_ref[...], key_grad)
        dkv_ref[:, :HD] = raw_grad
        dkv_ref[:, HD:] = dv_ref[...]
        kt_ref[...] = jnp.sum(terms, axis=0, keepdims=True)


def attention_specs(length, block):
    whole = lambda h, b: (0, 0)
    return [
        pl.BlockSpec((block, HD), lambda h, b: (b, h)),
        pl.BlockSpec((length, 2 * HD), whole),
        pl.BlockSpec((block, 1), lambda h, b: (b, 0)),
        pl.BlockSpec((length, HD), whole),
        pl.BlockSpec((length, HD), whole),
        pl.BlockSpec((1, HD), whole),
        pl.BlockSpec((1, HD), whole),
    ]


def attend(query_raw, kv_raw, doc_start, cosine, sine, query_gain, key_gain):
    length, width = query_raw.shape
    block = 256
    return pl.pallas_call(
        functools.partial(attend_kernel, block),
        out_shape=jax.ShapeDtypeStruct((length, width), BF16),
        grid_spec=pltpu.PrefetchScalarGridSpec(
            num_scalar_prefetch=0,
            grid=(width // HD, length // block),
            in_specs=attention_specs(length, block),
            out_specs=pl.BlockSpec((block, HD), lambda h, b: (b, h)),
            scratch_shapes=[pltpu.VMEM((length, HD), BF16), pltpu.VMEM((length, HD), BF16)],
        ),
        cost_estimate=pl.CostEstimate(
            flops=3 * length * length * width,
            bytes_accessed=length * width * 6,
            transcendentals=length * length * width // HD // 2,
        ),
        name="attend",
    )(query_raw, kv_raw, doc_start, cosine, sine, query_gain, key_gain)


def attend_back(query_raw, kv_raw, doc_start, cosine, sine, query_gain, key_gain, upstream):
    length, width = query_raw.shape
    block = 256
    whole = lambda h, b: (0, 0)
    return pl.pallas_call(
        functools.partial(attend_back_kernel, block),
        out_shape=(
            jax.ShapeDtypeStruct((length, width), BF16),
            jax.ShapeDtypeStruct((length, 2 * HD), F32),
            jax.ShapeDtypeStruct((1, HD), F32),
            jax.ShapeDtypeStruct((1, HD), F32),
        ),
        grid_spec=pltpu.PrefetchScalarGridSpec(
            num_scalar_prefetch=0,
            grid=(width // HD, length // block),
            in_specs=attention_specs(length, block)
            + [pl.BlockSpec((block, HD), lambda h, b: (b, h))],
            out_specs=(
                pl.BlockSpec((block, HD), lambda h, b: (b, h)),
                pl.BlockSpec((length, 2 * HD), whole),
                pl.BlockSpec((1, HD), whole),
                pl.BlockSpec((1, HD), whole),
            ),
            scratch_shapes=[
                pltpu.VMEM((length, HD), BF16),
                pltpu.VMEM((length, HD), BF16),
                pltpu.VMEM((length, HD), F32),
                pltpu.VMEM((length, HD), F32),
            ],
        ),
        cost_estimate=pl.CostEstimate(
            flops=7 * length * length * width,
            bytes_accessed=length * width * 8,
            transcendentals=length * length * width // HD // 2,
        ),
        name="attend_back",
    )(query_raw, kv_raw, doc_start, cosine, sine, query_gain, key_gain, upstream)


def ctx_place():
    here = lax.axis_index("ctx")
    return (here // 2, lax.rem(here, 2))


def peer(chip, core):
    return {"ctx": 2 * chip + core}


def greet(chips, owners=1):
    chip, core = ctx_place()
    group = lax.axis_index("group")
    barrier = pltpu.get_barrier_semaphore()
    pl.semaphore_signal(barrier, inc=1, device_id=peer(chip, 1 - core))

    @pl.when(chip > 0)
    def _():
        pl.semaphore_signal(barrier, inc=1, device_id=peer(chip - 1, core))

    @pl.when(chip < chips - 1)
    def _():
        pl.semaphore_signal(barrier, inc=1, device_id=peer(chip + 1, core))

    bits = owners.bit_length() - 1
    for bit in range(bits):
        pl.semaphore_signal(barrier, inc=1, device_id={"group": group ^ (1 << bit)})
    count = 1 + bits + (chip > 0).astype(jnp.int32) + (chip < chips - 1).astype(jnp.int32)
    pl.semaphore_wait(barrier, count)


class Gather:
    def __init__(self, chips, source, target, sems):
        self.chips, self.source, self.target = chips, source, target
        self.up, self.down, self.side, self.near, self.cross, self.local = sems
        self.chip, self.core = ctx_place()
        self.rows = source.shape[0]

    def block(self, chip, core):
        start = pl.multiple_of((2 * chip + core) * self.rows, self.rows)
        return self.target.at[pl.ds(start, self.rows)]

    def hop(self, origin, sem, arrive, device, own=False):
        return pltpu.make_async_remote_copy(
            src_ref=self.source if own else self.block(origin, self.core),
            dst_ref=self.block(origin, self.core),
            send_sem=sem.at[origin],
            recv_sem=arrive.at[origin],
            device_id=device,
        )

    def to_up(self, origin, own=False):
        return self.hop(origin, self.up, self.near, peer(self.chip + 1, self.core), own)

    def to_down(self, origin, own=False):
        return self.hop(origin, self.down, self.near, peer(self.chip - 1, self.core), own)

    def to_side(self, origin, own=False):
        return self.hop(origin, self.side, self.cross, peer(self.chip, 1 - self.core), own)

    def mine(self):
        return pltpu.make_async_copy(self.source, self.block(self.chip, self.core), self.local)

    def start(self):
        @pl.when(self.chip < self.chips - 1)
        def _():
            self.to_up(self.chip, True).start()

        @pl.when(self.chip > 0)
        def _():
            self.to_down(self.chip, True).start()

        self.to_side(self.chip, True).start()
        self.mine().start()

    def step(self, distance):
        below, above = self.chip - distance, self.chip + distance

        @pl.when(below >= 0)
        def _():
            self.to_up(below).wait_recv()

            @pl.when(self.chip < self.chips - 1)
            def _():
                self.to_up(below).start()

            self.to_side(below).start()

        @pl.when(above < self.chips)
        def _():
            self.to_down(above).wait_recv()

            @pl.when(self.chip > 0)
            def _():
                self.to_down(above).start()

            self.to_side(above).start()

    def finish(self):
        self.mine().wait()
        for origin in range(self.chips):
            pltpu.make_async_remote_copy(
                src_ref=self.source,
                dst_ref=self.block(origin, 1 - self.core),
                send_sem=self.side.at[origin],
                recv_sem=self.cross.at[origin],
                device_id=peer(self.chip, 1 - self.core),
            ).wait_recv()
            self.to_side(origin).wait_send()

            @pl.when((origin <= self.chip) & (self.chip < self.chips - 1))
            def _():
                self.to_up(origin).wait_send()

            @pl.when((origin >= self.chip) & (self.chip > 0))
            def _():
                self.to_down(origin).wait_send()


def gather_sems(chips):
    return [pltpu.SemaphoreType.DMA((chips,))] * 5 + [pltpu.SemaphoreType.DMA]


class Scatter:
    def __init__(self, chips, tile, refs):
        self.chips, self.tile = chips, tile
        self.give, self.take, self.send, self.low, self.high, *self.sems = refs
        self.chip, self.core = ctx_place()

    def side(self, target):
        return pltpu.make_async_remote_copy(
            src_ref=self.give.at[target],
            dst_ref=self.take.at[target],
            send_sem=self.sems[0].at[target],
            recv_sem=self.sems[1].at[target],
            device_id=peer(self.chip, 1 - self.core),
        )

    def up(self, target):
        return pltpu.make_async_remote_copy(
            src_ref=self.send.at[target],
            dst_ref=self.low.at[target],
            send_sem=self.sems[2].at[target],
            recv_sem=self.sems[3].at[target],
            device_id=peer(self.chip + 1, self.core),
        )

    def down(self, target):
        return pltpu.make_async_remote_copy(
            src_ref=self.send.at[target],
            dst_ref=self.high.at[target],
            send_sem=self.sems[2].at[target],
            recv_sem=self.sems[4].at[target],
            device_id=peer(self.chip - 1, self.core),
        )

    def start(self):
        last = self.chips - 1
        for target in sorted(range(self.chips), key=lambda t: min(t, last - t)):
            self.give[target] = self.tile(2 * target + 1 - self.core).astype(BF16)
            self.side(target).start()

    def pairs(self, out):
        last = self.chips - 1
        for target in sorted(range(self.chips), key=lambda t: min(t, last - t)):
            value = self.tile(2 * target + self.core)
            self.side(target).wait_recv()
            value = value + self.take[target].astype(F32)
            self.send[target] = value.astype(BF16)

            @pl.when(self.chip == target)
            def _():
                out[...] = value

            if target == last:

                @pl.when(self.chip == 0)
                def _():
                    self.up(target).start()

            if target == 0:

                @pl.when(self.chip == last)
                def _():
                    self.down(target).start()

    def step(self, number):
        first, final = number, self.chips - 1 - number

        @pl.when(final > self.chip)
        def _():
            @pl.when(self.chip > 0)
            def _():
                self.up(final).wait_recv()
                self.send[final] = (
                    self.send[final].astype(F32) + self.low[final].astype(F32)
                ).astype(BF16)

            @pl.when((self.chip > 0) | (number > 0))
            def _():
                self.up(final).start()

        @pl.when(first < self.chip)
        def _():
            @pl.when(self.chip < self.chips - 1)
            def _():
                self.down(first).wait_recv()
                self.send[first] = (
                    self.send[first].astype(F32) + self.high[first].astype(F32)
                ).astype(BF16)

            @pl.when((self.chip < self.chips - 1) | (number > 0))
            def _():
                self.down(first).start()

    def finish(self, out):
        for target in range(self.chips):

            @pl.when(self.chip == target)
            def _():
                if target > 0:
                    self.up(target).wait_recv()
                    out[...] += self.low[target].astype(F32)
                if target < self.chips - 1:
                    self.down(target).wait_recv()
                    out[...] += self.high[target].astype(F32)

        for target in range(self.chips):
            self.side(target).wait_send()

            @pl.when(self.chip != target)
            def _():
                self.up(target).wait_send()


def scatter_scratch(chips, rows, width):
    return [pltpu.VMEM((chips, rows, width), BF16)] * 5 + [pltpu.SemaphoreType.DMA((chips,))] * 5


def row_block(ref, block, rows):
    return ref[pl.ds(pl.multiple_of(block * rows, rows), rows), :]


class GroupGather:
    def __init__(self, owners, source, target, sems):
        self.owners, self.source, self.target = owners, source, target
        self.sent, self.got, self.local = sems
        self.group = lax.axis_index("group")
        self.rows = source.shape[0]
        self.bits = list(range(owners.bit_length() - 1))
        self.orders = (self.bits, self.bits[::-1])

    def piece(self, mask, half):
        start = (self.group ^ mask) * self.rows + half * (self.rows // 2)
        return self.target.at[pl.ds(pl.multiple_of(start, self.rows // 2), self.rows // 2)]

    def held(self, half, stage):
        masks = [0]
        for bit in self.orders[half][:stage]:
            masks += [mask | 1 << bit for mask in masks]
        return masks

    def hop(self, half, stage, mask):
        bit = self.orders[half][stage]
        source = self.piece(mask, half)
        if mask == 0:
            source = self.source.at[pl.ds(half * (self.rows // 2), self.rows // 2)]
        return pltpu.make_async_remote_copy(
            src_ref=source,
            dst_ref=self.piece(mask, half),
            send_sem=self.sent.at[half, stage * self.owners + mask],
            recv_sem=self.got.at[half, mask | 1 << bit],
            device_id={"group": self.group ^ (1 << bit)},
        )

    def mine(self):
        start = pl.multiple_of(self.group * self.rows, self.rows)
        return pltpu.make_async_copy(
            self.source, self.target.at[pl.ds(start, self.rows)], self.local
        )

    def start(self):
        for half in range(2):
            self.hop(half, 0, 0).start()
        self.mine().start()

    def step(self, stage):
        for half in range(2):
            for mask in self.held(half, stage):
                self.hop(half, stage, mask).wait_recv()
            if stage + 1 < len(self.bits):
                for mask in self.held(half, stage + 1):
                    self.hop(half, stage + 1, mask).start()

    def finish(self):
        self.mine().wait()
        for half in range(2):
            for stage in self.bits:
                for mask in self.held(half, stage):
                    self.hop(half, stage, mask).wait_send()


def group_gather_sems(owners):
    bits = owners.bit_length() - 1
    return [
        pltpu.SemaphoreType.DMA((2, bits * owners)),
        pltpu.SemaphoreType.DMA((2, owners)),
        pltpu.SemaphoreType.DMA,
    ]


class GroupScatter:
    def __init__(self, owners, part, out, refs):
        self.owners, self.part, self.out = owners, part, out
        self.land, (self.sent, self.got) = refs[:-2], refs[-2:]
        self.group = lax.axis_index("group")
        self.bits = list(range(owners.bit_length() - 1))
        self.orders = (self.bits, self.bits[::-1])
        self.rows, self.columns = out.shape[0], out.shape[1] // 2

    def kept(self, half, stage):
        done = self.orders[half][: stage + 1]
        return [r for r in range(self.owners) if not any(r >> bit & 1 for bit in done)]

    def place(self, half, stage, piece):
        if stage == 0:
            start = pl.multiple_of((self.group ^ piece) * self.rows, self.rows)
            return self.part.at[pl.ds(start, self.rows), pl.ds(half * self.columns, self.columns)]
        return self.land[stage - 1].at[half, self.kept(half, stage - 1).index(piece)]

    def hop(self, half, stage, piece):
        bit = self.orders[half][stage]
        at = self.kept(half, stage).index(piece)
        return pltpu.make_async_remote_copy(
            src_ref=self.place(half, stage, piece | 1 << bit),
            dst_ref=self.land[stage].at[half, at],
            send_sem=self.sent.at[half, stage * self.owners + piece],
            recv_sem=self.got.at[half, stage * self.owners + piece],
            device_id={"group": self.group ^ (1 << bit)},
        )

    def begin(self, half, stage):
        for piece in self.kept(half, stage):
            self.hop(half, stage, piece).start()

    def start(self):
        for half in range(2):
            self.begin(half, 0)

    def step(self, stage):
        for half in range(2):
            for piece in self.kept(half, stage):
                self.hop(half, stage, piece).wait_recv()
                mine = self.place(half, stage, piece)
                theirs = self.land[stage].at[half, self.kept(half, stage).index(piece)]
                final = stage + 1 == len(self.bits)
                chunk = min(64, self.rows)

                @pl.loop(0, self.rows // chunk)
                def _(number):
                    rows = pl.ds(pl.multiple_of(number * chunk, chunk), chunk)
                    value = (mine[rows, :].astype(F32) + theirs[rows, :].astype(F32)).astype(BF16)
                    if final:
                        self.out[rows, half * self.columns : (half + 1) * self.columns] = value
                    else:
                        theirs[rows, :] = value

            if stage + 1 < len(self.bits):
                self.begin(half, stage + 1)

    def finish(self):
        for half in range(2):
            for stage in self.bits:
                for piece in self.kept(half, stage):
                    self.hop(half, stage, piece).wait_send()


def group_scatter_scratch(owners, rows, width):
    bits = owners.bit_length() - 1
    return [
        pltpu.VMEM((2, owners >> stage + 1, rows, width // 2), BF16) for stage in range(bits)
    ] + [pltpu.SemaphoreType.DMA((2, bits * owners))] * 2


def comm_kernel(plan, chips, owners, counts, *refs):
    refs = list(refs)

    def pop(count):
        taken = refs[:count]
        del refs[:count]
        return taken

    scatter_ins = pop(counts["scatter_ins"])
    gather_ins = pop(counts["gather"])
    group_gather_ins = pop(counts["group_gather"])
    group_scatter_ins = pop(counts["group_scatter"])
    scatter_outs = pop(counts["scatter"])
    gather_outs = pop(counts["gather"])
    group_gather_outs = pop(counts["group_gather"])
    group_scatter_outs = pop(counts["group_scatter"])
    chained_outs = pop(counts["chained"])
    bits = owners.bit_length() - 1
    transfers = {"out": scatter_outs}
    if counts["scatter"]:
        rows = scatter_outs[0].shape[0]
        left, weight = scatter_ins[0], scatter_ins[1] if len(scatter_ins) > 1 else None

        def tile(block):
            value = row_block(left, block, rows)
            return value.astype(F32) if weight is None else dot_nt(value, weight[...])

        transfers["scatter"] = Scatter(chips, tile, pop(10))
    transfers["gather"] = [
        Gather(chips, i, o, pop(6)) for i, o in zip(gather_ins, gather_outs, strict=True)
    ]
    transfers["group_gather"] = [
        GroupGather(owners, i, o, pop(3))
        for i, o in zip(group_gather_ins, group_gather_outs, strict=True)
    ]
    transfers["group_scatter"] = [
        GroupScatter(owners, i, o, pop(bits + 2))
        for i, o in zip(group_scatter_ins, group_scatter_outs, strict=True)
    ]
    transfers["chained"] = [
        Gather(chips, group_scatter_outs[i], o, pop(6)) for i, o in enumerate(chained_outs)
    ]
    greet(chips, owners if group_gather_ins or group_scatter_ins else 1)
    plan(transfers, chips, bits)


def comm_call(
    plan,
    number,
    name,
    parts,
    owners,
    micros,
    scatter=(),
    gather=(),
    group_gather=(),
    group_scatter=(),
    chained=0,
):
    chips = parts // 2
    operands = [*scatter, *gather, *group_gather, *group_scatter]
    in_specs = (
        [VMEM] * len(scatter)
        + [ANY] * (len(gather) + len(group_gather))
        + [VMEM] * len(group_scatter)
    )
    shapes, out_specs, scratch = [], [], []
    if scatter:
        rows = scatter[0].shape[0] // parts
        width = scatter[0].shape[1] if len(scatter) == 1 else scatter[1].shape[0]
        shapes.append(jax.ShapeDtypeStruct((rows, width), F32))
        out_specs.append(VMEM)
        scratch += scatter_scratch(chips, rows, width)
    for array in gather:
        shapes.append(jax.ShapeDtypeStruct((parts * array.shape[0], array.shape[1]), array.dtype))
        out_specs.append(ANY)
        scratch += gather_sems(chips)
    for array in group_gather:
        shapes.append(jax.ShapeDtypeStruct((owners * array.shape[0], array.shape[1]), array.dtype))
        out_specs.append(ANY)
        scratch += group_gather_sems(owners)
    for array in group_scatter:
        rows, width = array.shape[0] // owners, array.shape[1]
        shapes.append(jax.ShapeDtypeStruct((rows, width), BF16))
        out_specs.append(VMEM)
        scratch += group_scatter_scratch(owners, rows, width)
    for array in group_scatter[:chained]:
        rows, width = array.shape[0] // owners, array.shape[1]
        shapes.append(jax.ShapeDtypeStruct((parts * rows, width), BF16))
        out_specs.append(ANY)
        scratch += gather_sems(chips)
    counts = {
        "scatter_ins": len(scatter),
        "scatter": 1 if scatter else 0,
        "gather": len(gather),
        "group_gather": len(group_gather),
        "group_scatter": len(group_scatter),
        "chained": chained,
    }
    return pl.pallas_call(
        functools.partial(comm_kernel, plan, chips, owners, counts),
        out_shape=tuple(shapes),
        in_specs=in_specs,
        out_specs=tuple(out_specs),
        scratch_shapes=scratch,
        compiler_params=comm_params(number),
        cost_estimate=comm_cost(micros),
        name=name,
    )(*operands)


def plan_gather(transfers, chips, bits):
    for one in transfers["gather"] + transfers["group_gather"]:
        one.start()
    for number in range(max(chips - 1, bits)):
        if number < bits:
            for one in transfers["group_gather"]:
                one.step(number)
        if number < chips - 1:
            for one in transfers["gather"]:
                one.step(number + 1)
    for one in transfers["gather"] + transfers["group_gather"]:
        one.finish()


def plan_scatter(transfers, chips, bits):
    scatter, out = transfers["scatter"], transfers["out"][0]
    for one in transfers["group_scatter"]:
        one.start()
    scatter.start()
    scatter.pairs(out)
    for one in transfers["gather"]:
        one.start()
    for number in range(max(chips - 1, bits)):
        if number < chips - 1:
            scatter.step(number)
            for one in transfers["gather"]:
                one.step(number + 1)
        if number < bits:
            for one in transfers["group_scatter"]:
                one.step(number)
    scatter.finish(out)
    for one in transfers["gather"] + transfers["group_scatter"]:
        one.finish()


def plan_finish(transfers, chips, bits):
    scatters, chained = transfers["group_scatter"], transfers["chained"]
    for one in transfers["gather"] + scatters:
        one.start()
    for stage in range(bits):
        for one in scatters:
            one.step(stage)
    for one in chained:
        one.start()
    for number in range(1, chips):
        for one in transfers["gather"] + chained:
            one.step(number)
    for one in transfers["gather"] + chained + scatters:
        one.finish()


def plan_group_scatter(transfers, chips, bits):
    scatters, chained = transfers["group_scatter"], transfers["chained"]
    steps = [(one, stage) for one in scatters for stage in range(bits)]
    for one in scatters[:2]:
        one.start()
    waiting = list(scatters[2:])
    hops = []
    for one, stage in steps:
        one.step(stage)
        if stage == 0 and waiting:
            waiting.pop(0).start()
        at = scatters.index(one)
        if hops:
            hops.pop(0)()
        if stage == bits - 1 and at < len(chained):
            chained[at].start()
            hops += [functools.partial(chained[at].step, d) for d in range(1, chips)]
    for hop in hops:
        hop()
    for one in chained + scatters:
        one.finish()


def comm_params(number, limit=48):
    return pltpu.CompilerParams(
        collective_id=number, has_side_effects=True, vmem_limit_bytes=limit * 2**20
    )


def comm_cost(micros):
    return pl.CostEstimate(flops=0, bytes_accessed=int(micros * 3.4e6), transcendentals=0)


ANY = pl.BlockSpec(memory_space=pl.ANY)
VMEM = pl.BlockSpec(memory_space=pltpu.VMEM)


def widen_kernel(counts, *refs):
    sources, targets = refs[: len(counts)], refs[-sum(counts) :]
    at = 0
    for source, count in zip(sources, counts, strict=True):
        for number in range(count):
            targets[at][0, 0] = source[0, number].astype(F32)
            at += 1


def widen(packs, number, experts, previous=()):
    parts, unused, shard, width = packs[0].shape
    counts = [pack.shape[1] for pack in packs]
    total = sum(counts)
    shape = jax.ShapeDtypeStruct((parts, experts, shard, width), F32)
    block = pl.BlockSpec((1, 1, shard // 2, width), lambda c, h: (c, number, h, 0))
    return pl.pallas_call(
        functools.partial(widen_kernel, counts),
        out_shape=(shape,) * total,
        grid=(parts, 2),
        in_specs=[
            pl.BlockSpec((1, count, shard // 2, width), lambda c, h: (c, 0, h, 0))
            for count in counts
        ]
        + [ANY] * len(previous),
        out_specs=(block,) * total,
        input_output_aliases={len(packs) + i: i for i in range(len(previous))},
        cost_estimate=pl.CostEstimate(
            flops=0, bytes_accessed=sum(p.size for p in packs) * 6, transcendentals=0
        ),
        name="widen",
    )(*packs, *previous)


def finish_attention_kernel(sharers, packed_ref, q_ref, k_ref, v_ref, o_ref, sums_ref):
    width = o_ref.shape[1]
    share = 2 * HD // sharers
    at = pl.program_id(0)
    o_ref[...] = packed_ref[0, :, :width].astype(F32)
    q_ref[...] = packed_ref[0, :, width : 2 * width].astype(F32)
    for number in range(sharers):

        @pl.when(lax.rem(at, sharers) == number)
        def _():
            piece = packed_ref[0, :, 2 * width : 2 * width + share].astype(F32)
            start = number * share
            if start < HD:
                k_ref[:, start : start + share] = piece
            else:
                v_ref[:, start - HD : start - HD + share] = piece

    @pl.when(at == 0)
    def _():
        sums_ref[...] = jnp.zeros_like(sums_ref)

    sums_ref[...] += packed_ref[0, :, 2 * width + share :].astype(F32)


def finish_attention(packed, width, sharers):
    parts, shard, total = packed.shape
    spare = total - 2 * width - 2 * HD // sharers
    head = lambda c: (0, c // sharers)
    return pl.pallas_call(
        functools.partial(finish_attention_kernel, sharers),
        out_shape=(
            jax.ShapeDtypeStruct((shard, width * parts), F32),
            jax.ShapeDtypeStruct((shard, HK * HD), F32),
            jax.ShapeDtypeStruct((shard, HK * HD), F32),
            jax.ShapeDtypeStruct((shard, width * parts), F32),
            jax.ShapeDtypeStruct((shard, spare), F32),
        ),
        grid=(parts,),
        in_specs=[pl.BlockSpec((1, shard, total), lambda c: (c, 0, 0))],
        out_specs=(
            pl.BlockSpec((shard, width), lambda c: (0, c)),
            pl.BlockSpec((shard, HD), head),
            pl.BlockSpec((shard, HD), head),
            pl.BlockSpec((shard, width), lambda c: (0, c)),
            pl.BlockSpec((shard, spare), lambda c: (0, 0)),
        ),
        cost_estimate=pl.CostEstimate(flops=0, bytes_accessed=packed.size * 6, transcendentals=0),
        name="finish_attention",
    )(packed)


def per_device(
    tokens,
    positions,
    expert_ids,
    cotangent,
    attention_gain,
    query_weight,
    key_weight,
    value_weight,
    output_weight,
    query_gain,
    key_gain,
    mixture_gain,
    router_weight,
    gate_weight,
    up_weight,
    down_weight,
):
    parts, owners = lax.axis_size("ctx"), lax.axis_size("group")
    here, group = lax.axis_index("ctx"), lax.axis_index("group")
    rows = tokens.shape[1]
    length = rows * parts
    shard = query_weight.shape[0]
    width = HQ * HD // parts
    experts = EXPERTS // parts
    sharers = parts // HK
    key_head = here // sharers
    share = 2 * HD // sharers
    share_at = (here % sharers) * share

    gather_group = lambda v: lax.all_gather(v, "group", axis=0, tiled=True)

    def column(vector):
        return jnp.pad(vector, (0, shard - vector.shape[0]))[:, None]

    def columns(array, start, count):
        return lax.dynamic_slice_in_dim(array, start, count, 1)

    extras = jnp.concatenate(
        [
            router_weight,
            attention_gain[:, None],
            mixture_gain[:, None],
            column(query_gain),
            column(key_gain),
            jnp.zeros((shard, PAD - EXPERTS - 4), BF16),
        ],
        axis=1,
    )
    comm = lambda plan, number, name, micros, **transfers: comm_call(
        plan, number, name, parts, owners, micros, **transfers
    )
    inputs_all, positions_all, wqkv, wout = comm(
        plan_gather,
        0,
        "gather_tokens",
        45,
        gather=(tokens[0], jnp.broadcast_to(positions, (8, rows))),
        group_gather=(
            jnp.concatenate(
                [
                    columns(query_weight, here * width, width),
                    columns(key_weight, key_head * HD, HD),
                    columns(value_weight, key_head * HD, HD),
                    extras,
                ],
                axis=1,
            ),
            columns(output_weight, here * width, width),
        ),
    )
    at = width + 2 * HD
    extras = wqkv[:, at:]
    wqkv = wqkv[:, :at]
    router = extras[:, :EXPERTS]
    attention_gains = extras[:, EXPERTS].astype(F32)
    mixture_gains = extras[:, EXPERTS + 1].astype(F32)
    head_gain = (
        lambda col: extras[:, col]
        .reshape(owners, shard)[:, : HD // owners]
        .reshape(1, HD)
        .astype(F32)
    )
    query_gains, key_gains = head_gain(EXPERTS + 2), head_gain(EXPERTS + 3)

    def expert_pack(number, index):
        take = lambda w: lax.dynamic_index_in_dim(w, index * experts + number, 0, keepdims=False)
        return jnp.concatenate([take(gate_weight), take(up_weight), take(down_weight)], axis=1)

    later = lax.optimization_barrier((positions_all, here))[1]
    expert_weights = [gather_group(expert_pack(number, later)) for number in range(experts)]
    positions_all = positions_all.reshape(parts, 8, rows)[:, 0].reshape(length)
    doc_start = (jnp.arange(length, dtype=jnp.int32) - positions_all)[:, None]
    cosine, sine = rope_tables(positions_all)
    inputs = tokens[0].astype(F32)
    unused, attn_factor = rms_parts(inputs, attention_gains)
    normed_all = rms_parts(inputs_all.astype(F32), attention_gains)[0].astype(BF16)
    qkv_raw = dot(normed_all, wqkv)
    query_raw, kv_raw = qkv_raw[:, :width], qkv_raw[:, width:]
    tables = (query_raw, kv_raw, doc_start, cosine, sine, query_gains, key_gains)
    mixed_low = attend(*tables)
    attn_out, upstream_all = comm(
        plan_scatter,
        1,
        "scatter_attention",
        50,
        scatter=(mixed_low, wout),
        gather=(cotangent[0],),
    )
    hidden = inputs + attn_out
    moe_normed, moe_factor = rms_parts(hidden, mixture_gains)
    moe_low = moe_normed.astype(BF16)
    logits = dot(moe_low, router)
    onehot = (
        expert_ids[0][:, :, None] == jnp.arange(EXPERTS, dtype=jnp.int32)[None, None, :]
    ).astype(F32)
    chosen = jnp.sum(onehot * logits[:, None, :], axis=-1)
    expo = jnp.exp(chosen - jnp.max(chosen, axis=-1, keepdims=True))
    gates = expo / jnp.sum(expo, axis=-1, keepdims=True)
    combine = jnp.sum(gates[:, :, None] * onehot, axis=1)
    moe_all, combine_all = comm(
        plan_gather,
        2,
        "gather_mixture",
        45,
        gather=(moe_low, jnp.pad(combine, ((0, 0), (0, PAD - EXPERTS)))),
    )
    combine_all = columns(combine_all, here * experts, experts)

    layer_part = jnp.zeros((length, D), F32)
    moe_part = jnp.zeros((length, D), F32)
    combine_grads = []
    first_pieces, last_grads = [], []
    for number in range(experts):
        pack = expert_weights[number]
        if first_pieces:
            pack = lax.optimization_barrier((pack, *first_pieces[-1]))[0]
        gate_up, down = pack[:, : 2 * F], pack[:, 2 * F :]
        weight = combine_all[:, number : number + 1]
        gate_up_all = dot(moe_all, gate_up)
        gate_all, up_all = gate_up_all[:, :F], gate_up_all[:, F:]
        back_all = dot(upstream_all, down)
        sigmoid = lax.logistic(gate_all)
        act_low = (gate_all * sigmoid * up_all).astype(BF16)
        act = act_low.astype(F32)
        combine_grads.append(jnp.sum(act * back_all, axis=-1, keepdims=True))
        act_grad = weight * back_all
        gate_grad = (act_grad * up_all * sigmoid * (1.0 + gate_all * (1.0 - sigmoid))).astype(BF16)
        up_grad = (act_grad * gate_all * sigmoid).astype(BF16)
        weighted = (weight * act).astype(BF16)
        grads = (
            dot_tn(upstream_all, weighted).astype(BF16),
            dot_tn(moe_all, gate_grad).astype(BF16),
            dot_tn(moe_all, up_grad).astype(BF16),
        )
        if number < experts - 1:
            first_pieces.append(
                comm(
                    plan_group_scatter,
                    10 + number,
                    "scatter_expert",
                    80,
                    group_scatter=grads,
                    chained=1,
                )
            )
        else:
            last_grads = grads
        layer_part = layer_part + dot_nt(weighted, down)
        moe_part = moe_part + dot_nt(jnp.concatenate([gate_grad, up_grad], axis=1), gate_up)
    combine_grad = jnp.concatenate(combine_grads, axis=1)
    high = combine_grad.astype(BF16)
    low = (combine_grad - high.astype(F32)).astype(BF16)
    place = lambda v: lax.dynamic_update_slice_in_dim(
        jnp.zeros((length, EXPERTS), BF16), v, here * experts, 1
    )
    moe_pack = jnp.concatenate(
        [
            moe_part.astype(BF16),
            place(high),
            place(low),
            jnp.zeros((length, PAD - 2 * EXPERTS), BF16),
        ],
        axis=1,
    )
    moe_sum, *last_pieces = comm(
        plan_scatter,
        3,
        "scatter_mixture",
        80,
        scatter=(moe_pack,),
        group_scatter=last_grads,
    )
    stack_shape = lambda v: v.reshape(parts, -1, shard, F)
    expert_packs = [
        (stack_shape(pieces[3]), lax.all_gather(jnp.stack(pieces[1:3]), "ctx"))
        for pieces in first_pieces
    ] + [(lax.all_gather(jnp.stack(last_pieces), "ctx"),)]

    dcombine = moe_sum[:, D : D + EXPERTS] + moe_sum[:, D + EXPERTS : D + 2 * EXPERTS]
    gates_grad = jnp.sum(onehot * dcombine[:, None, :], axis=-1)
    chosen_grad = gates * (gates_grad - jnp.sum(gates * gates_grad, axis=-1, keepdims=True))
    logit_grad_low = jnp.sum(chosen_grad[:, :, None] * onehot, axis=1).astype(BF16)
    router_partial = dot_tn(moe_low, logit_grad_low)
    moe_grad = moe_sum[:, :D] + dot_nt(logit_grad_low, router)
    hidden_part, mixture_terms = rms_back(hidden, moe_factor, mixture_gains, moe_grad)
    mixture_partial = jnp.sum(mixture_terms, axis=0)
    hidden_grad = cotangent[0].astype(F32) + hidden_part

    layer_sum, attn_grad_all = comm(
        plan_scatter,
        4,
        "scatter_layer",
        60,
        scatter=(layer_part.astype(BF16),),
        gather=(hidden_grad.astype(BF16),),
    )
    layer_out = (hidden + layer_sum).astype(BF16)[None]
    mixed_grad = dot(attn_grad_all, wout).astype(BF16)
    output_partial = dot_tn(attn_grad_all, mixed_low).astype(BF16)
    query_low, kv_part, query_terms, key_terms = attend_back(*tables, mixed_grad)
    step = 1
    while step < sharers:
        kv_part = kv_part + lax.ppermute(kv_part, "ctx", [(i, i ^ step) for i in range(parts)])
        step *= 2
    kv_low = columns(kv_part.astype(BF16), share_at, share)
    qkv_low = jnp.concatenate([query_low, kv_low], axis=1)
    wqkv_share = jnp.concatenate(
        [wqkv[:, :width], columns(wqkv[:, width:], share_at, share)], axis=1
    )
    def head_column(terms):
        spread = terms.reshape(owners, HD // owners)
        return jnp.pad(spread, ((0, 0), (0, shard - HD // owners))).reshape(D, 1)

    spare = next(n for n in range(EXPERTS + 3, 1024) if (width + share + n) % 256 == 0)
    qkv_partial = jnp.concatenate(
        [
            dot_tn(normed_all, qkv_low),
            router_partial,
            mixture_partial[:, None],
            head_column(query_terms),
            head_column(key_terms),
            jnp.zeros((D, spare - EXPERTS - 3), F32),
        ],
        axis=1,
    ).astype(BF16)
    normed_grad, output_piece, qkv_piece = comm(
        plan_scatter,
        5,
        "scatter_normed",
        60,
        scatter=(qkv_low, wqkv_share),
        group_scatter=(output_partial, qkv_partial),
    )
    input_part, attention_terms = rms_back(inputs, attn_factor, attention_gains, normed_grad)
    tokens_grad = (hidden_grad + input_part).astype(BF16)[None]
    attention_partial = jnp.sum(attention_terms, axis=0)
    gain_rows = jnp.pad(attention_partial.reshape(owners, shard), ((0, 0), (0, D - shard)))
    attn_grads, unused, gain_parts = comm(
        plan_finish,
        6,
        "gather_grads",
        90,
        gather=(jnp.concatenate([output_piece, qkv_piece], axis=1),),
        group_scatter=(gain_rows.reshape(owners * 8, D // 8).astype(BF16),),
        chained=1,
    )
    attention_gain_grad = jnp.sum(gain_parts.reshape(parts, D)[:, :shard].astype(F32), axis=0)
    query_grad, key_grad, value_grad, output_grad, sums = finish_attention(
        attn_grads.reshape(parts, shard, -1), width, sharers
    )
    finished = ()
    for number in range(experts):
        finished = widen(expert_packs[number], number, experts, finished)
    whole = lambda v: v.reshape(EXPERTS, shard, F)
    return (
        layer_out,
        tokens_grad,
        attention_gain_grad,
        query_grad,
        key_grad,
        value_grad,
        output_grad,
        sums[: HD // owners, EXPERTS + 1],
        sums[: HD // owners, EXPERTS + 2],
        sums[:, EXPERTS],
        sums[:, :EXPERTS],
        whole(finished[1]),
        whole(finished[2]),
        whole(finished[0]),
    )


def solution(mesh):
    return jax.shard_map(
        per_device,
        mesh=mesh,
        in_specs=(
            P("group", "ctx", None),
            P("group", "ctx"),
            P("group", "ctx", None),
            P("group", "ctx", None),
            P("group"),
            P("group", None),
            P("group", None),
            P("group", None),
            P("group", None),
            P("group"),
            P("group"),
            P("group"),
            P("group", None),
            P(None, "group", None),
            P(None, "group", None),
            P(None, "group", None),
        ),
        out_specs=(
            P("group", "ctx", None),
            P("group", "ctx", None),
            P("group"),
            P("group", None),
            P("group", None),
            P("group", None),
            P("group", None),
            P("group"),
            P("group"),
            P("group"),
            P("group", None),
            P(None, "group", None),
            P(None, "group", None),
            P(None, "group", None),
        ),
        check_vma=False,
    )
```

```python
import functools

import jax
import jax.numpy as jnp
from jax import lax
from jax.experimental import pallas as pl
from jax.experimental.pallas import tpu as pltpu
from jax.sharding import PartitionSpec as P

D = 2048
HQ = 32
HK = 4
HD = 128
F = 768
TOPK = 8
EXPERTS = 16
PAD = 128

EPS = 1e-06
ROPE_BASE = 1000000.0
FLOOR = -1e30
F32 = jnp.float32
BF16 = jnp.bfloat16


def rms_parts(values, gains):
    factor = lax.rsqrt(jnp.mean(values * values, axis=-1, keepdims=True) + EPS)
    return (values * factor * gains, factor)


def rms_back(values, factor, gains, gradient):
    weighted = gradient * gains
    inner = jnp.mean(weighted * values, axis=-1, keepdims=True)
    grad_values = factor * weighted - values * (factor * factor * factor) * inner
    return (grad_values, gradient * values * factor)


def dot(left, right):
    return jnp.dot(left, right, preferred_element_type=F32)


def dot_nt(left, right):
    return lax.dot_general(left, right, (((1,), (1,)), ((), ())), preferred_element_type=F32)


def dot_tn(left, right):
    return lax.dot_general(left, right, (((0,), (0,)), ((), ())), preferred_element_type=F32)


def rope_tables(position_row):
    frequency = ROPE_BASE ** (-2.0 * jnp.arange(HD // 2, dtype=F32) / HD)
    angles = position_row.astype(F32)[:, None] * frequency[None, :]
    cosine, sine = jnp.cos(angles), jnp.sin(angles)
    return jnp.concatenate([cosine, cosine, -sine, sine], axis=-1)


def turn(values):
    return pltpu.roll(values, HD // 2, 1)


def normed_rope(raw, gains, cosine, sine):
    normed, factor = rms_parts(raw, gains)
    return (normed * cosine + turn(normed) * sine, factor)


def softmax_weights(query, key_ref, doc_start, number):
    rows = query.shape[0]
    scale = HD**-0.5 * 1.4426950408889634
    parts = []
    if number:
        columns = number * rows
        key_index = lax.broadcasted_iota(jnp.int32, (rows, columns), 1)
        scores = dot_nt(query, key_ref[:columns, :]) * scale
        parts.append(jnp.where(key_index >= doc_start, scores, FLOOR))
    row_index = lax.broadcasted_iota(jnp.int32, (rows, rows), 0)
    key_index = lax.broadcasted_iota(jnp.int32, (rows, rows), 1)
    allowed = (key_index <= row_index) & (key_index >= doc_start - number * rows)
    scores = dot_nt(query, key_ref[number * rows : (number + 1) * rows, :]) * scale
    parts.append(jnp.where(allowed, scores, FLOOR))
    masked = jnp.concatenate(parts, axis=1) if number else parts[0]
    weights = jnp.exp2(masked - jnp.max(masked, axis=-1, keepdims=True))
    return weights, 1.0 / jnp.sum(weights, axis=-1, keepdims=True)


def attend_kernel(
    block, q_ref, kv_ref, doc_ref, cos_ref, sin_ref, qg_ref, kg_ref, out_ref, key_ref, val_ref
):
    length = kv_ref.shape[0]
    head, part = pl.program_id(0), pl.program_id(1)

    @pl.when((head == 0) & (part == 0))
    def _():
        key, unused = normed_rope(kv_ref[:, :HD], kg_ref[...], cos_ref[...], sin_ref[...])
        key_ref[...] = key.astype(BF16)
        val_ref[...] = kv_ref[:, HD:].astype(BF16)

    for number in range(length // block):

        @pl.when(part == number)
        def _():
            rows = pl.ds(number * block, block)
            columns = (number + 1) * block
            query, unused = normed_rope(q_ref[...], qg_ref[...], cos_ref[rows, :], sin_ref[rows, :])
            weights, share = softmax_weights(query.astype(BF16), key_ref, doc_ref[...], number)
            mixed = dot(weights.astype(BF16), val_ref[:columns, :])
            out_ref[...] = (mixed * share).astype(BF16)


def attend_back_kernel(
    block,
    q_ref,
    kv_ref,
    doc_ref,
    cos_ref,
    sin_ref,
    qg_ref,
    kg_ref,
    dm_ref,
    dq_ref,
    dkv_ref,
    qt_ref,
    kt_ref,
    key_ref,
    val_ref,
    dk_ref,
    dv_ref,
):
    length = kv_ref.shape[0]
    head, part = pl.program_id(0), pl.program_id(1)
    scaling = HD**-0.5

    @pl.when((head == 0) & (part == 0))
    def _():
        key, unused = normed_rope(kv_ref[:, :HD], kg_ref[...], cos_ref[...], sin_ref[...])
        key_ref[...] = key.astype(BF16)
        val_ref[...] = kv_ref[:, HD:].astype(BF16)
        dk_ref[...] = jnp.zeros_like(dk_ref)
        dv_ref[...] = jnp.zeros_like(dv_ref)
        qt_ref[...] = jnp.zeros_like(qt_ref)

    for number in range(length // block):

        @pl.when(part == number)
        def _():
            rows = pl.ds(number * block, block)
            columns = (number + 1) * block
            cosine, sine = cos_ref[rows, :], sin_ref[rows, :]
            raw = q_ref[...]
            query, factor = normed_rope(raw, qg_ref[...], cosine, sine)
            query = query.astype(BF16)
            key, value = key_ref[:columns, :], val_ref[:columns, :]
            upstream = dm_ref[...]
            weights, share = softmax_weights(query, key_ref, doc_ref[...], number)
            probs = weights * share
            prob_grad = dot_nt(upstream, value)
            delta = jnp.sum(probs * prob_grad, axis=-1, keepdims=True)
            score_grad = (probs * (prob_grad - delta)).astype(BF16)
            dk_ref[:columns, :] += dot_tn(score_grad, query)
            dv_ref[:columns, :] += dot_tn(probs.astype(BF16), upstream)
            rotated = dot(score_grad, key) * scaling
            query_grad = rotated * cosine - turn(rotated) * sine
            raw_grad, terms = rms_back(raw, factor, qg_ref[...], query_grad)
            dq_ref[...] = raw_grad.astype(BF16)
            qt_ref[...] += jnp.sum(terms, axis=0, keepdims=True)

    @pl.when((head == pl.num_programs(0) - 1) & (part == pl.num_programs(1) - 1))
    def _():
        raw = kv_ref[:, :HD]
        cosine, sine = cos_ref[...], sin_ref[...]
        unused, factor = rms_parts(raw, kg_ref[...])
        rotated = dk_ref[...] * scaling
        key_grad = rotated * cosine - turn(rotated) * sine
        raw_grad, terms = rms_back(raw, factor, kg_ref[...], key_grad)
        dkv_ref[:, :HD] = raw_grad
        dkv_ref[:, HD:] = dv_ref[...]
        kt_ref[...] = jnp.sum(terms, axis=0, keepdims=True)


def attention_specs(length, block, heads):
    whole = lambda h, b: (0, 0)
    return [
        pl.BlockSpec((block, HD), lambda h, b: (b, h)),
        pl.BlockSpec((length, 2 * HD), lambda h, b: (0, heads // 2)),
        pl.BlockSpec((block, 1), lambda h, b: (b, 0)),
        pl.BlockSpec((length, HD), whole),
        pl.BlockSpec((length, HD), lambda h, b: (0, 1)),
        pl.BlockSpec((1, HD), whole),
        pl.BlockSpec((1, HD), whole),
    ]


def attend(qkv_raw, doc_start, tables, query_gain, key_gain):
    length, width = qkv_raw.shape[0], qkv_raw.shape[1] - 2 * HD
    block = 256
    return pl.pallas_call(
        functools.partial(attend_kernel, block),
        out_shape=jax.ShapeDtypeStruct((length, width), BF16),
        grid_spec=pltpu.PrefetchScalarGridSpec(
            num_scalar_prefetch=0,
            grid=(width // HD, length // block),
            in_specs=attention_specs(length, block, width // HD),
            out_specs=pl.BlockSpec((block, HD), lambda h, b: (b, h)),
            scratch_shapes=[pltpu.VMEM((length, HD), BF16), pltpu.VMEM((length, HD), BF16)],
        ),
        cost_estimate=pl.CostEstimate(
            flops=length * length,
            bytes_accessed=length * width,
            transcendentals=0,
        ),
        name="attend",
    )(qkv_raw, qkv_raw, doc_start, tables, tables, query_gain, key_gain)


def attend_back(qkv_raw, doc_start, tables, query_gain, key_gain, upstream):
    length, width = qkv_raw.shape[0], qkv_raw.shape[1] - 2 * HD
    block = 256
    whole = lambda h, b: (0, 0)
    return pl.pallas_call(
        functools.partial(attend_back_kernel, block),
        out_shape=(
            jax.ShapeDtypeStruct((length, width), BF16),
            jax.ShapeDtypeStruct((length, 2 * HD), F32),
            jax.ShapeDtypeStruct((1, HD), F32),
            jax.ShapeDtypeStruct((1, HD), F32),
        ),
        grid_spec=pltpu.PrefetchScalarGridSpec(
            num_scalar_prefetch=0,
            grid=(width // HD, length // block),
            in_specs=attention_specs(length, block, width // HD)
            + [pl.BlockSpec((block, HD), lambda h, b: (b, h))],
            out_specs=(
                pl.BlockSpec((block, HD), lambda h, b: (b, h)),
                pl.BlockSpec((length, 2 * HD), whole),
                pl.BlockSpec((1, HD), whole),
                pl.BlockSpec((1, HD), whole),
            ),
            scratch_shapes=[
                pltpu.VMEM((length, HD), BF16),
                pltpu.VMEM((length, HD), BF16),
                pltpu.VMEM((length, HD), F32),
                pltpu.VMEM((length, HD), F32),
            ],
        ),
        cost_estimate=pl.CostEstimate(
            flops=length * length,
            bytes_accessed=length * width,
            transcendentals=0,
        ),
        name="attend_back",
    )(qkv_raw, qkv_raw, doc_start, tables, tables, query_gain, key_gain, upstream)


def ctx_place():
    here = lax.axis_index("ctx")
    return (here // 2, lax.rem(here, 2))


def peer(chip, core):
    return {"ctx": 2 * chip + core}


def greet(chips, owners=1):
    chip, core = ctx_place()
    group = lax.axis_index("group")
    barrier = pltpu.get_barrier_semaphore()
    pl.semaphore_signal(barrier, inc=1, device_id=peer(chip, 1 - core))

    @pl.when(chip > 0)
    def _():
        pl.semaphore_signal(barrier, inc=1, device_id=peer(chip - 1, core))

    @pl.when(chip < chips - 1)
    def _():
        pl.semaphore_signal(barrier, inc=1, device_id=peer(chip + 1, core))

    bits = owners.bit_length() - 1
    for bit in range(bits):
        pl.semaphore_signal(barrier, inc=1, device_id={"group": group ^ (1 << bit)})
    count = 1 + bits + (chip > 0).astype(jnp.int32) + (chip < chips - 1).astype(jnp.int32)
    pl.semaphore_wait(barrier, count)


class Gather:
    def __init__(self, chips, source, target, sems):
        self.chips, self.source, self.target = chips, source, target
        self.up, self.down, self.side, self.near, self.cross, self.local = sems
        self.chip, self.core = ctx_place()
        self.rows = source.shape[0]
        self.chunks = range(chunk_count(self.rows))
        self.piece = self.rows // len(self.chunks)

    def block(self, chip, core, chunk):
        start = (2 * chip + core) * self.rows + chunk * self.piece
        return self.target.at[pl.ds(pl.multiple_of(start, self.piece), self.piece)]

    def hop(self, origin, chunk, sem, arrive, device, own):
        source = self.block(origin, self.core, chunk)
        if own:
            source = self.source.at[pl.ds(chunk * self.piece, self.piece)]
        return pltpu.make_async_remote_copy(
            src_ref=source,
            dst_ref=self.block(origin, self.core, chunk),
            send_sem=sem.at[origin, chunk],
            recv_sem=arrive.at[origin, chunk],
            device_id=device,
        )

    def to_up(self, origin, chunk, own=False):
        return self.hop(origin, chunk, self.up, self.near, peer(self.chip + 1, self.core), own)

    def to_down(self, origin, chunk, own=False):
        return self.hop(origin, chunk, self.down, self.near, peer(self.chip - 1, self.core), own)

    def to_side(self, origin, chunk, own=False):
        return self.hop(origin, chunk, self.side, self.cross, peer(self.chip, 1 - self.core), own)

    def mine(self):
        start = pl.multiple_of((2 * self.chip + self.core) * self.rows, self.rows)
        return pltpu.make_async_copy(
            self.source, self.target.at[pl.ds(start, self.rows)], self.local
        )

    def start(self):
        for chunk in self.chunks:

            @pl.when(self.chip < self.chips - 1)
            def _():
                self.to_up(self.chip, chunk, True).start()

            @pl.when(self.chip > 0)
            def _():
                self.to_down(self.chip, chunk, True).start()

        for chunk in self.chunks:
            self.to_side(self.chip, chunk, True).start()
        self.mine().start()

    def step(self, distance):
        below, above = self.chip - distance, self.chip + distance
        for chunk in self.chunks:

            @pl.when(below >= 0)
            def _():
                self.to_up(below, chunk).wait_recv()

                @pl.when(self.chip < self.chips - 1)
                def _():
                    self.to_up(below, chunk).start()

                self.to_side(below, chunk).start()

            @pl.when(above < self.chips)
            def _():
                self.to_down(above, chunk).wait_recv()

                @pl.when(self.chip > 0)
                def _():
                    self.to_down(above, chunk).start()

                self.to_side(above, chunk).start()

    def finish(self):
        self.mine().wait()
        for origin in range(self.chips):
            for chunk in self.chunks:
                pltpu.make_async_remote_copy(
                    src_ref=self.source.at[pl.ds(chunk * self.piece, self.piece)],
                    dst_ref=self.block(origin, 1 - self.core, chunk),
                    send_sem=self.side.at[origin, chunk],
                    recv_sem=self.cross.at[origin, chunk],
                    device_id=peer(self.chip, 1 - self.core),
                ).wait_recv()
                self.to_side(origin, chunk).wait_send()

                @pl.when((origin <= self.chip) & (self.chip < self.chips - 1))
                def _():
                    self.to_up(origin, chunk).wait_send()

                @pl.when((origin >= self.chip) & (self.chip > 0))
                def _():
                    self.to_down(origin, chunk).wait_send()


def chunk_count(rows):
    return 4 if rows % 64 == 0 else 1


def gather_sems(chips, rows):
    return [pltpu.SemaphoreType.DMA((chips, chunk_count(rows)))] * 5 + [pltpu.SemaphoreType.DMA]


class Scatter:
    def __init__(self, chips, tile, outs, refs):
        self.chips, self.tile, self.outs = chips, tile, outs
        self.give, self.take, self.send, self.low, self.high, *self.sems = refs
        self.chip, self.core = ctx_place()
        self.rows = outs[0].shape[0]
        self.chunks = range(chunk_count(self.rows))
        self.piece = self.rows // len(self.chunks)

    def part(self, ref, target, chunk):
        return ref.at[target, pl.ds(chunk * self.piece, self.piece)]

    def side(self, target):
        return pltpu.make_async_remote_copy(
            src_ref=self.give.at[target],
            dst_ref=self.take.at[target],
            send_sem=self.sems[0].at[target],
            recv_sem=self.sems[1].at[target],
            device_id=peer(self.chip, 1 - self.core),
        )

    def up(self, target, chunk):
        return pltpu.make_async_remote_copy(
            src_ref=self.part(self.send, target, chunk),
            dst_ref=self.part(self.low, target, chunk),
            send_sem=self.sems[2].at[target, chunk],
            recv_sem=self.sems[3].at[target, chunk],
            device_id=peer(self.chip + 1, self.core),
        )

    def down(self, target, chunk):
        return pltpu.make_async_remote_copy(
            src_ref=self.part(self.send, target, chunk),
            dst_ref=self.part(self.high, target, chunk),
            send_sem=self.sems[2].at[target, chunk],
            recv_sem=self.sems[4].at[target, chunk],
            device_id=peer(self.chip - 1, self.core),
        )

    def order(self):
        last = self.chips - 1
        return sorted(range(self.chips), key=lambda target: min(target, last - target))

    def start(self):
        for target in self.order():
            self.give[target] = self.tile(2 * target + 1 - self.core).astype(BF16)
            self.side(target).start()

    def store(self, value):
        at = 0
        for out in self.outs:
            out[...] = value[:, at : at + out.shape[1]]
            at += out.shape[1]

    def pairs(self):
        last = self.chips - 1
        for target in self.order():
            value = self.tile(2 * target + self.core)
            self.side(target).wait_recv()
            value = value + self.take[target].astype(F32)
            self.send[target] = value.astype(BF16)

            @pl.when(self.chip == target)
            def _():
                self.store(value)

            if target == last:

                @pl.when(self.chip == 0)
                def _():
                    for chunk in self.chunks:
                        self.up(target, chunk).start()

            if target == 0:

                @pl.when(self.chip == last)
                def _():
                    for chunk in self.chunks:
                        self.down(target, chunk).start()

    def add(self, target, chunk, ref):
        mine, theirs = self.part(self.send, target, chunk), self.part(ref, target, chunk)
        mine[...] = (mine[...].astype(F32) + theirs[...].astype(F32)).astype(BF16)

    def upward(self, number):
        target = self.chips - 1 - number

        @pl.when(target > self.chip)
        def _():
            for chunk in self.chunks:

                @pl.when(self.chip > 0)
                def _():
                    self.up(target, chunk).wait_recv()
                    self.add(target, chunk, self.low)

                @pl.when((self.chip > 0) | (number > 0))
                def _():
                    self.up(target, chunk).start()

    def downward(self, number):
        last = self.chips - 1

        @pl.when(number < self.chip)
        def _():
            for chunk in self.chunks:

                @pl.when(self.chip < last)
                def _():
                    self.down(number, chunk).wait_recv()
                    self.add(number, chunk, self.high)

                @pl.when((self.chip < last) | (number > 0))
                def _():
                    self.down(number, chunk).start()

    def step(self, number):
        @pl.when(self.chip < self.chips // 2)
        def _():
            self.upward(number)
            self.downward(number)

        @pl.when(self.chip >= self.chips // 2)
        def _():
            self.downward(number)
            self.upward(number)

    def gain(self, target, chunk, ref):
        theirs = self.part(ref, target, chunk)[...].astype(F32)
        rows, at = pl.ds(chunk * self.piece, self.piece), 0
        for out in self.outs:
            out[rows, :] += theirs[:, at : at + out.shape[1]]
            at += out.shape[1]

    def finish(self):
        for target in range(self.chips):

            @pl.when(self.chip == target)
            def _():
                for chunk in self.chunks:
                    if target > 0:
                        self.up(target, chunk).wait_recv()
                        self.gain(target, chunk, self.low)
                    if target < self.chips - 1:
                        self.down(target, chunk).wait_recv()
                        self.gain(target, chunk, self.high)

        for target in range(self.chips):
            self.side(target).wait_send()

            @pl.when(self.chip != target)
            def _():
                for chunk in self.chunks:
                    self.up(target, chunk).wait_send()


def scatter_scratch(chips, rows, width):
    hops = pltpu.SemaphoreType.DMA((chips, chunk_count(rows)))
    return (
        [pltpu.VMEM((chips, rows, width), BF16)] * 5
        + [pltpu.SemaphoreType.DMA((chips,))] * 2
        + [hops] * 3
    )


def row_block(ref, block, rows):
    return ref[pl.ds(pl.multiple_of(block * rows, rows), rows), :]


class GroupGather:
    def __init__(self, owners, source, target, sems):
        self.owners, self.source, self.target = owners, source, target
        self.sent, self.got, self.local = sems
        self.group = lax.axis_index("group")
        self.rows = source.shape[0]
        self.bits = list(range(owners.bit_length() - 1))
        self.orders = (self.bits, self.bits[::-1])

    def piece(self, mask, half):
        start = (self.group ^ mask) * self.rows + half * (self.rows // 2)
        return self.target.at[pl.ds(pl.multiple_of(start, self.rows // 2), self.rows // 2)]

    def held(self, half, stage):
        masks = [0]
        for bit in self.orders[half][:stage]:
            masks += [mask | 1 << bit for mask in masks]
        return masks

    def hop(self, half, stage, mask):
        bit = self.orders[half][stage]
        source = self.piece(mask, half)
        if mask == 0:
            source = self.source.at[pl.ds(half * (self.rows // 2), self.rows // 2)]
        return pltpu.make_async_remote_copy(
            src_ref=source,
            dst_ref=self.piece(mask, half),
            send_sem=self.sent.at[half, stage * self.owners + mask],
            recv_sem=self.got.at[half, mask | 1 << bit],
            device_id={"group": self.group ^ (1 << bit)},
        )

    def mine(self):
        start = pl.multiple_of(self.group * self.rows, self.rows)
        return pltpu.make_async_copy(
            self.source, self.target.at[pl.ds(start, self.rows)], self.local
        )

    def start(self):
        for half in range(2):
            self.hop(half, 0, 0).start()
        self.mine().start()

    def step(self, stage):
        for half in range(2):
            for mask in self.held(half, stage):
                self.hop(half, stage, mask).wait_recv()
            if stage + 1 < len(self.bits):
                for mask in self.held(half, stage + 1):
                    self.hop(half, stage + 1, mask).start()

    def finish(self):
        self.mine().wait()
        for half in range(2):
            for stage in self.bits:
                for mask in self.held(half, stage):
                    self.hop(half, stage, mask).wait_send()


def group_gather_sems(owners):
    bits = owners.bit_length() - 1
    return [
        pltpu.SemaphoreType.DMA((2, bits * owners)),
        pltpu.SemaphoreType.DMA((2, owners)),
        pltpu.SemaphoreType.DMA,
    ]


class GroupScatter:
    def __init__(self, owners, part, out, refs):
        self.owners, self.part, self.out = owners, part, out
        self.land, (self.sent, self.got) = refs[:-2], refs[-2:]
        self.group = lax.axis_index("group")
        self.bits = list(range(owners.bit_length() - 1))
        self.orders = (self.bits, self.bits[::-1])
        self.rows, self.columns = out.shape[0], out.shape[1] // 2

    def kept(self, half, stage):
        done = self.orders[half][: stage + 1]
        return [r for r in range(self.owners) if not any(r >> bit & 1 for bit in done)]

    def place(self, half, stage, piece):
        if stage == 0:
            start = pl.multiple_of((self.group ^ piece) * self.rows, self.rows)
            return self.part.at[pl.ds(start, self.rows), pl.ds(half * self.columns, self.columns)]
        return self.land[stage - 1].at[half, self.kept(half, stage - 1).index(piece)]

    def hop(self, half, stage, piece):
        bit = self.orders[half][stage]
        at = self.kept(half, stage).index(piece)
        return pltpu.make_async_remote_copy(
            src_ref=self.place(half, stage, piece | 1 << bit),
            dst_ref=self.land[stage].at[half, at],
            send_sem=self.sent.at[half, stage * self.owners + piece],
            recv_sem=self.got.at[half, stage * self.owners + piece],
            device_id={"group": self.group ^ (1 << bit)},
        )

    def begin(self, half, stage):
        for piece in self.kept(half, stage):
            self.hop(half, stage, piece).start()

    def start(self):
        for half in range(2):
            self.begin(half, 0)

    def step(self, stage):
        for half in range(2):
            for piece in self.kept(half, stage):
                self.hop(half, stage, piece).wait_recv()
                mine = self.place(half, stage, piece)
                theirs = self.land[stage].at[half, self.kept(half, stage).index(piece)]
                final = stage + 1 == len(self.bits)
                chunk = min(64, self.rows)

                @pl.loop(0, self.rows // chunk)
                def _(number):
                    rows = pl.ds(pl.multiple_of(number * chunk, chunk), chunk)
                    value = (mine[rows, :].astype(F32) + theirs[rows, :].astype(F32)).astype(BF16)
                    if final:
                        self.out[rows, half * self.columns : (half + 1) * self.columns] = value
                    else:
                        theirs[rows, :] = value

            if stage + 1 < len(self.bits):
                self.begin(half, stage + 1)

    def finish(self):
        for half in range(2):
            for stage in self.bits:
                for piece in self.kept(half, stage):
                    self.hop(half, stage, piece).wait_send()


def group_scatter_scratch(owners, rows, width):
    bits = owners.bit_length() - 1
    return [
        pltpu.VMEM((2, owners >> stage + 1, rows, width // 2), BF16) for stage in range(bits)
    ] + [pltpu.SemaphoreType.DMA((2, bits * owners))] * 2


def comm_kernel(plan, chips, owners, counts, views, *refs):
    refs = list(refs)

    def pop(count):
        taken = refs[:count]
        del refs[:count]
        return taken

    scatter_ins = [pop(count) for count in counts["scatter_ins"]]
    gather_ins = pop(counts["gather"])
    group_gather_ins = [view(ref) for view, ref in zip(views[0], pop(len(views[0])), strict=True)]
    group_scatter_ins = pop(counts["group_scatter"])
    pack_ins = [[view(ref) for view, ref in zip(v, pop(len(v)), strict=True)] for v in views[1]]
    scatter_outs = pop(counts["scatter"])
    gather_outs = pop(counts["gather"])
    group_gather_outs = pop(len(views[0]))
    group_scatter_outs = pop(counts["group_scatter"])
    chained_outs = pop(counts["chained"])
    pack_outs = pop(len(views[1]))
    bits = owners.bit_length() - 1
    transfers = {}
    if scatter_outs:
        rows = scatter_outs[0].shape[0]

        def tile(block):
            values = []
            for left, *weight in scatter_ins:
                value = row_block(left, block, rows)
                values.append(dot_nt(value, weight[0][...]) if weight else value.astype(F32))
            return values[0] if len(values) == 1 else jnp.concatenate(values, axis=1)

        transfers["scatter"] = Scatter(chips, tile, scatter_outs, pop(10))
    transfers["gather"] = [
        Gather(chips, i, o, pop(6)) for i, o in zip(gather_ins, gather_outs, strict=True)
    ]
    transfers["group_gather"] = [
        GroupGather(owners, i, o, pop(3))
        for i, o in zip(group_gather_ins, group_gather_outs, strict=True)
    ]
    transfers["group_scatter"] = [
        GroupScatter(owners, i, o, pop(bits + 2))
        for i, o in zip(group_scatter_ins, group_scatter_outs, strict=True)
    ]
    transfers["chained"] = [
        Gather(chips, group_scatter_outs[i], o, pop(6)) for i, o in enumerate(chained_outs)
    ]
    copies = []
    for sources, target in zip(pack_ins, pack_outs, strict=True):
        sems, at = pop(1)[0], 0
        for number, source in enumerate(sources):
            copies.append(
                pltpu.make_async_copy(
                    source, target.at[:, pl.ds(at, source.shape[1])], sems.at[number]
                )
            )
            at += source.shape[1]
    greet(chips, owners if group_gather_ins or group_scatter_ins else 1)
    for copy in copies:
        copy.start()
    plan(transfers, chips, bits)
    for copy in copies:
        copy.wait()


def comm_call(
    plan,
    number,
    name,
    parts,
    owners,
    micros,
    scatter=(),
    gather=(),
    group_gather=(),
    group_scatter=(),
    chained=0,
    packs=(),
):
    chips = parts // 2
    flat = [array for item in scatter for array in item]
    operands = [*flat, *gather, *(g[0] for g in group_gather), *group_scatter]
    operands += [item[0] for pack in packs for item in pack]
    in_specs = (
        [VMEM] * len(flat)
        + [ANY] * (len(gather) + len(group_gather))
        + [VMEM] * len(group_scatter)
        + [ANY] * sum(len(pack) for pack in packs)
    )
    shapes, out_specs, scratch = [], [], []
    if scatter:
        rows = flat[0].shape[0] // parts
        widths = [item[0].shape[1] if len(item) == 1 else item[1].shape[0] for item in scatter]
        shapes += [jax.ShapeDtypeStruct((rows, width), F32) for width in widths]
        out_specs += [VMEM] * len(widths)
        scratch += scatter_scratch(chips, rows, sum(widths))
    for array in gather:
        shapes.append(jax.ShapeDtypeStruct((parts * array.shape[0], array.shape[1]), array.dtype))
        out_specs.append(ANY)
        scratch += gather_sems(chips, array.shape[0])
    for array, unused, (rows, width) in group_gather:
        shapes.append(jax.ShapeDtypeStruct((owners * rows, width), array.dtype))
        out_specs.append(ANY)
        scratch += group_gather_sems(owners)
    for array in group_scatter:
        rows, width = array.shape[0] // owners, array.shape[1]
        shapes.append(jax.ShapeDtypeStruct((rows, width), BF16))
        out_specs.append(VMEM)
        scratch += group_scatter_scratch(owners, rows, width)
    for array in group_scatter[:chained]:
        rows, width = array.shape[0] // owners, array.shape[1]
        shapes.append(jax.ShapeDtypeStruct((parts * rows, width), BF16))
        out_specs.append(ANY)
        scratch += gather_sems(chips, rows)
    for pack in packs:
        width = sum(item[2][1] for item in pack)
        shapes.append(jax.ShapeDtypeStruct((pack[0][2][0], width), pack[0][0].dtype))
        out_specs.append(ANY)
        scratch.append(pltpu.SemaphoreType.DMA((len(pack),)))
    counts = {
        "scatter_ins": [len(item) for item in scatter],
        "scatter": len(widths) if scatter else 0,
        "gather": len(gather),
        "group_scatter": len(group_scatter),
        "chained": chained,
    }
    views = ([g[1] for g in group_gather], [[item[1] for item in pack] for pack in packs])
    return pl.pallas_call(
        functools.partial(comm_kernel, plan, chips, owners, counts, views),
        out_shape=tuple(shapes),
        in_specs=in_specs,
        out_specs=tuple(out_specs),
        scratch_shapes=scratch,
        compiler_params=comm_params(number),
        cost_estimate=comm_cost(micros),
        name=name,
    )(*operands)


def plan_gather(transfers, chips, bits):
    ends = transfers["group_gather"]
    for one in transfers["gather"] + ends:
        one.start()
    for number in range(1, chips):
        for one in transfers["gather"]:
            one.step(number)
        if number < bits:
            for one in ends:
                one.step(number - 1)
    for number in range(min(bits, chips) - 1, bits):
        for one in ends:
            one.step(number)
    for one in transfers["gather"] + ends:
        one.finish()


def plan_scatter(transfers, chips, bits):
    scatter = transfers["scatter"]
    beside = transfers["group_scatter"] + transfers["group_gather"]
    for one in beside:
        one.start()
    scatter.start()
    scatter.pairs()
    for one in transfers["gather"]:
        one.start()
    for number in range(chips - 1):
        scatter.step(number)
        for one in transfers["gather"]:
            one.step(number + 1)
        if number < bits - 1:
            for one in beside:
                one.step(number)
    scatter.finish()
    for number in range(min(bits, chips) - 1, bits):
        for one in beside:
            one.step(number)
    for one in transfers["gather"] + beside:
        one.finish()


def plan_finish(transfers, chips, bits):
    scatters, chained = transfers["group_scatter"], transfers["chained"]
    for one in transfers["gather"] + scatters:
        one.start()
    for stage in range(bits):
        for one in scatters:
            one.step(stage)
    for one in chained:
        one.start()
    for number in range(1, chips):
        for one in transfers["gather"] + chained:
            one.step(number)
    for one in transfers["gather"] + chained + scatters:
        one.finish()


def plan_group_scatter(transfers, chips, bits):
    scatters, chained = transfers["group_scatter"], transfers["chained"]
    steps = [(one, stage) for one in scatters for stage in range(bits)]
    for one in scatters[:2]:
        one.start()
    waiting = list(scatters[2:])
    hops = []
    for one, stage in steps:
        one.step(stage)
        if stage == 0 and waiting:
            waiting.pop(0).start()
        at = scatters.index(one)
        if hops:
            hops.pop(0)()
        if stage == bits - 1 and at < len(chained):
            chained[at].start()
            hops += [functools.partial(chained[at].step, d) for d in range(1, chips)]
    for hop in hops:
        hop()
    for one in chained + scatters:
        one.finish()


def comm_params(number, limit=48):
    return pltpu.CompilerParams(
        collective_id=number, has_side_effects=True, vmem_limit_bytes=limit * 2**20
    )


def comm_cost(micros):
    return pl.CostEstimate(flops=0, bytes_accessed=int(micros * 3.4e4), transcendentals=0)


ANY = pl.BlockSpec(memory_space=pl.ANY)
VMEM = pl.BlockSpec(memory_space=pltpu.VMEM)


def after(values, *earlier):
    tied = lax.optimization_barrier((values, earlier))[0]
    return tied


class GroupSum:
    def __init__(self, partial, owners, group, flip):
        self.owners, self.group = owners, group
        self.rows = partial.shape[0] // owners
        bits = list(range(owners.bit_length() - 1))
        self.order = bits[::-1] if flip else bits
        self.held = {piece: None for piece in range(owners)}
        self.partial = partial

    def piece(self, number):
        if self.held[number] is not None:
            return self.held[number]
        start = (self.group ^ number) * self.rows
        return lax.dynamic_slice_in_dim(self.partial, start, self.rows, 0)

    def send(self):
        bit = self.order.pop(0)
        self.keep = [piece for piece in self.held if not piece >> bit & 1]
        self.sent = jnp.stack([self.piece(piece | 1 << bit) for piece in self.keep])
        pairs = [(i, i ^ 1 << bit) for i in range(self.owners)]
        self.got = lax.ppermute(self.sent, "group", pairs)
        return self.sent

    def add(self, *earlier):
        got = after(self.got, *earlier)
        self.held = {
            piece: (self.piece(piece).astype(F32) + got[at].astype(F32)).astype(BF16)
            for at, piece in enumerate(self.keep)
        }


def finish_all(sums):
    for one in sums:
        while one.order:
            one.send()
            one.add()


def send_all(sums):
    return [one.send() for one in sums]


def add_all(sums, *earlier):
    for one in sums:
        one.add(*earlier)


def widen_kernel(counts, *refs):
    sources, targets = refs[: len(counts)], refs[-sum(counts) :]
    at = 0
    for source, count in zip(sources, counts, strict=True):
        for number in range(count):
            targets[at][0, 0] = source[0, number].astype(F32)
            at += 1


def widen(packs, number, experts, previous=()):
    parts, unused, shard, width = packs[0].shape
    counts = [pack.shape[1] for pack in packs]
    total = sum(counts)
    shape = jax.ShapeDtypeStruct((parts, experts, shard, width), F32)
    block = pl.BlockSpec((1, 1, shard // 2, width), lambda c, h: (c, number, h, 0))
    return pl.pallas_call(
        functools.partial(widen_kernel, counts),
        out_shape=(shape,) * total,
        grid=(parts, 2),
        in_specs=[
            pl.BlockSpec((1, count, shard // 2, width), lambda c, h: (c, 0, h, 0))
            for count in counts
        ]
        + [ANY] * len(previous),
        out_specs=(block,) * total,
        input_output_aliases={len(packs) + i: i for i in range(len(previous))},
        cost_estimate=pl.CostEstimate(
            flops=0, bytes_accessed=sum(p.size for p in packs) // 16, transcendentals=0
        ),
        name="widen",
    )(*packs, *previous)


def finish_attention_kernel(
    sharers,
    packed_ref,
    query_ref,
    key_ref,
    value_ref,
    q_ref,
    k_ref,
    v_ref,
    o_ref,
    router_ref,
    rows_ref,
    sums_ref,
):
    width = o_ref.shape[1]
    share = 2 * HD // sharers
    at = pl.program_id(0)
    o_ref[...] = packed_ref[0, :, :width].astype(F32)
    query = packed_ref[0, :, width : 2 * width].astype(F32)
    q_ref[...] = query
    gain = jnp.sum(query * query_ref[...].astype(F32), axis=1, keepdims=True)
    small = packed_ref[0, :, 2 * width + share :].astype(F32)

    @pl.when(at == 0)
    def _():
        sums_ref[...] = jnp.zeros_like(sums_ref)

    lane = lax.broadcasted_iota(jnp.int32, small.shape, 1)
    sums_ref[...] += small + jnp.where(lane == EXPERTS + 3, gain, 0.0)
    for number in range(sharers):

        @pl.when(lax.rem(at, sharers) == number)
        def _():
            piece = packed_ref[0, :, 2 * width : 2 * width + share].astype(F32)
            start = number * share
            if start < HD:
                weight = key_ref[:, start : start + share]
                k_ref[:, start : start + share] = piece
            else:
                weight = value_ref[:, start - HD : start - HD + share]
                v_ref[:, start - HD : start - HD + share] = piece
            more = jnp.sum(piece * weight.astype(F32), axis=1, keepdims=True)
            sums_ref[...] += jnp.where(lane == EXPERTS + 3, more, 0.0)

    @pl.when(at == pl.num_programs(0) - 1)
    def _():
        router_ref[...] = sums_ref[:, :EXPERTS]
        rows_ref[...] = jnp.transpose(sums_ref[...], (1, 0))[EXPERTS : EXPERTS + 8, :]


def finish_attention(packed, weights, width, sharers):
    parts, shard, total = packed.shape
    spare = total - 2 * width - 2 * HD // sharers
    head = pl.BlockSpec((shard, HD), lambda c: (0, c // sharers))
    own = pl.BlockSpec((shard, width), lambda c: (0, c))
    whole = lambda c: (0, 0)
    return pl.pallas_call(
        functools.partial(finish_attention_kernel, sharers),
        out_shape=(
            jax.ShapeDtypeStruct((shard, width * parts), F32),
            jax.ShapeDtypeStruct((shard, HK * HD), F32),
            jax.ShapeDtypeStruct((shard, HK * HD), F32),
            jax.ShapeDtypeStruct((shard, width * parts), F32),
            jax.ShapeDtypeStruct((shard, EXPERTS), F32),
            jax.ShapeDtypeStruct((8, shard), F32),
        ),
        grid_spec=pltpu.PrefetchScalarGridSpec(
            num_scalar_prefetch=0,
            grid=(parts,),
            in_specs=[pl.BlockSpec((1, shard, total), lambda c: (c, 0, 0)), own, head, head],
            out_specs=(
                own,
                head,
                head,
                own,
                pl.BlockSpec((shard, EXPERTS), whole),
                pl.BlockSpec((8, shard), whole),
            ),
            scratch_shapes=[pltpu.VMEM((shard, spare), F32)],
        ),
        cost_estimate=pl.CostEstimate(flops=0, bytes_accessed=packed.size // 16, transcendentals=0),
        name="finish_attention",
    )(packed, *weights)


def per_device(
    tokens,
    positions,
    expert_ids,
    cotangent,
    attention_gain,
    query_weight,
    key_weight,
    value_weight,
    output_weight,
    query_gain,
    key_gain,
    mixture_gain,
    router_weight,
    gate_weight,
    up_weight,
    down_weight,
):
    parts, owners = lax.axis_size("ctx"), lax.axis_size("group")
    here, group = lax.axis_index("ctx"), lax.axis_index("group")
    rows = tokens.shape[1]
    length = rows * parts
    shard = query_weight.shape[0]
    width = HQ * HD // parts
    experts = EXPERTS // parts
    sharers = parts // HK
    key_head = here // sharers
    share = 2 * HD // sharers
    share_at = (here % sharers) * share

    gather_group = lambda v: lax.all_gather(v, "group", axis=0, tiled=True)

    def column(vector):
        return jnp.pad(vector, (0, shard - vector.shape[0]))[:, None]

    def columns(array, start, count):
        return lax.dynamic_slice_in_dim(array, start, count, 1)

    extras = jnp.concatenate(
        [
            router_weight,
            attention_gain[:, None],
            mixture_gain[:, None],
            column(query_gain),
            column(key_gain),
            jnp.zeros((shard, PAD - EXPERTS - 4), BF16),
        ],
        axis=1,
    )
    comm = lambda plan, number, name, micros, **transfers: comm_call(
        plan, number, name, parts, owners, micros, **transfers
    )
    def expert_pack(number, at):
        return jnp.concatenate(
            [
                lax.dynamic_index_in_dim(w, at * experts + number, 0, keepdims=False)
                for w in (gate_weight, up_weight, down_weight)
            ],
            axis=1,
        )

    packs = [expert_pack(number, here) for number in range(experts)]
    extras = after(extras, *packs)

    def cut(start, count):
        return lambda ref: ref.at[:, pl.ds(pl.multiple_of(start(), count), count)]

    place = lambda: lax.axis_index("ctx")
    key_cut = cut(lambda: place() // sharers * HD, HD)
    own_cut = cut(lambda: place() * width, width)

    inputs_all, positions_all, extras, wquery, wkey, wvalue, wout = comm(
        plan_gather,
        0,
        "gather_tokens",
        45,
        gather=(tokens[0], jnp.broadcast_to(positions, (8, rows))),
        group_gather=(
            (extras, lambda ref: ref, (shard, PAD)),
            (query_weight, own_cut, (shard, width)),
            (key_weight, key_cut, (shard, HD)),
            (value_weight, key_cut, (shard, HD)),
            (output_weight, own_cut, (shard, width)),
        ),
    )
    packs = [gather_group(after(pack, positions_all)) for pack in packs]
    wqkv = jnp.concatenate([wquery, wkey, wvalue], axis=1)

    router = extras[:, :EXPERTS]
    attention_gains = extras[:, EXPERTS].astype(F32)
    mixture_gains = extras[:, EXPERTS + 1].astype(F32)
    head_gain = (
        lambda col: extras[:, col]
        .reshape(owners, shard)[:, : HD // owners]
        .reshape(1, HD)
        .astype(F32)
    )
    query_gains, key_gains = head_gain(EXPERTS + 2), head_gain(EXPERTS + 3)

    positions_all = positions_all.reshape(parts, 8, rows)[:, 0].reshape(length)
    doc_start = (jnp.arange(length, dtype=jnp.int32) - positions_all)[:, None]
    inputs = tokens[0].astype(F32)
    unused, attn_factor = rms_parts(inputs, attention_gains)
    normed_all = rms_parts(inputs_all.astype(F32), attention_gains)[0].astype(BF16)
    qkv_raw = dot(normed_all, wqkv)
    tables = (qkv_raw, doc_start, rope_tables(positions_all), query_gains, key_gains)
    mixed_low = attend(*tables)
    attn_out, upstream_all = comm(
        plan_scatter,
        1,
        "scatter_attention",
        50,
        scatter=((mixed_low, wout),),
        gather=(cotangent[0],),
    )
    hidden = inputs + attn_out
    moe_normed, moe_factor = rms_parts(hidden, mixture_gains)
    moe_low = moe_normed.astype(BF16)
    logits = dot(moe_low, router)
    onehot = (
        expert_ids[0][:, :, None] == jnp.arange(EXPERTS, dtype=jnp.int32)[None, None, :]
    ).astype(F32)
    chosen = jnp.sum(onehot * logits[:, None, :], axis=-1)
    expo = jnp.exp(chosen - jnp.max(chosen, axis=-1, keepdims=True))
    gates = expo / jnp.sum(expo, axis=-1, keepdims=True)
    combine = jnp.sum(gates[:, :, None] * onehot, axis=1)
    moe_all, combine_all = comm(
        plan_gather,
        2,
        "gather_mixture",
        45,
        gather=(moe_low, jnp.pad(combine, ((0, 0), (0, PAD - EXPERTS)))),
    )
    combine_all = columns(combine_all, here * experts, experts)

    def expert_forward(number, weights, gate_all):
        up_all = dot(moe_all, weights[1])
        sigmoid = lax.logistic(gate_all)
        act_low = (gate_all * sigmoid * up_all).astype(BF16)
        weighted = (combine_all[:, number : number + 1] * act_low.astype(F32)).astype(BF16)
        return gate_all, up_all, act_low, weighted

    def expert_back(number, gate_all, up_all, act_low, weights):
        back_all = dot(upstream_all, weights[2])
        sigmoid = lax.logistic(gate_all)
        combine_grad = jnp.sum(act_low.astype(F32) * back_all, axis=-1, keepdims=True)
        act_grad = combine_all[:, number : number + 1] * back_all
        gate_grad = (act_grad * up_all * sigmoid * (1.0 + gate_all * (1.0 - sigmoid))).astype(BF16)
        up_grad = (act_grad * gate_all * sigmoid).astype(BF16)
        return combine_grad, gate_grad, up_grad

    def weight_grad(left, right):
        return dot_tn(left, right).astype(BF16)

    split = lambda pack: (pack[:, :F], pack[:, F : 2 * F], pack[:, 2 * F :])
    weights = split(packs[0])
    gate_all = dot(moe_all, weights[0])
    gate_all, up_all, act_low, weighted = expert_forward(0, weights, gate_all)
    combine_grads, layer_terms, moe_terms, gathered = [], [], [], []
    last_grads = [weight_grad(upstream_all, weighted)]
    for number in range(1, experts):
        half = F // 2
        down_sums = [
            GroupSum(last_grads[0][:, :half], owners, group, False),
            GroupSum(last_grads[0][:, half:], owners, group, True),
        ]
        gate_all, up_all = after((gate_all, up_all), *send_all(down_sums))
        combine_grad, gate_grad, up_grad = expert_back(
            number - 1, gate_all, up_all, act_low, weights
        )
        combine_grads.append(combine_grad)
        layer_terms.append((weighted, weights[2]))
        moe_terms += [(gate_grad, weights[0]), (up_grad, weights[1])]
        grads = weight_grad(moe_all, gate_grad), weight_grad(moe_all, up_grad)
        layer_part = dot_nt(weighted, weights[2])
        add_all(down_sums, layer_part, *grads)
        sent = send_all(down_sums) if down_sums[0].order else []
        other_sums = [
            GroupSum(after(grads[0], *sent), owners, group, False),
            GroupSum(after(grads[1], *sent), owners, group, True),
        ]
        weights = split(after(packs[number], *send_all(other_sums)))
        gate_all = dot(moe_all, weights[0])
        add_all(down_sums, gate_all)
        finish_all(down_sums)
        down = jnp.concatenate([one.held[0] for one in down_sums], axis=1)
        weights = (weights[0], after(weights[1], down), weights[2])
        gate_all, up_all, act_low, weighted = expert_forward(number, weights, gate_all)
        last_grads = [weight_grad(upstream_all, weighted)]
        gathered.append([down.reshape(2, shard // 2, F), other_sums])
    combine_grad, gate_grad, up_grad = expert_back(
        experts - 1, gate_all, up_all, act_low, weights
    )
    combine_grads.append(combine_grad)
    layer_terms.append((weighted, weights[2]))
    moe_terms += [(gate_grad, weights[0]), (up_grad, weights[1])]
    last_grads += [weight_grad(moe_all, gate_grad), weight_grad(moe_all, up_grad)]
    for pieces in gathered:
        add_all(pieces[1], *last_grads)
        if pieces[1][0].order:
            moe_terms = after(moe_terms, *send_all(pieces[1]))
    moe_part = sum(dot_nt(left, right) for left, right in moe_terms[:2])
    layer_part = sum(dot_nt(left, right) for left, right in layer_terms)
    for pieces in gathered:
        add_all(pieces[1], moe_part, layer_part)
        finish_all(pieces[1])
        pieces[1] = jnp.stack([one.held[0] for one in pieces[1]])
        moe_terms[2:] = after(moe_terms[2:], pieces[1])
    for left, right in moe_terms[2:]:
        moe_part = moe_part + dot_nt(left, right)
    moe_part_low = moe_part.astype(BF16)
    combine_grad = jnp.concatenate(combine_grads, axis=1)
    high = combine_grad.astype(BF16).astype(F32)
    low = combine_grad - high
    at = jnp.arange(PAD, dtype=jnp.int32)[None, :]
    small = sum(
        jnp.where(at == here * experts + number, high[:, number : number + 1], 0.0)
        + jnp.where(at == EXPERTS + here * experts + number, low[:, number : number + 1], 0.0)
        for number in range(experts)
    ).astype(BF16)
    moe_sum, small_sum, *last_pieces = comm(
        plan_scatter,
        3,
        "scatter_mixture",
        60,
        scatter=((moe_part_low,), (small,)),
        group_scatter=last_grads,
    )
    gathered.append([jnp.stack(last_pieces)])
    unfold = lambda piece: lax.all_gather(piece, "ctx").reshape(parts, -1, shard, F)
    expert_packs = [[unfold(piece) for piece in pieces] for pieces in gathered]

    dcombine = small_sum[:, :EXPERTS] + small_sum[:, EXPERTS : 2 * EXPERTS]
    gates_grad = jnp.sum(onehot * dcombine[:, None, :], axis=-1)
    chosen_grad = gates * (gates_grad - jnp.sum(gates * gates_grad, axis=-1, keepdims=True))
    logit_grad_low = jnp.sum(chosen_grad[:, :, None] * onehot, axis=1).astype(BF16)
    router_partial = dot_tn(moe_low, logit_grad_low)
    moe_grad = moe_sum + dot_nt(logit_grad_low, router)
    hidden_part, mixture_terms = rms_back(hidden, moe_factor, mixture_gains, moe_grad)
    mixture_partial = jnp.sum(mixture_terms, axis=0)
    hidden_grad = cotangent[0].astype(F32) + hidden_part

    (attn_grad_all,) = comm(
        plan_gather,
        4,
        "gather_attention",
        45,
        gather=(
            after(hidden_grad.astype(BF16), *(pack[0] for pack in expert_packs[:-1])),
        ),
    )
    mixed_grad = dot(attn_grad_all, wout).astype(BF16)
    output_partial = weight_grad(attn_grad_all, mixed_low)
    output_sums = [
        GroupSum(output_partial[:, : width // 2], owners, group, False),
        GroupSum(output_partial[:, width // 2 :], owners, group, True),
    ]
    mixed_grad = after(mixed_grad, *send_all(output_sums))
    query_low, kv_part, query_terms, key_terms = attend_back(*tables, mixed_grad)
    step = 1
    while step < sharers:
        kv_part = kv_part + lax.ppermute(kv_part, "ctx", [(i, i ^ step) for i in range(parts)])
        step *= 2
    kv_low = columns(kv_part.astype(BF16), share_at, share)
    qkv_low = jnp.concatenate([query_low, kv_low], axis=1)
    wqkv_share = jnp.concatenate(
        [wqkv[:, :width], columns(wqkv[:, width:], share_at, share)], axis=1
    )
    def head_column(terms):
        spread = terms.reshape(owners, HD // owners)
        return jnp.pad(spread, ((0, 0), (0, shard - HD // owners))).reshape(D, 1)

    add_all(output_sums, qkv_low)
    qkv_tied = qkv_low
    if output_sums[0].order:
        qkv_tied = after(qkv_low, *send_all(output_sums))
    spare = next(n for n in range(EXPERTS + 8, 1024) if (width + share + n) % 256 == 0)
    grad_extras = jnp.concatenate(
        [
            router_partial,
            mixture_partial[:, None],
            head_column(query_terms),
            head_column(key_terms),
        ],
        axis=1,
    )
    grad_extras = jnp.pad(grad_extras, ((0, 0), (width + share, spare - EXPERTS - 3)))
    qkv_wide = jnp.pad(qkv_tied, ((0, 0), (0, spare)))
    qkv_partial = (dot_tn(normed_all, qkv_wide) + grad_extras).astype(BF16)
    layer_sum, qkv_piece = comm(
        plan_scatter,
        6,
        "scatter_grads",
        60,
        scatter=((layer_part.astype(BF16),),),
        group_scatter=(after(qkv_partial, *(pack[-1] for pack in expert_packs[:-1])),),
    )
    layer_out = (hidden + layer_sum).astype(BF16)[None]
    add_all(output_sums, qkv_piece)
    finish_all(output_sums)
    attn_piece = jnp.concatenate([one.held[0] for one in output_sums] + [qkv_piece], axis=1)
    attn_grads = lax.all_gather(attn_piece, "ctx")
    (normed_grad,) = comm(
        plan_scatter,
        5,
        "scatter_normed",
        60,
        scatter=((after(qkv_low, attn_piece), wqkv_share),),
    )
    input_part, unused = rms_back(inputs, attn_factor, attention_gains, normed_grad)
    tokens_grad = (hidden_grad + input_part).astype(BF16)[None]
    query_grad, key_grad, value_grad, output_grad, router_grad, gain_rows = finish_attention(
        attn_grads, (query_weight, key_weight, value_weight), width, sharers
    )
    finished = ()
    for number in range(experts):
        finished = widen(expert_packs[number], number, experts, finished)
    whole = lambda v: v.reshape(EXPERTS, shard, F)
    return (
        layer_out,
        tokens_grad,
        gain_rows[3] / attention_gain.astype(F32),
        query_grad,
        key_grad,
        value_grad,
        output_grad,
        gain_rows[1, : HD // owners],
        gain_rows[2, : HD // owners],
        gain_rows[0],
        router_grad,
        whole(finished[1]),
        whole(finished[2]),
        whole(finished[0]),
    )


def solution(mesh):
    return jax.shard_map(
        per_device,
        mesh=mesh,
        in_specs=(
            P("group", "ctx", None),
            P("group", "ctx"),
            P("group", "ctx", None),
            P("group", "ctx", None),
            P("group"),
            P("group", None),
            P("group", None),
            P("group", None),
            P("group", None),
            P("group"),
            P("group"),
            P("group"),
            P("group", None),
            P(None, "group", None),
            P(None, "group", None),
            P(None, "group", None),
        ),
        out_specs=(
            P("group", "ctx", None),
            P("group", "ctx", None),
            P("group"),
            P("group", None),
            P("group", None),
            P("group", None),
            P("group", None),
            P("group"),
            P("group"),
            P("group"),
            P("group", None),
            P(None, "group", None),
            P(None, "group", None),
            P(None, "group", None),
        ),
        check_vma=False,
    )
```

```python
import functools

import jax
import jax.numpy as jnp
from jax import lax
from jax.experimental import pallas as pl
from jax.experimental.pallas import tpu as pltpu
from jax.sharding import PartitionSpec as P

D = 2048
HQ = 32
HK = 4
HD = 128
F = 768
TOPK = 8
EXPERTS = 16
PAD = 128

EPS = 1e-06
ROPE_BASE = 1000000.0
FLOOR = -1e30
F32 = jnp.float32
BF16 = jnp.bfloat16


def rms_parts(values, gains):
    factor = lax.rsqrt(jnp.mean(values * values, axis=-1, keepdims=True) + EPS)
    return (values * factor * gains, factor)


def rms_back(values, factor, gains, gradient):
    weighted = gradient * gains
    inner = jnp.mean(weighted * values, axis=-1, keepdims=True)
    grad_values = factor * weighted - values * (factor * factor * factor) * inner
    return (grad_values, gradient * values * factor)


def dot(left, right):
    return jnp.dot(left, right, preferred_element_type=F32)


def dot_nt(left, right):
    return lax.dot_general(left, right, (((1,), (1,)), ((), ())), preferred_element_type=F32)


def dot_tn(left, right):
    return lax.dot_general(left, right, (((0,), (0,)), ((), ())), preferred_element_type=F32)


def rope_tables(position_row):
    frequency = ROPE_BASE ** (-2.0 * jnp.arange(HD // 2, dtype=F32) / HD)
    angles = position_row.astype(F32)[:, None] * frequency[None, :]
    cosine, sine = jnp.cos(angles), jnp.sin(angles)
    return jnp.concatenate([cosine, cosine, -sine, sine], axis=-1)


def turn(values):
    return pltpu.roll(values, HD // 2, 1)


def normed_rope(raw, gains, cosine, sine):
    normed, factor = rms_parts(raw, gains)
    return (normed * cosine + turn(normed) * sine, factor)


def softmax_weights(query, key_ref, doc_start, number):
    rows = query.shape[0]
    scale = HD**-0.5 * 1.4426950408889634
    parts = []
    if number:
        columns = number * rows
        key_index = lax.broadcasted_iota(jnp.int32, (rows, columns), 1)
        scores = dot_nt(query, key_ref[:columns, :]) * scale
        parts.append(jnp.where(key_index >= doc_start, scores, FLOOR))
    row_index = lax.broadcasted_iota(jnp.int32, (rows, rows), 0)
    key_index = lax.broadcasted_iota(jnp.int32, (rows, rows), 1)
    allowed = (key_index <= row_index) & (key_index >= doc_start - number * rows)
    scores = dot_nt(query, key_ref[number * rows : (number + 1) * rows, :]) * scale
    parts.append(jnp.where(allowed, scores, FLOOR))
    masked = jnp.concatenate(parts, axis=1) if number else parts[0]
    weights = jnp.exp2(masked - jnp.max(masked, axis=-1, keepdims=True))
    return weights, 1.0 / jnp.sum(weights, axis=-1, keepdims=True)


def attend_kernel(
    block, q_ref, kv_ref, doc_ref, cos_ref, sin_ref, qg_ref, kg_ref, out_ref, key_ref, val_ref
):
    @pl.when(pl.program_id(0) == 0)
    def _():
        key, unused = normed_rope(kv_ref[:, :HD], kg_ref[...], cos_ref[...], sin_ref[...])
        key_ref[...] = key.astype(BF16)
        val_ref[...] = kv_ref[:, HD:].astype(BF16)

    for number in range(kv_ref.shape[0] // block):
        rows = pl.ds(number * block, block)
        query, unused = normed_rope(q_ref[rows, :], qg_ref[...], cos_ref[rows, :], sin_ref[rows, :])
        weights, share = softmax_weights(query.astype(BF16), key_ref, doc_ref[rows, :], number)
        mixed = dot(weights.astype(BF16), val_ref[: (number + 1) * block, :])
        out_ref[rows, :] = (mixed * share).astype(BF16)


def attend_back_kernel(
    block,
    q_ref,
    kv_ref,
    doc_ref,
    cos_ref,
    sin_ref,
    qg_ref,
    kg_ref,
    dm_ref,
    dq_ref,
    dkv_ref,
    qt_ref,
    kt_ref,
    key_ref,
    val_ref,
    dk_ref,
    dv_ref,
):
    head = pl.program_id(0)
    scaling = HD**-0.5

    @pl.when(head == 0)
    def _():
        key, unused = normed_rope(kv_ref[:, :HD], kg_ref[...], cos_ref[...], sin_ref[...])
        key_ref[...] = key.astype(BF16)
        val_ref[...] = kv_ref[:, HD:].astype(BF16)
        dk_ref[...] = jnp.zeros_like(dk_ref)
        dv_ref[...] = jnp.zeros_like(dv_ref)
        qt_ref[...] = jnp.zeros_like(qt_ref)

    for number in range(kv_ref.shape[0] // block):
        rows = pl.ds(number * block, block)
        columns = (number + 1) * block
        cosine, sine = cos_ref[rows, :], sin_ref[rows, :]
        raw = q_ref[rows, :]
        query, factor = normed_rope(raw, qg_ref[...], cosine, sine)
        query = query.astype(BF16)
        key, value = key_ref[:columns, :], val_ref[:columns, :]
        upstream = dm_ref[rows, :]
        weights, share = softmax_weights(query, key_ref, doc_ref[rows, :], number)
        probs = weights * share
        prob_grad = dot_nt(upstream, value)
        delta = jnp.sum(probs * prob_grad, axis=-1, keepdims=True)
        score_grad = (probs * (prob_grad - delta)).astype(BF16)
        dk_ref[:columns, :] += dot_tn(score_grad, query)
        dv_ref[:columns, :] += dot_tn(probs.astype(BF16), upstream)
        rotated = dot(score_grad, key) * scaling
        query_grad = rotated * cosine - turn(rotated) * sine
        raw_grad, terms = rms_back(raw, factor, qg_ref[...], query_grad)
        dq_ref[rows, :] = raw_grad.astype(BF16)
        qt_ref[...] += jnp.sum(terms, axis=0, keepdims=True)

    @pl.when(head == pl.num_programs(0) - 1)
    def _():
        raw = kv_ref[:, :HD]
        cosine, sine = cos_ref[...], sin_ref[...]
        unused, factor = rms_parts(raw, kg_ref[...])
        rotated = dk_ref[...] * scaling
        key_grad = rotated * cosine - turn(rotated) * sine
        raw_grad, terms = rms_back(raw, factor, kg_ref[...], key_grad)
        dkv_ref[:, :HD] = raw_grad
        dkv_ref[:, HD:] = dv_ref[...]
        kt_ref[...] = jnp.sum(terms, axis=0, keepdims=True)


def attention_specs(length, heads):
    whole = lambda h: (0, 0)
    return [
        pl.BlockSpec((length, HD), lambda h: (0, h)),
        pl.BlockSpec((length, 2 * HD), lambda h: (0, heads // 2)),
        pl.BlockSpec((length, 1), whole),
        pl.BlockSpec((length, HD), whole),
        pl.BlockSpec((length, HD), lambda h: (0, 1)),
        pl.BlockSpec((1, HD), whole),
        pl.BlockSpec((1, HD), whole),
    ]


def attend(qkv_raw, doc_start, tables, query_gain, key_gain):
    length, width = qkv_raw.shape[0], qkv_raw.shape[1] - 2 * HD
    return pl.pallas_call(
        functools.partial(attend_kernel, 256),
        out_shape=jax.ShapeDtypeStruct((length, width), BF16),
        grid_spec=pltpu.PrefetchScalarGridSpec(
            num_scalar_prefetch=0,
            grid=(width // HD,),
            in_specs=attention_specs(length, width // HD),
            out_specs=pl.BlockSpec((length, HD), lambda h: (0, h)),
            scratch_shapes=[pltpu.VMEM((length, HD), BF16), pltpu.VMEM((length, HD), BF16)],
        ),
        compiler_params=pltpu.CompilerParams(vmem_limit_bytes=40 * 2**20),
        cost_estimate=pl.CostEstimate(
            flops=length * length, bytes_accessed=length * width, transcendentals=0
        ),
        name="attend",
    )(qkv_raw, qkv_raw, doc_start, tables, tables, query_gain, key_gain)


def attend_back(qkv_raw, doc_start, tables, query_gain, key_gain, upstream):
    length, width = qkv_raw.shape[0], qkv_raw.shape[1] - 2 * HD
    whole = lambda h: (0, 0)
    return pl.pallas_call(
        functools.partial(attend_back_kernel, 256),
        out_shape=(
            jax.ShapeDtypeStruct((length, width), BF16),
            jax.ShapeDtypeStruct((length, 2 * HD), F32),
            jax.ShapeDtypeStruct((1, HD), F32),
            jax.ShapeDtypeStruct((1, HD), F32),
        ),
        grid_spec=pltpu.PrefetchScalarGridSpec(
            num_scalar_prefetch=0,
            grid=(width // HD,),
            in_specs=attention_specs(length, width // HD)
            + [pl.BlockSpec((length, HD), lambda h: (0, h))],
            out_specs=(
                pl.BlockSpec((length, HD), lambda h: (0, h)),
                pl.BlockSpec((length, 2 * HD), whole),
                pl.BlockSpec((1, HD), whole),
                pl.BlockSpec((1, HD), whole),
            ),
            scratch_shapes=[
                pltpu.VMEM((length, HD), BF16),
                pltpu.VMEM((length, HD), BF16),
                pltpu.VMEM((length, HD), F32),
                pltpu.VMEM((length, HD), F32),
            ],
        ),
        compiler_params=pltpu.CompilerParams(vmem_limit_bytes=40 * 2**20),
        cost_estimate=pl.CostEstimate(
            flops=length * length, bytes_accessed=length * width, transcendentals=0
        ),
        name="attend_back",
    )(qkv_raw, qkv_raw, doc_start, tables, tables, query_gain, key_gain, upstream)


def ctx_place():
    here = lax.axis_index("ctx")
    return (here // 2, lax.rem(here, 2))


def peer(chip, core):
    return {"ctx": 2 * chip + core}


def greet(chips, owners=1):
    chip, core = ctx_place()
    group = lax.axis_index("group")
    barrier = pltpu.get_barrier_semaphore()
    pl.semaphore_signal(barrier, inc=1, device_id=peer(chip, 1 - core))

    @pl.when(chip > 0)
    def _():
        pl.semaphore_signal(barrier, inc=1, device_id=peer(chip - 1, core))

    @pl.when(chip < chips - 1)
    def _():
        pl.semaphore_signal(barrier, inc=1, device_id=peer(chip + 1, core))

    bits = owners.bit_length() - 1
    for bit in range(bits):
        pl.semaphore_signal(barrier, inc=1, device_id={"group": group ^ (1 << bit)})
    count = 1 + bits + (chip > 0).astype(jnp.int32) + (chip < chips - 1).astype(jnp.int32)
    pl.semaphore_wait(barrier, count)


class Gather:
    def __init__(self, chips, source, target, sems):
        self.chips, self.source, self.target = chips, source, target
        self.up, self.down, self.side, self.near, self.cross, self.local = sems
        self.chip, self.core = ctx_place()
        self.rows = source.shape[0]
        self.chunks = range(chunk_count(self.rows))
        self.piece = self.rows // len(self.chunks)

    def block(self, chip, core, chunk):
        start = (2 * chip + core) * self.rows + chunk * self.piece
        return self.target.at[pl.ds(pl.multiple_of(start, self.piece), self.piece)]

    def hop(self, origin, chunk, sem, arrive, device, own):
        source = self.block(origin, self.core, chunk)
        if own:
            source = self.source.at[pl.ds(chunk * self.piece, self.piece)]
        return pltpu.make_async_remote_copy(
            src_ref=source,
            dst_ref=self.block(origin, self.core, chunk),
            send_sem=sem.at[origin, chunk],
            recv_sem=arrive.at[origin, chunk],
            device_id=device,
        )

    def to_up(self, origin, chunk, own=False):
        return self.hop(origin, chunk, self.up, self.near, peer(self.chip + 1, self.core), own)

    def to_down(self, origin, chunk, own=False):
        return self.hop(origin, chunk, self.down, self.near, peer(self.chip - 1, self.core), own)

    def to_side(self, origin, chunk, own=False):
        return self.hop(origin, chunk, self.side, self.cross, peer(self.chip, 1 - self.core), own)

    def mine(self):
        start = pl.multiple_of((2 * self.chip + self.core) * self.rows, self.rows)
        return pltpu.make_async_copy(
            self.source, self.target.at[pl.ds(start, self.rows)], self.local
        )

    def start(self):
        for chunk in self.chunks:

            @pl.when(self.chip < self.chips - 1)
            def _():
                self.to_up(self.chip, chunk, True).start()

            @pl.when(self.chip > 0)
            def _():
                self.to_down(self.chip, chunk, True).start()

        for chunk in self.chunks:
            self.to_side(self.chip, chunk, True).start()
        self.mine().start()

    def step(self, distance):
        below, above = self.chip - distance, self.chip + distance
        for chunk in self.chunks:

            @pl.when(below >= 0)
            def _():
                self.to_up(below, chunk).wait_recv()

                @pl.when(self.chip < self.chips - 1)
                def _():
                    self.to_up(below, chunk).start()

                self.to_side(below, chunk).start()

            @pl.when(above < self.chips)
            def _():
                self.to_down(above, chunk).wait_recv()

                @pl.when(self.chip > 0)
                def _():
                    self.to_down(above, chunk).start()

                self.to_side(above, chunk).start()

    def finish(self):
        self.mine().wait()
        for origin in range(self.chips):
            for chunk in self.chunks:
                pltpu.make_async_remote_copy(
                    src_ref=self.source.at[pl.ds(chunk * self.piece, self.piece)],
                    dst_ref=self.block(origin, 1 - self.core, chunk),
                    send_sem=self.side.at[origin, chunk],
                    recv_sem=self.cross.at[origin, chunk],
                    device_id=peer(self.chip, 1 - self.core),
                ).wait_recv()
                self.to_side(origin, chunk).wait_send()

                @pl.when((origin <= self.chip) & (self.chip < self.chips - 1))
                def _():
                    self.to_up(origin, chunk).wait_send()

                @pl.when((origin >= self.chip) & (self.chip > 0))
                def _():
                    self.to_down(origin, chunk).wait_send()


def chunk_count(rows):
    return 4 if rows % 64 == 0 else 1


def gather_sems(chips, rows):
    return [pltpu.SemaphoreType.DMA((chips, chunk_count(rows)))] * 5 + [pltpu.SemaphoreType.DMA]


class Scatter:
    def __init__(self, chips, tile, outs, refs):
        self.chips, self.tile, self.outs = chips, tile, outs
        self.give, self.take, self.send, self.low, self.high, *self.sems = refs
        self.chip, self.core = ctx_place()
        self.rows = outs[0].shape[0]
        self.chunks = range(chunk_count(self.rows))
        self.piece = self.rows // len(self.chunks)

    def part(self, ref, target, chunk):
        return ref.at[target, pl.ds(chunk * self.piece, self.piece)]

    def side(self, target):
        return pltpu.make_async_remote_copy(
            src_ref=self.give.at[target],
            dst_ref=self.take.at[target],
            send_sem=self.sems[0].at[target],
            recv_sem=self.sems[1].at[target],
            device_id=peer(self.chip, 1 - self.core),
        )

    def up(self, target, chunk):
        return pltpu.make_async_remote_copy(
            src_ref=self.part(self.send, target, chunk),
            dst_ref=self.part(self.low, target, chunk),
            send_sem=self.sems[2].at[target, chunk],
            recv_sem=self.sems[3].at[target, chunk],
            device_id=peer(self.chip + 1, self.core),
        )

    def down(self, target, chunk):
        return pltpu.make_async_remote_copy(
            src_ref=self.part(self.send, target, chunk),
            dst_ref=self.part(self.high, target, chunk),
            send_sem=self.sems[2].at[target, chunk],
            recv_sem=self.sems[4].at[target, chunk],
            device_id=peer(self.chip - 1, self.core),
        )

    def order(self):
        last = self.chips - 1
        return sorted(range(self.chips), key=lambda target: min(target, last - target))

    def start(self):
        for target in self.order():
            self.give[target] = self.tile(2 * target + 1 - self.core).astype(BF16)
            self.side(target).start()

    def store(self, value):
        at = 0
        for out in self.outs:
            out[...] = value[:, at : at + out.shape[1]]
            at += out.shape[1]

    def pairs(self):
        last = self.chips - 1
        for target in self.order():
            value = self.tile(2 * target + self.core)
            self.side(target).wait_recv()
            value = value + self.take[target].astype(F32)
            self.send[target] = value.astype(BF16)

            @pl.when(self.chip == target)
            def _():
                self.store(value)

            if target == last:

                @pl.when(self.chip == 0)
                def _():
                    for chunk in self.chunks:
                        self.up(target, chunk).start()

            if target == 0:

                @pl.when(self.chip == last)
                def _():
                    for chunk in self.chunks:
                        self.down(target, chunk).start()

    def add(self, target, chunk, ref):
        mine, theirs = self.part(self.send, target, chunk), self.part(ref, target, chunk)
        mine[...] = (mine[...].astype(F32) + theirs[...].astype(F32)).astype(BF16)

    def upward(self, number):
        target = self.chips - 1 - number

        @pl.when(target > self.chip)
        def _():
            for chunk in self.chunks:

                @pl.when(self.chip > 0)
                def _():
                    self.up(target, chunk).wait_recv()
                    self.add(target, chunk, self.low)

                @pl.when((self.chip > 0) | (number > 0))
                def _():
                    self.up(target, chunk).start()

    def downward(self, number):
        last = self.chips - 1

        @pl.when(number < self.chip)
        def _():
            for chunk in self.chunks:

                @pl.when(self.chip < last)
                def _():
                    self.down(number, chunk).wait_recv()
                    self.add(number, chunk, self.high)

                @pl.when((self.chip < last) | (number > 0))
                def _():
                    self.down(number, chunk).start()

    def step(self, number):
        @pl.when(self.chip < self.chips // 2)
        def _():
            self.upward(number)
            self.downward(number)

        @pl.when(self.chip >= self.chips // 2)
        def _():
            self.downward(number)
            self.upward(number)

    def gain(self, target, chunk, ref):
        theirs = self.part(ref, target, chunk)[...].astype(F32)
        rows, at = pl.ds(chunk * self.piece, self.piece), 0
        for out in self.outs:
            out[rows, :] += theirs[:, at : at + out.shape[1]]
            at += out.shape[1]

    def finish(self):
        for target in range(self.chips):

            @pl.when(self.chip == target)
            def _():
                for chunk in self.chunks:
                    if target > 0:
                        self.up(target, chunk).wait_recv()
                        self.gain(target, chunk, self.low)
                    if target < self.chips - 1:
                        self.down(target, chunk).wait_recv()
                        self.gain(target, chunk, self.high)

        for target in range(self.chips):
            self.side(target).wait_send()

            @pl.when(self.chip != target)
            def _():
                for chunk in self.chunks:
                    self.up(target, chunk).wait_send()


def scatter_scratch(chips, rows, width):
    hops = pltpu.SemaphoreType.DMA((chips, chunk_count(rows)))
    return (
        [pltpu.VMEM((chips, rows, width), BF16)] * 5
        + [pltpu.SemaphoreType.DMA((chips,))] * 2
        + [hops] * 3
    )


def row_block(ref, block, rows):
    return ref[pl.ds(pl.multiple_of(block * rows, rows), rows), :]


class GroupGather:
    def __init__(self, owners, source, target, sems):
        self.owners, self.source, self.target = owners, source, target
        self.sent, self.got, self.local = sems
        self.group = lax.axis_index("group")
        self.rows = source.shape[0]
        self.bits = list(range(owners.bit_length() - 1))
        self.orders = (self.bits, self.bits[::-1])

    def piece(self, mask, half):
        start = (self.group ^ mask) * self.rows + half * (self.rows // 2)
        return self.target.at[pl.ds(pl.multiple_of(start, self.rows // 2), self.rows // 2)]

    def held(self, half, stage):
        masks = [0]
        for bit in self.orders[half][:stage]:
            masks += [mask | 1 << bit for mask in masks]
        return masks

    def hop(self, half, stage, mask):
        bit = self.orders[half][stage]
        source = self.piece(mask, half)
        if mask == 0:
            source = self.source.at[pl.ds(half * (self.rows // 2), self.rows // 2)]
        return pltpu.make_async_remote_copy(
            src_ref=source,
            dst_ref=self.piece(mask, half),
            send_sem=self.sent.at[half, stage * self.owners + mask],
            recv_sem=self.got.at[half, mask | 1 << bit],
            device_id={"group": self.group ^ (1 << bit)},
        )

    def mine(self):
        start = pl.multiple_of(self.group * self.rows, self.rows)
        return pltpu.make_async_copy(
            self.source, self.target.at[pl.ds(start, self.rows)], self.local
        )

    def start(self):
        for half in range(2):
            self.hop(half, 0, 0).start()
        self.mine().start()

    def step(self, stage):
        for half in range(2):
            for mask in self.held(half, stage):
                self.hop(half, stage, mask).wait_recv()
            if stage + 1 < len(self.bits):
                for mask in self.held(half, stage + 1):
                    self.hop(half, stage + 1, mask).start()

    def finish(self):
        self.mine().wait()
        for half in range(2):
            for stage in self.bits:
                for mask in self.held(half, stage):
                    self.hop(half, stage, mask).wait_send()


def group_gather_sems(owners):
    bits = owners.bit_length() - 1
    return [
        pltpu.SemaphoreType.DMA((2, bits * owners)),
        pltpu.SemaphoreType.DMA((2, owners)),
        pltpu.SemaphoreType.DMA,
    ]


class GroupScatter:
    def __init__(self, owners, part, out, refs):
        self.owners, self.part, self.out = owners, part, out
        self.land, (self.sent, self.got) = refs[:-2], refs[-2:]
        self.group = lax.axis_index("group")
        self.bits = list(range(owners.bit_length() - 1))
        self.orders = (self.bits, self.bits[::-1])
        self.rows, self.columns = out.shape[0], out.shape[1] // 2

    def kept(self, half, stage):
        done = self.orders[half][: stage + 1]
        return [r for r in range(self.owners) if not any(r >> bit & 1 for bit in done)]

    def place(self, half, stage, piece):
        if stage == 0:
            start = pl.multiple_of((self.group ^ piece) * self.rows, self.rows)
            return self.part.at[pl.ds(start, self.rows), pl.ds(half * self.columns, self.columns)]
        return self.land[stage - 1].at[half, self.kept(half, stage - 1).index(piece)]

    def hop(self, half, stage, piece):
        bit = self.orders[half][stage]
        at = self.kept(half, stage).index(piece)
        return pltpu.make_async_remote_copy(
            src_ref=self.place(half, stage, piece | 1 << bit),
            dst_ref=self.land[stage].at[half, at],
            send_sem=self.sent.at[half, stage * self.owners + piece],
            recv_sem=self.got.at[half, stage * self.owners + piece],
            device_id={"group": self.group ^ (1 << bit)},
        )

    def begin(self, half, stage):
        for piece in self.kept(half, stage):
            self.hop(half, stage, piece).start()

    def start(self):
        for half in range(2):
            self.begin(half, 0)

    def step(self, stage):
        for half in range(2):
            for piece in self.kept(half, stage):
                self.hop(half, stage, piece).wait_recv()
                mine = self.place(half, stage, piece)
                theirs = self.land[stage].at[half, self.kept(half, stage).index(piece)]
                final = stage + 1 == len(self.bits)
                chunk = min(64, self.rows)

                @pl.loop(0, self.rows // chunk)
                def _(number):
                    rows = pl.ds(pl.multiple_of(number * chunk, chunk), chunk)
                    value = (mine[rows, :].astype(F32) + theirs[rows, :].astype(F32)).astype(BF16)
                    if final:
                        self.out[rows, half * self.columns : (half + 1) * self.columns] = value
                    else:
                        theirs[rows, :] = value

            if stage + 1 < len(self.bits):
                self.begin(half, stage + 1)

    def finish(self):
        for half in range(2):
            for stage in self.bits:
                for piece in self.kept(half, stage):
                    self.hop(half, stage, piece).wait_send()


def group_scatter_scratch(owners, rows, width):
    bits = owners.bit_length() - 1
    return [
        pltpu.VMEM((2, owners >> stage + 1, rows, width // 2), BF16) for stage in range(bits)
    ] + [pltpu.SemaphoreType.DMA((2, bits * owners))] * 2


def comm_kernel(plan, chips, owners, counts, views, *refs):
    refs = list(refs)

    def pop(count):
        taken = refs[:count]
        del refs[:count]
        return taken

    scatter_ins = [pop(count) for count in counts["scatter_ins"]]
    gather_ins = pop(counts["gather"])
    group_gather_ins = [view(ref) for view, ref in zip(views[0], pop(len(views[0])), strict=True)]
    group_scatter_ins = pop(counts["group_scatter"])
    pack_ins = [[view(ref) for view, ref in zip(v, pop(len(v)), strict=True)] for v in views[1]]
    scatter_outs = pop(counts["scatter"])
    gather_outs = pop(counts["gather"])
    group_gather_outs = pop(len(views[0]))
    group_scatter_outs = pop(counts["group_scatter"])
    chained_outs = pop(counts["chained"])
    pack_outs = pop(len(views[1]))
    bits = owners.bit_length() - 1
    transfers = {}
    if scatter_outs:
        rows = scatter_outs[0].shape[0]

        def tile(block):
            values = []
            for left, *weight in scatter_ins:
                value = row_block(left, block, rows)
                values.append(dot_nt(value, weight[0][...]) if weight else value.astype(F32))
            return values[0] if len(values) == 1 else jnp.concatenate(values, axis=1)

        transfers["scatter"] = Scatter(chips, tile, scatter_outs, pop(10))
    transfers["gather"] = [
        Gather(chips, i, o, pop(6)) for i, o in zip(gather_ins, gather_outs, strict=True)
    ]
    transfers["group_gather"] = [
        GroupGather(owners, i, o, pop(3))
        for i, o in zip(group_gather_ins, group_gather_outs, strict=True)
    ]
    transfers["group_scatter"] = [
        GroupScatter(owners, i, o, pop(bits + 2))
        for i, o in zip(group_scatter_ins, group_scatter_outs, strict=True)
    ]
    transfers["chained"] = [
        Gather(chips, group_scatter_outs[i], o, pop(6)) for i, o in enumerate(chained_outs)
    ]
    copies = []
    for sources, target in zip(pack_ins, pack_outs, strict=True):
        sems, at = pop(1)[0], 0
        for number, source in enumerate(sources):
            copies.append(
                pltpu.make_async_copy(
                    source, target.at[:, pl.ds(at, source.shape[1])], sems.at[number]
                )
            )
            at += source.shape[1]
    greet(chips, owners if group_gather_ins or group_scatter_ins else 1)
    for copy in copies:
        copy.start()
    plan(transfers, chips, bits)
    for copy in copies:
        copy.wait()


def comm_call(
    plan,
    number,
    name,
    parts,
    owners,
    micros,
    scatter=(),
    gather=(),
    group_gather=(),
    group_scatter=(),
    chained=0,
    packs=(),
):
    chips = parts // 2
    flat = [array for item in scatter for array in item]
    operands = [*flat, *gather, *(g[0] for g in group_gather), *group_scatter]
    operands += [item[0] for pack in packs for item in pack]
    in_specs = (
        [VMEM] * len(flat)
        + [ANY] * (len(gather) + len(group_gather))
        + [VMEM] * len(group_scatter)
        + [ANY] * sum(len(pack) for pack in packs)
    )
    shapes, out_specs, scratch = [], [], []
    if scatter:
        rows = flat[0].shape[0] // parts
        widths = [item[0].shape[1] if len(item) == 1 else item[1].shape[0] for item in scatter]
        shapes += [jax.ShapeDtypeStruct((rows, width), F32) for width in widths]
        out_specs += [VMEM] * len(widths)
        scratch += scatter_scratch(chips, rows, sum(widths))
    for array in gather:
        shapes.append(jax.ShapeDtypeStruct((parts * array.shape[0], array.shape[1]), array.dtype))
        out_specs.append(ANY)
        scratch += gather_sems(chips, array.shape[0])
    for array, unused, (rows, width) in group_gather:
        shapes.append(jax.ShapeDtypeStruct((owners * rows, width), array.dtype))
        out_specs.append(ANY)
        scratch += group_gather_sems(owners)
    for array in group_scatter:
        rows, width = array.shape[0] // owners, array.shape[1]
        shapes.append(jax.ShapeDtypeStruct((rows, width), BF16))
        out_specs.append(VMEM)
        scratch += group_scatter_scratch(owners, rows, width)
    for array in group_scatter[:chained]:
        rows, width = array.shape[0] // owners, array.shape[1]
        shapes.append(jax.ShapeDtypeStruct((parts * rows, width), BF16))
        out_specs.append(ANY)
        scratch += gather_sems(chips, rows)
    for pack in packs:
        width = sum(item[2][1] for item in pack)
        shapes.append(jax.ShapeDtypeStruct((pack[0][2][0], width), pack[0][0].dtype))
        out_specs.append(ANY)
        scratch.append(pltpu.SemaphoreType.DMA((len(pack),)))
    counts = {
        "scatter_ins": [len(item) for item in scatter],
        "scatter": len(widths) if scatter else 0,
        "gather": len(gather),
        "group_scatter": len(group_scatter),
        "chained": chained,
    }
    views = ([g[1] for g in group_gather], [[item[1] for item in pack] for pack in packs])
    return pl.pallas_call(
        functools.partial(comm_kernel, plan, chips, owners, counts, views),
        out_shape=tuple(shapes),
        in_specs=in_specs,
        out_specs=tuple(out_specs),
        scratch_shapes=scratch,
        compiler_params=comm_params(number),
        cost_estimate=comm_cost(micros),
        name=name,
    )(*operands)


def plan_gather(transfers, chips, bits):
    ends = transfers["group_gather"]
    for one in transfers["gather"] + ends:
        one.start()
    for number in range(1, chips):
        for one in transfers["gather"]:
            one.step(number)
        if number < bits:
            for one in ends:
                one.step(number - 1)
    for number in range(min(bits, chips) - 1, bits):
        for one in ends:
            one.step(number)
    for one in transfers["gather"] + ends:
        one.finish()


def plan_scatter(transfers, chips, bits):
    scatter = transfers["scatter"]
    beside = transfers["group_scatter"] + transfers["group_gather"]
    for one in beside:
        one.start()
    scatter.start()
    scatter.pairs()
    for one in transfers["gather"]:
        one.start()
    for number in range(chips - 1):
        scatter.step(number)
        for one in transfers["gather"]:
            one.step(number + 1)
        if number < bits - 1:
            for one in beside:
                one.step(number)
    scatter.finish()
    for number in range(min(bits, chips) - 1, bits):
        for one in beside:
            one.step(number)
    for one in transfers["gather"] + beside:
        one.finish()


def plan_finish(transfers, chips, bits):
    scatters, chained = transfers["group_scatter"], transfers["chained"]
    for one in transfers["gather"] + scatters:
        one.start()
    for stage in range(bits):
        for one in scatters:
            one.step(stage)
    for one in chained:
        one.start()
    for number in range(1, chips):
        for one in transfers["gather"] + chained:
            one.step(number)
    for one in transfers["gather"] + chained + scatters:
        one.finish()


def plan_group_scatter(transfers, chips, bits):
    scatters, chained = transfers["group_scatter"], transfers["chained"]
    steps = [(one, stage) for one in scatters for stage in range(bits)]
    for one in scatters[:2]:
        one.start()
    waiting = list(scatters[2:])
    hops = []
    for one, stage in steps:
        one.step(stage)
        if stage == 0 and waiting:
            waiting.pop(0).start()
        at = scatters.index(one)
        if hops:
            hops.pop(0)()
        if stage == bits - 1 and at < len(chained):
            chained[at].start()
            hops += [functools.partial(chained[at].step, d) for d in range(1, chips)]
    for hop in hops:
        hop()
    for one in chained + scatters:
        one.finish()


def comm_params(number, limit=48):
    return pltpu.CompilerParams(
        collective_id=number, has_side_effects=True, vmem_limit_bytes=limit * 2**20
    )


def comm_cost(micros):
    return pl.CostEstimate(flops=0, bytes_accessed=int(micros * 3.4e4), transcendentals=0)


ANY = pl.BlockSpec(memory_space=pl.ANY)
VMEM = pl.BlockSpec(memory_space=pltpu.VMEM)


def after(values, *earlier):
    tied = lax.optimization_barrier((values, earlier))[0]
    return tied


class GroupSum:
    def __init__(self, partials, owners, group, flip):
        self.owners, self.group = owners, group
        self.partials = partials if isinstance(partials, list) else [partials]
        self.rows = self.partials[0].shape[0] // owners
        bits = list(range(owners.bit_length() - 1))
        self.order = bits[::-1] if flip else bits
        self.held = {piece: None for piece in range(owners)}

    def piece(self, number):
        if self.held[number] is not None:
            return self.held[number]
        start = (self.group ^ number) * self.rows
        slices = [lax.dynamic_slice_in_dim(p, start, self.rows, 0) for p in self.partials]
        return slices[0] if len(slices) == 1 else jnp.concatenate(slices, axis=1)

    def send(self):
        bit = self.order.pop(0)
        self.keep = [piece for piece in self.held if not piece >> bit & 1]
        self.sent = jnp.stack([self.piece(piece | 1 << bit) for piece in self.keep])
        pairs = [(i, i ^ 1 << bit) for i in range(self.owners)]
        self.got = lax.ppermute(self.sent, "group", pairs)
        return self.sent

    def add(self, *earlier):
        got = after(self.got, *earlier)
        self.held = {
            piece: (self.piece(piece).astype(F32) + got[at].astype(F32)).astype(BF16)
            for at, piece in enumerate(self.keep)
        }


def finish_all(sums):
    for one in sums:
        while one.order:
            one.send()
            one.add()


def send_all(sums):
    return [one.send() for one in sums]


def add_all(sums, *earlier):
    for one in sums:
        one.add(*earlier)


def widen_kernel(counts, *refs):
    sources, targets = refs[: len(counts)], refs[-sum(counts) :]
    at = 0
    for source, count in zip(sources, counts, strict=True):
        for number in range(count):
            targets[at][0, 0] = source[0, number].astype(F32)
            at += 1


def widen(packs, number, experts, previous=()):
    parts, unused, shard, width = packs[0].shape
    counts = [pack.shape[1] for pack in packs]
    total = sum(counts)
    shape = jax.ShapeDtypeStruct((parts, experts, shard, width), F32)
    block = pl.BlockSpec((1, 1, shard // 2, width), lambda c, h: (c, number, h, 0))
    return pl.pallas_call(
        functools.partial(widen_kernel, counts),
        out_shape=(shape,) * total,
        grid=(parts, 2),
        in_specs=[
            pl.BlockSpec((1, count, shard // 2, width), lambda c, h: (c, 0, h, 0))
            for count in counts
        ]
        + [ANY] * len(previous),
        out_specs=(block,) * total,
        input_output_aliases={len(packs) + i: i for i in range(len(previous))},
        cost_estimate=pl.CostEstimate(
            flops=0, bytes_accessed=sum(p.size for p in packs) // 16, transcendentals=0
        ),
        name="widen",
    )(*packs, *previous)


def finish_attention_kernel(
    sharers,
    packed_ref,
    query_ref,
    key_ref,
    value_ref,
    gain_ref,
    q_ref,
    k_ref,
    v_ref,
    o_ref,
    router_ref,
    attention_ref,
    mixture_ref,
    qg_ref,
    kg_ref,
    sums_ref,
):
    width = o_ref.shape[1]
    share = 2 * HD // sharers
    at = pl.program_id(0)
    o_ref[...] = packed_ref[0, :, :width].astype(F32)
    query = packed_ref[0, :, width : 2 * width].astype(F32)
    q_ref[...] = query
    gain = jnp.sum(query * query_ref[...].astype(F32), axis=1, keepdims=True)
    small = packed_ref[0, :, 2 * width + share :].astype(F32)

    @pl.when(at == 0)
    def _():
        sums_ref[...] = jnp.zeros_like(sums_ref)

    lane = lax.broadcasted_iota(jnp.int32, small.shape, 1)
    sums_ref[...] += small + jnp.where(lane == EXPERTS + 3, gain, 0.0)
    for number in range(sharers):

        @pl.when(lax.rem(at, sharers) == number)
        def _():
            piece = packed_ref[0, :, 2 * width : 2 * width + share].astype(F32)
            start = number * share
            if start < HD:
                weight = key_ref[:, start : start + share]
                k_ref[:, start : start + share] = piece
            else:
                weight = value_ref[:, start - HD : start - HD + share]
                v_ref[:, start - HD : start - HD + share] = piece
            more = jnp.sum(piece * weight.astype(F32), axis=1, keepdims=True)
            sums_ref[...] += jnp.where(lane == EXPERTS + 3, more, 0.0)

    @pl.when(at == pl.num_programs(0) - 1)
    def _():
        rows = jnp.transpose(sums_ref[...], (1, 0))
        router_ref[...] = rows[:EXPERTS, :]
        mixture_ref[...] = rows[EXPERTS : EXPERTS + 1, :]
        qg_ref[...] = rows[EXPERTS + 1 : EXPERTS + 2, :]
        kg_ref[...] = rows[EXPERTS + 2 : EXPERTS + 3, :]
        attention_ref[...] = rows[EXPERTS + 3 : EXPERTS + 4, :] / gain_ref[...]


def finish_attention(packed, weights, width, sharers):
    parts, shard, total = packed.shape
    spare = total - 2 * width - 2 * HD // sharers
    head = pl.BlockSpec((shard, HD), lambda c: (0, c // sharers))
    own = pl.BlockSpec((shard, width), lambda c: (0, c))
    whole = lambda c: (0, 0)
    return pl.pallas_call(
        functools.partial(finish_attention_kernel, sharers),
        out_shape=(
            jax.ShapeDtypeStruct((shard, width * parts), F32),
            jax.ShapeDtypeStruct((shard, HK * HD), F32),
            jax.ShapeDtypeStruct((shard, HK * HD), F32),
            jax.ShapeDtypeStruct((shard, width * parts), F32),
            jax.ShapeDtypeStruct((EXPERTS, shard), F32),
        )
        + (jax.ShapeDtypeStruct((1, shard), F32),) * 4,
        grid_spec=pltpu.PrefetchScalarGridSpec(
            num_scalar_prefetch=0,
            grid=(parts,),
            in_specs=[
                pl.BlockSpec((1, shard, total), lambda c: (c, 0, 0)),
                own,
                head,
                head,
                pl.BlockSpec((1, shard), whole),
            ],
            out_specs=(
                own,
                head,
                head,
                own,
                pl.BlockSpec((EXPERTS, shard), whole),
            )
            + (pl.BlockSpec((1, shard), whole),) * 4,
            scratch_shapes=[pltpu.VMEM((shard, spare), F32)],
        ),
        cost_estimate=pl.CostEstimate(flops=0, bytes_accessed=packed.size // 16, transcendentals=0),
        name="finish_attention",
    )(packed, *weights)


def per_device(
    tokens,
    positions,
    expert_ids,
    cotangent,
    attention_gain,
    query_weight,
    key_weight,
    value_weight,
    output_weight,
    query_gain,
    key_gain,
    mixture_gain,
    router_weight,
    gate_weight,
    up_weight,
    down_weight,
):
    parts, owners = lax.axis_size("ctx"), lax.axis_size("group")
    here, group = lax.axis_index("ctx"), lax.axis_index("group")
    rows = tokens.shape[1]
    length = rows * parts
    shard = query_weight.shape[0]
    width = HQ * HD // parts
    experts = EXPERTS // parts
    sharers = parts // HK
    key_head = here // sharers
    share = 2 * HD // sharers
    share_at = (here % sharers) * share

    gather_group = lambda v: lax.all_gather(v, "group", axis=0, tiled=True)

    def columns(array, start, count):
        return lax.dynamic_slice_in_dim(array, start, count, 1)

    spread = lambda vector: jnp.pad(vector, (0, shard - vector.shape[0]))
    gain_rows = jnp.concatenate(
        [
            attention_gain,
            mixture_gain,
            spread(query_gain),
            spread(key_gain),
            jnp.zeros((12 * shard,), BF16),
        ]
    ).reshape(16, shard)
    comm = lambda plan, number, name, micros, **transfers: comm_call(
        plan, number, name, parts, owners, micros, **transfers
    )
    def expert_pack(number, at):
        return jnp.concatenate(
            [
                lax.dynamic_index_in_dim(w, at * experts + number, 0, keepdims=False)
                for w in (up_weight, down_weight)
            ],
            axis=1,
        )

    packs = [expert_pack(number, here) for number in range(experts)]
    gain_rows = after(gain_rows, *packs)

    def cut(start, count):
        return lambda ref: ref.at[:, pl.ds(pl.multiple_of(start(), count), count)]

    place = lambda: lax.axis_index("ctx")
    key_cut = cut(lambda: place() // sharers * HD, HD)
    own_cut = cut(lambda: place() * width, width)

    def gate_item(number):
        return (gate_weight, lambda ref: ref.at[place() * experts + number], (shard, F))


    inputs_all, positions_all, gain_rows, router, wquery, wkey, wvalue, wout = comm(
        plan_gather,
        0,
        "gather_tokens",
        45,
        gather=(tokens[0], jnp.broadcast_to(positions, (8, rows))),
        group_gather=(
            (gain_rows, lambda ref: ref, (16, shard)),
            (router_weight, lambda ref: ref, (shard, EXPERTS)),
            (query_weight, own_cut, (shard, width)),
            (key_weight, key_cut, (shard, HD)),
            (value_weight, key_cut, (shard, HD)),
            (output_weight, own_cut, (shard, width)),
        ),
    )
    packs = [gather_group(after(pack, positions_all)) for pack in packs]
    wqkv = jnp.concatenate([wquery, wkey, wvalue], axis=1)

    gain_rows = gain_rows.reshape(owners, 16, shard).astype(F32)
    attention_gains, mixture_gains = gain_rows[:, 0].reshape(D), gain_rows[:, 1].reshape(D)
    query_gains = gain_rows[:, 2, : HD // owners].reshape(1, HD)
    key_gains = gain_rows[:, 3, : HD // owners].reshape(1, HD)

    positions_all = positions_all.reshape(parts, 8, rows)[:, 0].reshape(length)
    doc_start = (jnp.arange(length, dtype=jnp.int32) - positions_all)[:, None]
    inputs = tokens[0].astype(F32)
    unused, attn_factor = rms_parts(inputs, attention_gains)
    normed_all = rms_parts(inputs_all.astype(F32), attention_gains)[0].astype(BF16)
    qkv_raw = dot(normed_all, wqkv)
    tables = (qkv_raw, doc_start, rope_tables(positions_all), query_gains, key_gains)
    mixed_low = attend(*tables)
    attn_out, upstream_all, first_gate = comm(
        plan_scatter,
        1,
        "scatter_attention",
        50,
        scatter=((mixed_low, wout),),
        gather=(cotangent[0],),
        group_gather=(gate_item(0),),
    )
    hidden = inputs + attn_out
    moe_normed, moe_factor = rms_parts(hidden, mixture_gains)
    moe_low = moe_normed.astype(BF16)
    logits = dot(moe_low, router)
    onehot = (
        expert_ids[0][:, :, None] == jnp.arange(EXPERTS, dtype=jnp.int32)[None, None, :]
    ).astype(F32)
    chosen = jnp.sum(onehot * logits[:, None, :], axis=-1)
    expo = jnp.exp(chosen - jnp.max(chosen, axis=-1, keepdims=True))
    gates = expo / jnp.sum(expo, axis=-1, keepdims=True)
    combine = jnp.sum(gates[:, :, None] * onehot, axis=1)
    moe_all, combine_all, *gates_all = comm(
        plan_gather,
        2,
        "gather_mixture",
        45,
        gather=(moe_low, jnp.pad(combine, ((0, 0), (0, PAD - EXPERTS)))),
        group_gather=[gate_item(number) for number in range(1, experts)],
    )
    gates_all = [first_gate, *gates_all]
    combine_all = columns(combine_all, here * experts, experts)

    def expert_forward(number, weights, gate_all):
        up_all = dot(moe_all, weights[1])
        sigmoid = lax.logistic(gate_all)
        act_low = (gate_all * sigmoid * up_all).astype(BF16)
        weighted = (combine_all[:, number : number + 1] * act_low.astype(F32)).astype(BF16)
        return gate_all, up_all, act_low, weighted

    def expert_back(number, gate_all, up_all, act_low, weights):
        back_all = dot(upstream_all, weights[2])
        sigmoid = lax.logistic(gate_all)
        combine_grad = jnp.sum(act_low.astype(F32) * back_all, axis=-1, keepdims=True)
        act_grad = combine_all[:, number : number + 1] * back_all
        gate_grad = (act_grad * up_all * sigmoid * (1.0 + gate_all * (1.0 - sigmoid))).astype(BF16)
        up_grad = (act_grad * gate_all * sigmoid).astype(BF16)
        return combine_grad, gate_grad, up_grad

    def weight_grad(left, right):
        return dot_tn(left, right).astype(BF16)

    split = lambda number, pack: (gates_all[number], pack[:, :F], pack[:, F:])
    weights = split(0, packs[0])
    gate_all = dot(moe_all, weights[0])
    gate_all, up_all, act_low, weighted = expert_forward(0, weights, gate_all)
    combine_grads, layer_terms, moe_terms, gathered = [], [], [], []
    last_grads = [weight_grad(upstream_all, weighted)]
    for number in range(1, experts):
        half = F // 2
        down_sums = [
            GroupSum(last_grads[0][:, :half], owners, group, False),
            GroupSum(last_grads[0][:, half:], owners, group, True),
        ]
        gate_all, up_all = after((gate_all, up_all), *send_all(down_sums))
        combine_grad, gate_grad, up_grad = expert_back(
            number - 1, gate_all, up_all, act_low, weights
        )
        combine_grads.append(combine_grad)
        layer_terms.append((weighted, weights[2]))
        moe_terms += [(gate_grad, weights[0]), (up_grad, weights[1])]
        grads = weight_grad(moe_all, gate_grad), weight_grad(moe_all, up_grad)
        layer_part = dot_nt(weighted, weights[2])
        add_all(down_sums, layer_part, *grads)
        sent = send_all(down_sums) if down_sums[0].order else []
        other_sums = [
            GroupSum(after(grads[0], *sent), owners, group, False),
            GroupSum(after(grads[1], *sent), owners, group, True),
        ]
        weights = split(number, after(packs[number], *send_all(other_sums)))
        gate_all = dot(moe_all, weights[0])
        add_all(down_sums, gate_all)
        finish_all(down_sums)
        down = jnp.concatenate([one.held[0] for one in down_sums], axis=1)
        weights = (weights[0], after(weights[1], down), weights[2])
        gate_all, up_all, act_low, weighted = expert_forward(number, weights, gate_all)
        last_grads = [weight_grad(upstream_all, weighted)]
        gathered.append([down.reshape(2, shard // 2, F), other_sums])
    combine_grad, gate_grad, up_grad = expert_back(
        experts - 1, gate_all, up_all, act_low, weights
    )
    combine_grads.append(combine_grad)
    layer_terms.append((weighted, weights[2]))
    moe_terms += [(gate_grad, weights[0]), (up_grad, weights[1])]
    for pieces in gathered:
        add_all(pieces[1], gate_grad, up_grad)
        if pieces[1][0].order:
            gate_grad, up_grad = after((gate_grad, up_grad), *send_all(pieces[1]))
    last_grads += [weight_grad(moe_all, gate_grad), weight_grad(moe_all, up_grad)]
    for pieces in gathered:
        add_all(pieces[1], *last_grads)
        finish_all(pieces[1])
        pieces[1] = jnp.stack([one.held[0] for one in pieces[1]])
        last_grads = list(after(last_grads, pieces[1]))
    half = F // 2
    last_sums = [
        GroupSum([last_grads[0][:, :half], last_grads[1]], owners, group, False),
        GroupSum([last_grads[0][:, half:], last_grads[2]], owners, group, True),
    ]
    moe_terms = after(moe_terms, *send_all(last_sums))
    moe_part = sum(dot_nt(left, right) for left, right in moe_terms[:2])
    layer_part = sum(dot_nt(left, right) for left, right in layer_terms)
    for left, right in moe_terms[2:]:
        moe_part = moe_part + dot_nt(left, right)
    moe_part_low = moe_part.astype(BF16)
    add_all(last_sums, moe_part_low)
    if last_sums[0].order:
        moe_part_low = after(moe_part_low, *send_all(last_sums))
    combine_grad = jnp.concatenate(combine_grads, axis=1)
    high = combine_grad.astype(BF16).astype(F32)
    low = combine_grad - high
    at = jnp.arange(PAD, dtype=jnp.int32)[None, :]
    small = sum(
        jnp.where(at == here * experts + number, high[:, number : number + 1], 0.0)
        + jnp.where(at == EXPERTS + here * experts + number, low[:, number : number + 1], 0.0)
        for number in range(experts)
    ).astype(BF16)
    moe_sum, small_sum = comm(
        plan_scatter, 3, "scatter_mixture", 60, scatter=((moe_part_low,), (small,))
    )
    add_all(last_sums, moe_sum)
    finish_all(last_sums)
    ends = [one.held[0] for one in last_sums]
    down = jnp.concatenate([end[:, :half] for end in ends], axis=1)
    gathered.append([jnp.stack([down] + [end[:, half:] for end in ends])])
    unfold = lambda piece: lax.all_gather(piece, "ctx").reshape(parts, -1, shard, F)
    expert_packs = [[unfold(piece) for piece in pieces] for pieces in gathered]

    dcombine = small_sum[:, :EXPERTS] + small_sum[:, EXPERTS : 2 * EXPERTS]
    gates_grad = jnp.sum(onehot * dcombine[:, None, :], axis=-1)
    chosen_grad = gates * (gates_grad - jnp.sum(gates * gates_grad, axis=-1, keepdims=True))
    logit_grad_low = jnp.sum(chosen_grad[:, :, None] * onehot, axis=1).astype(BF16)
    router_partial = dot_tn(moe_low, logit_grad_low)
    moe_grad = moe_sum + dot_nt(logit_grad_low, router)
    hidden_part, mixture_terms = rms_back(hidden, moe_factor, mixture_gains, moe_grad)
    mixture_partial = jnp.sum(mixture_terms, axis=0)
    hidden_grad = cotangent[0].astype(F32) + hidden_part

    (attn_grad_all,) = comm(
        plan_gather,
        4,
        "gather_attention",
        45,
        gather=(
            after(hidden_grad.astype(BF16), *(pack[0] for pack in expert_packs[:-1])),
        ),
    )
    mixed_grad = dot(attn_grad_all, wout).astype(BF16)
    output_partial = weight_grad(attn_grad_all, mixed_low)
    output_sums = [
        GroupSum(output_partial[:, : width // 2], owners, group, False),
        GroupSum(output_partial[:, width // 2 :], owners, group, True),
    ]
    mixed_grad = after(mixed_grad, *send_all(output_sums))
    query_low, kv_part, query_terms, key_terms = attend_back(*tables, mixed_grad)
    step = 1
    while step < sharers:
        kv_part = kv_part + lax.ppermute(kv_part, "ctx", [(i, i ^ step) for i in range(parts)])
        step *= 2
    kv_low = columns(kv_part.astype(BF16), share_at, share)
    qkv_low = jnp.concatenate([query_low, kv_low], axis=1)
    wqkv_share = jnp.concatenate(
        [wqkv[:, :width], columns(wqkv[:, width:], share_at, share)], axis=1
    )
    def head_column(terms):
        spread = terms.reshape(owners, HD // owners)
        return jnp.pad(spread, ((0, 0), (0, shard - HD // owners))).reshape(D, 1)

    add_all(output_sums, qkv_low)
    qkv_tied = qkv_low
    if output_sums[0].order:
        qkv_tied = after(qkv_low, *send_all(output_sums))
    spare = next(n for n in range(EXPERTS + 8, 1024) if (width + share + n) % 256 == 0)
    grad_extras = jnp.concatenate(
        [
            router_partial,
            mixture_partial[:, None],
            head_column(query_terms),
            head_column(key_terms),
        ],
        axis=1,
    )
    grad_extras = jnp.pad(grad_extras, ((0, 0), (width + share, spare - EXPERTS - 3)))
    qkv_wide = jnp.pad(qkv_tied, ((0, 0), (0, spare)))
    qkv_partial = (dot_tn(normed_all, qkv_wide) + grad_extras).astype(BF16)
    layer_sum, qkv_piece = comm(
        plan_scatter,
        6,
        "scatter_grads",
        60,
        scatter=((layer_part.astype(BF16),),),
        group_scatter=(after(qkv_partial, *(pack[-1] for pack in expert_packs[:-1])),),
    )
    layer_out = (hidden + layer_sum).astype(BF16)[None]
    add_all(output_sums, qkv_piece)
    finish_all(output_sums)
    attn_piece = jnp.concatenate([one.held[0] for one in output_sums] + [qkv_piece], axis=1)
    attn_grads = lax.all_gather(attn_piece, "ctx")
    (normed_grad,) = comm(
        plan_scatter,
        5,
        "scatter_normed",
        60,
        scatter=((after(qkv_low, attn_piece), wqkv_share),),
    )
    input_part, unused = rms_back(inputs, attn_factor, attention_gains, normed_grad)
    tokens_grad = (hidden_grad + input_part).astype(BF16)[None]
    query_grad, key_grad, value_grad, output_grad, router_grad, *gain_grads = finish_attention(
        attn_grads,
        (query_weight, key_weight, value_weight, attention_gain.astype(F32).reshape(1, shard)),
        width,
        sharers,
    )
    finished = ()
    for number in range(experts):
        finished = widen(expert_packs[number], number, experts, finished)
    whole = lambda v: v.reshape(EXPERTS, shard, F)
    return (
        layer_out,
        tokens_grad,
        gain_grads[0].reshape(shard),
        query_grad,
        key_grad,
        value_grad,
        output_grad,
        gain_grads[2][0, : HD // owners],
        gain_grads[3][0, : HD // owners],
        gain_grads[1].reshape(shard),
        router_grad.T,
        whole(finished[1]),
        whole(finished[2]),
        whole(finished[0]),
    )


def solution(mesh):
    return jax.shard_map(
        per_device,
        mesh=mesh,
        in_specs=(
            P("group", "ctx", None),
            P("group", "ctx"),
            P("group", "ctx", None),
            P("group", "ctx", None),
            P("group"),
            P("group", None),
            P("group", None),
            P("group", None),
            P("group", None),
            P("group"),
            P("group"),
            P("group"),
            P("group", None),
            P(None, "group", None),
            P(None, "group", None),
            P(None, "group", None),
        ),
        out_specs=(
            P("group", "ctx", None),
            P("group", "ctx", None),
            P("group"),
            P("group", None),
            P("group", None),
            P("group", None),
            P("group", None),
            P("group"),
            P("group"),
            P("group"),
            P("group", None),
            P(None, "group", None),
            P(None, "group", None),
            P(None, "group", None),
        ),
        check_vma=False,
    )
```

```python
import functools

import jax
import jax.numpy as jnp
from jax import lax
from jax.experimental import pallas as pl
from jax.experimental.pallas import tpu as pltpu
from jax.sharding import PartitionSpec as P

D = 2048
HQ = 32
HK = 4
HD = 128
F = 768
TOPK = 8
EXPERTS = 16
PAD = 128
SMALL = 32

EPS = 1e-06
ROPE_BASE = 1000000.0
FLOOR = -1e30
F32 = jnp.float32
BF16 = jnp.bfloat16


def rms_parts(values, gains):
    factor = lax.rsqrt(jnp.mean(values * values, axis=-1, keepdims=True) + EPS)
    return (values * factor * gains, factor)


def rms_back(values, factor, gains, gradient):
    weighted = gradient * gains
    inner = jnp.mean(weighted * values, axis=-1, keepdims=True)
    grad_values = factor * weighted - values * (factor * factor * factor) * inner
    return (grad_values, gradient * values * factor)


def dot(left, right):
    return jnp.dot(left, right, preferred_element_type=F32)


def dot_nt(left, right):
    return lax.dot_general(left, right, (((1,), (1,)), ((), ())), preferred_element_type=F32)


def dot_tn(left, right):
    return lax.dot_general(left, right, (((0,), (0,)), ((), ())), preferred_element_type=F32)


def rope_tables(position_row):
    frequency = ROPE_BASE ** (-2.0 * jnp.arange(HD // 2, dtype=F32) / HD)
    angles = position_row.astype(F32)[:, None] * frequency[None, :]
    cosine, sine = jnp.cos(angles), jnp.sin(angles)
    return jnp.concatenate([cosine, cosine, -sine, sine], axis=-1)


def turn(values):
    return pltpu.roll(values, HD // 2, 1)


def normed_rope(raw, gains, cosine, sine):
    normed, factor = rms_parts(raw, gains)
    return (normed * cosine + turn(normed) * sine, factor)


def softmax_weights(query, key_ref, doc_start, number):
    rows = query.shape[0]
    scale = HD**-0.5 * 1.4426950408889634
    parts = []
    if number:
        columns = number * rows
        key_index = lax.broadcasted_iota(jnp.int32, (rows, columns), 1)
        scores = dot_nt(query, key_ref[:columns, :]) * scale
        parts.append(jnp.where(key_index >= doc_start, scores, FLOOR))
    row_index = lax.broadcasted_iota(jnp.int32, (rows, rows), 0)
    key_index = lax.broadcasted_iota(jnp.int32, (rows, rows), 1)
    allowed = (key_index <= row_index) & (key_index >= doc_start - number * rows)
    scores = dot_nt(query, key_ref[number * rows : (number + 1) * rows, :]) * scale
    parts.append(jnp.where(allowed, scores, FLOOR))
    masked = jnp.concatenate(parts, axis=1) if number else parts[0]
    weights = jnp.exp2(masked - jnp.max(masked, axis=-1, keepdims=True))
    return weights, 1.0 / jnp.sum(weights, axis=-1, keepdims=True)


def attend_kernel(
    block, q_ref, kv_ref, doc_ref, cos_ref, sin_ref, qg_ref, kg_ref, out_ref, key_ref, val_ref
):
    @pl.when(pl.program_id(0) == 0)
    def _():
        key, unused = normed_rope(kv_ref[:, :HD], kg_ref[...], cos_ref[...], sin_ref[...])
        key_ref[...] = key.astype(BF16)
        val_ref[...] = kv_ref[:, HD:].astype(BF16)

    for number in range(kv_ref.shape[0] // block):
        rows = pl.ds(number * block, block)
        query, unused = normed_rope(q_ref[rows, :], qg_ref[...], cos_ref[rows, :], sin_ref[rows, :])
        weights, share = softmax_weights(query.astype(BF16), key_ref, doc_ref[rows, :], number)
        mixed = dot(weights.astype(BF16), val_ref[: (number + 1) * block, :])
        out_ref[rows, :] = (mixed * share).astype(BF16)


def attend_back_kernel(
    block,
    q_ref,
    kv_ref,
    doc_ref,
    cos_ref,
    sin_ref,
    qg_ref,
    kg_ref,
    dm_ref,
    dq_ref,
    dkv_ref,
    qt_ref,
    kt_ref,
    key_ref,
    val_ref,
    dk_ref,
    dv_ref,
):
    head = pl.program_id(0)
    scaling = HD**-0.5

    @pl.when(head == 0)
    def _():
        key, unused = normed_rope(kv_ref[:, :HD], kg_ref[...], cos_ref[...], sin_ref[...])
        key_ref[...] = key.astype(BF16)
        val_ref[...] = kv_ref[:, HD:].astype(BF16)
        dk_ref[...] = jnp.zeros_like(dk_ref)
        dv_ref[...] = jnp.zeros_like(dv_ref)
        qt_ref[...] = jnp.zeros_like(qt_ref)

    for number in range(kv_ref.shape[0] // block):
        rows = pl.ds(number * block, block)
        columns = (number + 1) * block
        cosine, sine = cos_ref[rows, :], sin_ref[rows, :]
        raw = q_ref[rows, :]
        query, factor = normed_rope(raw, qg_ref[...], cosine, sine)
        query = query.astype(BF16)
        key, value = key_ref[:columns, :], val_ref[:columns, :]
        upstream = dm_ref[rows, :]
        weights, share = softmax_weights(query, key_ref, doc_ref[rows, :], number)
        probs = weights * share
        prob_grad = dot_nt(upstream, value)
        delta = jnp.sum(probs * prob_grad, axis=-1, keepdims=True)
        score_grad = (probs * (prob_grad - delta)).astype(BF16)
        dk_ref[:columns, :] += dot_tn(score_grad, query)
        dv_ref[:columns, :] += dot_tn(probs.astype(BF16), upstream)
        rotated = dot(score_grad, key) * scaling
        query_grad = rotated * cosine - turn(rotated) * sine
        raw_grad, terms = rms_back(raw, factor, qg_ref[...], query_grad)
        dq_ref[rows, :] = raw_grad.astype(BF16)
        qt_ref[...] += jnp.sum(terms, axis=0, keepdims=True)

    @pl.when(head == pl.num_programs(0) - 1)
    def _():
        raw = kv_ref[:, :HD]
        cosine, sine = cos_ref[...], sin_ref[...]
        unused, factor = rms_parts(raw, kg_ref[...])
        rotated = dk_ref[...] * scaling
        key_grad = rotated * cosine - turn(rotated) * sine
        raw_grad, terms = rms_back(raw, factor, kg_ref[...], key_grad)
        dkv_ref[:, :HD] = raw_grad
        dkv_ref[:, HD:] = dv_ref[...]
        kt_ref[...] = jnp.sum(terms, axis=0, keepdims=True)


def attention_specs(length, heads):
    whole = lambda h: (0, 0)
    return [
        pl.BlockSpec((length, HD), lambda h: (0, h)),
        pl.BlockSpec((length, 2 * HD), lambda h: (0, heads // 2)),
        pl.BlockSpec((length, 1), whole),
        pl.BlockSpec((length, HD), whole),
        pl.BlockSpec((length, HD), lambda h: (0, 1)),
        pl.BlockSpec((1, HD), whole),
        pl.BlockSpec((1, HD), whole),
    ]


def attend(qkv_raw, doc_start, tables, query_gain, key_gain):
    length, width = qkv_raw.shape[0], qkv_raw.shape[1] - 2 * HD
    return pl.pallas_call(
        functools.partial(attend_kernel, 256),
        out_shape=jax.ShapeDtypeStruct((length, width), BF16),
        grid_spec=pltpu.PrefetchScalarGridSpec(
            num_scalar_prefetch=0,
            grid=(width // HD,),
            in_specs=attention_specs(length, width // HD),
            out_specs=pl.BlockSpec((length, HD), lambda h: (0, h)),
            scratch_shapes=[pltpu.VMEM((length, HD), BF16), pltpu.VMEM((length, HD), BF16)],
        ),
        compiler_params=pltpu.CompilerParams(vmem_limit_bytes=40 * 2**20),
        cost_estimate=pl.CostEstimate(
            flops=length * length, bytes_accessed=length * width, transcendentals=0
        ),
        name="attend",
    )(qkv_raw, qkv_raw, doc_start, tables, tables, query_gain, key_gain)


def attend_back(qkv_raw, doc_start, tables, query_gain, key_gain, upstream):
    length, width = qkv_raw.shape[0], qkv_raw.shape[1] - 2 * HD
    whole = lambda h: (0, 0)
    return pl.pallas_call(
        functools.partial(attend_back_kernel, 256),
        out_shape=(
            jax.ShapeDtypeStruct((length, width), BF16),
            jax.ShapeDtypeStruct((length, 2 * HD), F32),
            jax.ShapeDtypeStruct((1, HD), F32),
            jax.ShapeDtypeStruct((1, HD), F32),
        ),
        grid_spec=pltpu.PrefetchScalarGridSpec(
            num_scalar_prefetch=0,
            grid=(width // HD,),
            in_specs=attention_specs(length, width // HD)
            + [pl.BlockSpec((length, HD), lambda h: (0, h))],
            out_specs=(
                pl.BlockSpec((length, HD), lambda h: (0, h)),
                pl.BlockSpec((length, 2 * HD), whole),
                pl.BlockSpec((1, HD), whole),
                pl.BlockSpec((1, HD), whole),
            ),
            scratch_shapes=[
                pltpu.VMEM((length, HD), BF16),
                pltpu.VMEM((length, HD), BF16),
                pltpu.VMEM((length, HD), F32),
                pltpu.VMEM((length, HD), F32),
            ],
        ),
        compiler_params=pltpu.CompilerParams(vmem_limit_bytes=40 * 2**20),
        cost_estimate=pl.CostEstimate(
            flops=length * length, bytes_accessed=length * width, transcendentals=0
        ),
        name="attend_back",
    )(qkv_raw, qkv_raw, doc_start, tables, tables, query_gain, key_gain, upstream)


def ctx_place():
    here = lax.axis_index("ctx")
    return (here // 2, lax.rem(here, 2))


def peer(chip, core):
    return {"ctx": 2 * chip + core}


def greet(chips, owners=1):
    chip, core = ctx_place()
    group = lax.axis_index("group")
    barrier = pltpu.get_barrier_semaphore()
    pl.semaphore_signal(barrier, inc=1, device_id=peer(chip, 1 - core))

    @pl.when(chip > 0)
    def _():
        pl.semaphore_signal(barrier, inc=1, device_id=peer(chip - 1, core))

    @pl.when(chip < chips - 1)
    def _():
        pl.semaphore_signal(barrier, inc=1, device_id=peer(chip + 1, core))

    bits = owners.bit_length() - 1
    for bit in range(bits):
        pl.semaphore_signal(barrier, inc=1, device_id={"group": group ^ (1 << bit)})
    count = 1 + bits + (chip > 0).astype(jnp.int32) + (chip < chips - 1).astype(jnp.int32)
    pl.semaphore_wait(barrier, count)


class Gather:
    def __init__(self, chips, source, target, sems):
        self.chips, self.source, self.target = chips, source, target
        self.up, self.down, self.side, self.near, self.cross, self.local = sems
        self.chip, self.core = ctx_place()
        self.rows = source.shape[0]
        self.chunks = range(chunk_count(self.rows))
        self.piece = self.rows // len(self.chunks)

    def block(self, chip, core, chunk):
        start = (2 * chip + core) * self.rows + chunk * self.piece
        return self.target.at[pl.ds(pl.multiple_of(start, self.piece), self.piece)]

    def hop(self, origin, chunk, sem, arrive, device, own):
        source = self.block(origin, self.core, chunk)
        if own:
            source = self.source.at[pl.ds(chunk * self.piece, self.piece)]
        return pltpu.make_async_remote_copy(
            src_ref=source,
            dst_ref=self.block(origin, self.core, chunk),
            send_sem=sem.at[origin, chunk],
            recv_sem=arrive.at[origin, chunk],
            device_id=device,
        )

    def to_up(self, origin, chunk, own=False):
        return self.hop(origin, chunk, self.up, self.near, peer(self.chip + 1, self.core), own)

    def to_down(self, origin, chunk, own=False):
        return self.hop(origin, chunk, self.down, self.near, peer(self.chip - 1, self.core), own)

    def to_side(self, origin, chunk, own=False):
        return self.hop(origin, chunk, self.side, self.cross, peer(self.chip, 1 - self.core), own)

    def mine(self):
        start = pl.multiple_of((2 * self.chip + self.core) * self.rows, self.rows)
        return pltpu.make_async_copy(
            self.source, self.target.at[pl.ds(start, self.rows)], self.local
        )

    def start(self):
        for chunk in self.chunks:

            @pl.when(self.chip < self.chips - 1)
            def _():
                self.to_up(self.chip, chunk, True).start()

            @pl.when(self.chip > 0)
            def _():
                self.to_down(self.chip, chunk, True).start()

        for chunk in self.chunks:
            self.to_side(self.chip, chunk, True).start()
        self.mine().start()

    def step(self, distance):
        below, above = self.chip - distance, self.chip + distance
        for chunk in self.chunks:

            @pl.when(below >= 0)
            def _():
                self.to_up(below, chunk).wait_recv()

                @pl.when(self.chip < self.chips - 1)
                def _():
                    self.to_up(below, chunk).start()

                self.to_side(below, chunk).start()

            @pl.when(above < self.chips)
            def _():
                self.to_down(above, chunk).wait_recv()

                @pl.when(self.chip > 0)
                def _():
                    self.to_down(above, chunk).start()

                self.to_side(above, chunk).start()

    def finish(self):
        self.mine().wait()
        for origin in range(self.chips):
            for chunk in self.chunks:
                pltpu.make_async_remote_copy(
                    src_ref=self.source.at[pl.ds(chunk * self.piece, self.piece)],
                    dst_ref=self.block(origin, 1 - self.core, chunk),
                    send_sem=self.side.at[origin, chunk],
                    recv_sem=self.cross.at[origin, chunk],
                    device_id=peer(self.chip, 1 - self.core),
                ).wait_recv()
                self.to_side(origin, chunk).wait_send()

                @pl.when((origin <= self.chip) & (self.chip < self.chips - 1))
                def _():
                    self.to_up(origin, chunk).wait_send()

                @pl.when((origin >= self.chip) & (self.chip > 0))
                def _():
                    self.to_down(origin, chunk).wait_send()


def chunk_count(rows):
    return 4 if rows % 64 == 0 else 1


def gather_sems(chips, rows):
    return [pltpu.SemaphoreType.DMA((chips, chunk_count(rows)))] * 5 + [pltpu.SemaphoreType.DMA]


class Scatter:
    def __init__(self, chips, tile, outs, refs):
        self.chips, self.tile, self.outs = chips, tile, outs
        self.give, self.take, self.send, self.low, self.high, *self.sems = refs
        self.chip, self.core = ctx_place()
        self.rows = outs[0].shape[0]
        self.chunks = range(chunk_count(self.rows))
        self.piece = self.rows // len(self.chunks)

    def part(self, ref, target, chunk):
        return ref.at[target, pl.ds(chunk * self.piece, self.piece)]

    def side(self, target):
        return pltpu.make_async_remote_copy(
            src_ref=self.give.at[target],
            dst_ref=self.take.at[target],
            send_sem=self.sems[0].at[target],
            recv_sem=self.sems[1].at[target],
            device_id=peer(self.chip, 1 - self.core),
        )

    def up(self, target, chunk):
        return pltpu.make_async_remote_copy(
            src_ref=self.part(self.send, target, chunk),
            dst_ref=self.part(self.low, target, chunk),
            send_sem=self.sems[2].at[target, chunk],
            recv_sem=self.sems[3].at[target, chunk],
            device_id=peer(self.chip + 1, self.core),
        )

    def down(self, target, chunk):
        return pltpu.make_async_remote_copy(
            src_ref=self.part(self.send, target, chunk),
            dst_ref=self.part(self.high, target, chunk),
            send_sem=self.sems[2].at[target, chunk],
            recv_sem=self.sems[4].at[target, chunk],
            device_id=peer(self.chip - 1, self.core),
        )

    def order(self):
        last = self.chips - 1
        return sorted(range(self.chips), key=lambda target: min(target, last - target))

    def start(self):
        for target in self.order():
            self.give[target] = self.tile(2 * target + 1 - self.core).astype(BF16)
            self.side(target).start()

    def store(self, value):
        at = 0
        for out in self.outs:
            out[...] = value[:, at : at + out.shape[1]]
            at += out.shape[1]

    def pairs(self):
        last = self.chips - 1
        for target in self.order():
            value = self.tile(2 * target + self.core)
            self.side(target).wait_recv()
            value = value + self.take[target].astype(F32)
            self.send[target] = value.astype(BF16)

            @pl.when(self.chip == target)
            def _():
                self.store(value)

            if target == last:

                @pl.when(self.chip == 0)
                def _():
                    for chunk in self.chunks:
                        self.up(target, chunk).start()

            if target == 0:

                @pl.when(self.chip == last)
                def _():
                    for chunk in self.chunks:
                        self.down(target, chunk).start()

    def add(self, target, chunk, ref):
        mine, theirs = self.part(self.send, target, chunk), self.part(ref, target, chunk)
        mine[...] = (mine[...].astype(F32) + theirs[...].astype(F32)).astype(BF16)

    def upward(self, number):
        target = self.chips - 1 - number

        @pl.when(target > self.chip)
        def _():
            for chunk in self.chunks:

                @pl.when(self.chip > 0)
                def _():
                    self.up(target, chunk).wait_recv()
                    self.add(target, chunk, self.low)

                @pl.when((self.chip > 0) | (number > 0))
                def _():
                    self.up(target, chunk).start()

    def downward(self, number):
        last = self.chips - 1

        @pl.when(number < self.chip)
        def _():
            for chunk in self.chunks:

                @pl.when(self.chip < last)
                def _():
                    self.down(number, chunk).wait_recv()
                    self.add(number, chunk, self.high)

                @pl.when((self.chip < last) | (number > 0))
                def _():
                    self.down(number, chunk).start()

    def step(self, number):
        @pl.when(self.chip < self.chips // 2)
        def _():
            self.upward(number)
            self.downward(number)

        @pl.when(self.chip >= self.chips // 2)
        def _():
            self.downward(number)
            self.upward(number)

    def gain(self, target, chunk, ref):
        theirs = self.part(ref, target, chunk)[...].astype(F32)
        rows, at = pl.ds(chunk * self.piece, self.piece), 0
        for out in self.outs:
            out[rows, :] += theirs[:, at : at + out.shape[1]]
            at += out.shape[1]

    def finish(self):
        for target in range(self.chips):

            @pl.when(self.chip == target)
            def _():
                for chunk in self.chunks:
                    if target > 0:
                        self.up(target, chunk).wait_recv()
                        self.gain(target, chunk, self.low)
                    if target < self.chips - 1:
                        self.down(target, chunk).wait_recv()
                        self.gain(target, chunk, self.high)

        for target in range(self.chips):
            self.side(target).wait_send()

            @pl.when(self.chip != target)
            def _():
                for chunk in self.chunks:
                    self.up(target, chunk).wait_send()


def scatter_scratch(chips, rows, width):
    hops = pltpu.SemaphoreType.DMA((chips, chunk_count(rows)))
    return (
        [pltpu.VMEM((chips, rows, width), BF16)] * 5
        + [pltpu.SemaphoreType.DMA((chips,))] * 2
        + [hops] * 3
    )


def row_block(ref, block, rows):
    return ref[pl.ds(pl.multiple_of(block * rows, rows), rows), :]


class GroupGather:
    def __init__(self, owners, source, target, sems):
        self.owners, self.source, self.target = owners, source, target
        self.sent, self.got, self.local = sems
        self.group = lax.axis_index("group")
        self.rows = source.shape[0]
        self.bits = list(range(owners.bit_length() - 1))
        self.orders = (self.bits, self.bits[::-1])

    def piece(self, mask, half):
        start = (self.group ^ mask) * self.rows + half * (self.rows // 2)
        return self.target.at[pl.ds(pl.multiple_of(start, self.rows // 2), self.rows // 2)]

    def held(self, half, stage):
        masks = [0]
        for bit in self.orders[half][:stage]:
            masks += [mask | 1 << bit for mask in masks]
        return masks

    def hop(self, half, stage, mask):
        bit = self.orders[half][stage]
        source = self.piece(mask, half)
        if mask == 0:
            source = self.source.at[pl.ds(half * (self.rows // 2), self.rows // 2)]
        return pltpu.make_async_remote_copy(
            src_ref=source,
            dst_ref=self.piece(mask, half),
            send_sem=self.sent.at[half, stage * self.owners + mask],
            recv_sem=self.got.at[half, mask | 1 << bit],
            device_id={"group": self.group ^ (1 << bit)},
        )

    def mine(self):
        start = pl.multiple_of(self.group * self.rows, self.rows)
        return pltpu.make_async_copy(
            self.source, self.target.at[pl.ds(start, self.rows)], self.local
        )

    def start(self):
        for half in range(2):
            self.hop(half, 0, 0).start()
        self.mine().start()

    def step(self, stage):
        for half in range(2):
            for mask in self.held(half, stage):
                self.hop(half, stage, mask).wait_recv()
            if stage + 1 < len(self.bits):
                for mask in self.held(half, stage + 1):
                    self.hop(half, stage + 1, mask).start()

    def finish(self):
        self.mine().wait()
        for half in range(2):
            for stage in self.bits:
                for mask in self.held(half, stage):
                    self.hop(half, stage, mask).wait_send()


def group_gather_sems(owners):
    bits = owners.bit_length() - 1
    return [
        pltpu.SemaphoreType.DMA((2, bits * owners)),
        pltpu.SemaphoreType.DMA((2, owners)),
        pltpu.SemaphoreType.DMA,
    ]


class GroupScatter:
    def __init__(self, owners, part, out, refs):
        self.owners, self.part, self.out = owners, part, out
        self.land, (self.sent, self.got) = refs[:-2], refs[-2:]
        self.group = lax.axis_index("group")
        self.bits = list(range(owners.bit_length() - 1))
        self.orders = (self.bits, self.bits[::-1])
        self.rows, self.columns = out.shape[0], out.shape[1] // 2

    def kept(self, half, stage):
        done = self.orders[half][: stage + 1]
        return [r for r in range(self.owners) if not any(r >> bit & 1 for bit in done)]

    def place(self, half, stage, piece):
        if stage == 0:
            start = pl.multiple_of((self.group ^ piece) * self.rows, self.rows)
            return self.part.at[pl.ds(start, self.rows), pl.ds(half * self.columns, self.columns)]
        return self.land[stage - 1].at[half, self.kept(half, stage - 1).index(piece)]

    def hop(self, half, stage, piece):
        bit = self.orders[half][stage]
        at = self.kept(half, stage).index(piece)
        return pltpu.make_async_remote_copy(
            src_ref=self.place(half, stage, piece | 1 << bit),
            dst_ref=self.land[stage].at[half, at],
            send_sem=self.sent.at[half, stage * self.owners + piece],
            recv_sem=self.got.at[half, stage * self.owners + piece],
            device_id={"group": self.group ^ (1 << bit)},
        )

    def begin(self, half, stage):
        for piece in self.kept(half, stage):
            self.hop(half, stage, piece).start()

    def start(self):
        for half in range(2):
            self.begin(half, 0)

    def step(self, stage):
        for half in range(2):
            for piece in self.kept(half, stage):
                self.hop(half, stage, piece).wait_recv()
                mine = self.place(half, stage, piece)
                theirs = self.land[stage].at[half, self.kept(half, stage).index(piece)]
                final = stage + 1 == len(self.bits)
                chunk = min(64, self.rows)

                @pl.loop(0, self.rows // chunk)
                def _(number):
                    rows = pl.ds(pl.multiple_of(number * chunk, chunk), chunk)
                    value = (mine[rows, :].astype(F32) + theirs[rows, :].astype(F32)).astype(BF16)
                    if final:
                        self.out[rows, half * self.columns : (half + 1) * self.columns] = value
                    else:
                        theirs[rows, :] = value

            if stage + 1 < len(self.bits):
                self.begin(half, stage + 1)

    def finish(self):
        for half in range(2):
            for stage in self.bits:
                for piece in self.kept(half, stage):
                    self.hop(half, stage, piece).wait_send()


def group_scatter_scratch(owners, rows, width):
    bits = owners.bit_length() - 1
    return [
        pltpu.VMEM((2, owners >> stage + 1, rows, width // 2), BF16) for stage in range(bits)
    ] + [pltpu.SemaphoreType.DMA((2, bits * owners))] * 2


def comm_kernel(plan, chips, owners, counts, views, *refs):
    refs = list(refs)

    def pop(count):
        taken = refs[:count]
        del refs[:count]
        return taken

    scatter_ins = [pop(count) for count in counts["scatter_ins"]]
    gather_ins = pop(counts["gather"])
    group_gather_ins = [view(ref) for view, ref in zip(views[0], pop(len(views[0])), strict=True)]
    group_scatter_ins = pop(counts["group_scatter"])
    pack_ins = [[view(ref) for view, ref in zip(v, pop(len(v)), strict=True)] for v in views[1]]
    scatter_outs = pop(counts["scatter"])
    gather_outs = pop(counts["gather"])
    group_gather_outs = pop(len(views[0]))
    group_scatter_outs = pop(counts["group_scatter"])
    chained_outs = pop(counts["chained"])
    pack_outs = pop(len(views[1]))
    bits = owners.bit_length() - 1
    transfers = {}
    if scatter_outs:
        rows = scatter_outs[0].shape[0]

        def tile(block):
            values = []
            for left, *weight in scatter_ins:
                value = row_block(left, block, rows)
                values.append(dot_nt(value, weight[0][...]) if weight else value.astype(F32))
            return values[0] if len(values) == 1 else jnp.concatenate(values, axis=1)

        transfers["scatter"] = Scatter(chips, tile, scatter_outs, pop(10))
    transfers["gather"] = [
        Gather(chips, i, o, pop(6)) for i, o in zip(gather_ins, gather_outs, strict=True)
    ]
    transfers["group_gather"] = [
        GroupGather(owners, i, o, pop(3))
        for i, o in zip(group_gather_ins, group_gather_outs, strict=True)
    ]
    transfers["group_scatter"] = [
        GroupScatter(owners, i, o, pop(bits + 2))
        for i, o in zip(group_scatter_ins, group_scatter_outs, strict=True)
    ]
    transfers["chained"] = [
        Gather(chips, group_scatter_outs[i], o, pop(6)) for i, o in enumerate(chained_outs)
    ]
    copies = []
    for sources, target in zip(pack_ins, pack_outs, strict=True):
        sems, at = pop(1)[0], 0
        for number, source in enumerate(sources):
            copies.append(
                pltpu.make_async_copy(
                    source, target.at[:, pl.ds(at, source.shape[1])], sems.at[number]
                )
            )
            at += source.shape[1]
    greet(chips, owners if group_gather_ins or group_scatter_ins else 1)
    for copy in copies:
        copy.start()
    plan(transfers, chips, bits)
    for copy in copies:
        copy.wait()


def comm_call(
    plan,
    number,
    name,
    parts,
    owners,
    micros,
    scatter=(),
    gather=(),
    group_gather=(),
    group_scatter=(),
    chained=0,
    packs=(),
):
    chips = parts // 2
    flat = [array for item in scatter for array in item]
    operands = [*flat, *gather, *(g[0] for g in group_gather), *group_scatter]
    operands += [item[0] for pack in packs for item in pack]
    in_specs = (
        [VMEM] * len(flat)
        + [ANY] * (len(gather) + len(group_gather))
        + [VMEM] * len(group_scatter)
        + [ANY] * sum(len(pack) for pack in packs)
    )
    shapes, out_specs, scratch = [], [], []
    if scatter:
        rows = flat[0].shape[0] // parts
        widths = [item[0].shape[1] if len(item) == 1 else item[1].shape[0] for item in scatter]
        shapes += [jax.ShapeDtypeStruct((rows, width), F32) for width in widths]
        out_specs += [VMEM] * len(widths)
        scratch += scatter_scratch(chips, rows, sum(widths))
    for array in gather:
        shapes.append(jax.ShapeDtypeStruct((parts * array.shape[0], array.shape[1]), array.dtype))
        out_specs.append(ANY)
        scratch += gather_sems(chips, array.shape[0])
    for array, unused, (rows, width) in group_gather:
        shapes.append(jax.ShapeDtypeStruct((owners * rows, width), array.dtype))
        out_specs.append(ANY)
        scratch += group_gather_sems(owners)
    for array in group_scatter:
        rows, width = array.shape[0] // owners, array.shape[1]
        shapes.append(jax.ShapeDtypeStruct((rows, width), BF16))
        out_specs.append(VMEM)
        scratch += group_scatter_scratch(owners, rows, width)
    for array in group_scatter[:chained]:
        rows, width = array.shape[0] // owners, array.shape[1]
        shapes.append(jax.ShapeDtypeStruct((parts * rows, width), BF16))
        out_specs.append(ANY)
        scratch += gather_sems(chips, rows)
    for pack in packs:
        width = sum(item[2][1] for item in pack)
        shapes.append(jax.ShapeDtypeStruct((pack[0][2][0], width), pack[0][0].dtype))
        out_specs.append(ANY)
        scratch.append(pltpu.SemaphoreType.DMA((len(pack),)))
    counts = {
        "scatter_ins": [len(item) for item in scatter],
        "scatter": len(widths) if scatter else 0,
        "gather": len(gather),
        "group_scatter": len(group_scatter),
        "chained": chained,
    }
    views = ([g[1] for g in group_gather], [[item[1] for item in pack] for pack in packs])
    return pl.pallas_call(
        functools.partial(comm_kernel, plan, chips, owners, counts, views),
        out_shape=tuple(shapes),
        in_specs=in_specs,
        out_specs=tuple(out_specs),
        scratch_shapes=scratch,
        compiler_params=comm_params(number),
        cost_estimate=comm_cost(micros),
        name=name,
    )(*operands)


def plan_gather(transfers, chips, bits):
    ends = transfers["group_gather"]
    for one in transfers["gather"] + ends:
        one.start()
    for number in range(1, chips):
        for one in transfers["gather"]:
            one.step(number)
        if number < bits:
            for one in ends:
                one.step(number - 1)
    for number in range(min(bits, chips) - 1, bits):
        for one in ends:
            one.step(number)
    for one in transfers["gather"] + ends:
        one.finish()


def plan_scatter(transfers, chips, bits):
    scatter = transfers["scatter"]
    beside = transfers["group_scatter"] + transfers["group_gather"]
    for one in beside:
        one.start()
    scatter.start()
    scatter.pairs()
    for one in transfers["gather"]:
        one.start()
    for number in range(chips - 1):
        scatter.step(number)
        for one in transfers["gather"]:
            one.step(number + 1)
        if number < bits - 1:
            for one in beside:
                one.step(number)
    scatter.finish()
    for number in range(min(bits, chips) - 1, bits):
        for one in beside:
            one.step(number)
    for one in transfers["gather"] + beside:
        one.finish()


def plan_finish(transfers, chips, bits):
    scatters, chained = transfers["group_scatter"], transfers["chained"]
    for one in transfers["gather"] + scatters:
        one.start()
    for stage in range(bits):
        for one in scatters:
            one.step(stage)
    for one in chained:
        one.start()
    for number in range(1, chips):
        for one in transfers["gather"] + chained:
            one.step(number)
    for one in transfers["gather"] + chained + scatters:
        one.finish()


def plan_group_scatter(transfers, chips, bits):
    scatters, chained = transfers["group_scatter"], transfers["chained"]
    steps = [(one, stage) for one in scatters for stage in range(bits)]
    for one in scatters[:2]:
        one.start()
    waiting = list(scatters[2:])
    hops = []
    for one, stage in steps:
        one.step(stage)
        if stage == 0 and waiting:
            waiting.pop(0).start()
        at = scatters.index(one)
        if hops:
            hops.pop(0)()
        if stage == bits - 1 and at < len(chained):
            chained[at].start()
            hops += [functools.partial(chained[at].step, d) for d in range(1, chips)]
    for hop in hops:
        hop()
    for one in chained + scatters:
        one.finish()


def comm_params(number, limit=48):
    return pltpu.CompilerParams(
        collective_id=number, has_side_effects=True, vmem_limit_bytes=limit * 2**20
    )


def comm_cost(micros):
    return pl.CostEstimate(flops=0, bytes_accessed=int(micros * 3.4e4), transcendentals=0)


ANY = pl.BlockSpec(memory_space=pl.ANY)
VMEM = pl.BlockSpec(memory_space=pltpu.VMEM)


def after(values, *earlier):
    tied = lax.optimization_barrier((values, earlier))[0]
    return tied


class GroupSum:
    def __init__(self, partials, owners, group, flip):
        self.owners, self.group = owners, group
        self.partials = partials if isinstance(partials, list) else [partials]
        self.rows = self.partials[0].shape[0] // owners
        bits = list(range(owners.bit_length() - 1))
        self.order = bits[::-1] if flip else bits
        self.held = {piece: None for piece in range(owners)}

    def piece(self, number):
        if self.held[number] is not None:
            return self.held[number]
        start = (self.group ^ number) * self.rows
        slices = [lax.dynamic_slice_in_dim(p, start, self.rows, 0) for p in self.partials]
        return slices[0] if len(slices) == 1 else jnp.concatenate(slices, axis=1)

    def send(self):
        bit = self.order.pop(0)
        self.keep = [piece for piece in self.held if not piece >> bit & 1]
        self.sent = jnp.stack([self.piece(piece | 1 << bit) for piece in self.keep])
        pairs = [(i, i ^ 1 << bit) for i in range(self.owners)]
        self.got = lax.ppermute(self.sent, "group", pairs)
        return self.sent

    def add(self, *earlier):
        got = after(self.got, *earlier)
        self.held = {
            piece: (self.piece(piece).astype(F32) + got[at].astype(F32)).astype(BF16)
            for at, piece in enumerate(self.keep)
        }


def finish_all(sums):
    for one in sums:
        while one.order:
            one.send()
            one.add()


def send_all(sums):
    return [one.send() for one in sums]


def add_all(sums, *earlier):
    for one in sums:
        one.add(*earlier)


def widen_kernel(counts, *refs):
    sources, targets = refs[: len(counts)], refs[-sum(counts) :]
    at = 0
    for source, count in zip(sources, counts, strict=True):
        for number in range(count):
            targets[at][0, 0] = source[0, number].astype(F32)
            at += 1


def widen(packs, number, experts, previous=()):
    parts, unused, shard, width = packs[0].shape
    counts = [pack.shape[1] for pack in packs]
    total = sum(counts)
    shape = jax.ShapeDtypeStruct((parts, experts, shard, width), F32)
    block = pl.BlockSpec((1, 1, shard // 2, width), lambda c, h: (c, number, h, 0))
    return pl.pallas_call(
        functools.partial(widen_kernel, counts),
        out_shape=(shape,) * total,
        grid=(parts, 2),
        in_specs=[
            pl.BlockSpec((1, count, shard // 2, width), lambda c, h: (c, 0, h, 0))
            for count in counts
        ]
        + [ANY] * len(previous),
        out_specs=(block,) * total,
        input_output_aliases={len(packs) + i: i for i in range(len(previous))},
        cost_estimate=pl.CostEstimate(
            flops=0, bytes_accessed=sum(p.size for p in packs) // 16, transcendentals=0
        ),
        name="widen",
    )(*packs, *previous)


def finish_attention_kernel(
    sharers,
    packed_ref,
    small_ref,
    query_ref,
    key_ref,
    value_ref,
    gain_ref,
    q_ref,
    k_ref,
    v_ref,
    o_ref,
    router_ref,
    attention_ref,
    mixture_ref,
    qg_ref,
    kg_ref,
    rows_ref,
    sums_ref,
):
    shard, width = o_ref.shape
    share = 2 * HD // sharers
    at = pl.program_id(0)
    o_ref[...] = packed_ref[0, :, :width].astype(F32)
    query = packed_ref[0, :, width : 2 * width].astype(F32)
    q_ref[...] = query

    @pl.when(at == 0)
    def _():
        rows_ref[...] = jnp.zeros_like(rows_ref)
        sums_ref[...] = jnp.zeros_like(sums_ref)

    rows_ref[...] += small_ref[0, :, :shard].astype(F32)
    sums_ref[...] += jnp.sum(query * query_ref[...].astype(F32), axis=1, keepdims=True)
    for number in range(sharers):

        @pl.when(lax.rem(at, sharers) == number)
        def _():
            piece = packed_ref[0, :, 2 * width : 2 * width + share].astype(F32)
            start = number * share
            if start < HD:
                weight = key_ref[:, start : start + share]
                k_ref[:, start : start + share] = piece
            else:
                weight = value_ref[:, start - HD : start - HD + share]
                v_ref[:, start - HD : start - HD + share] = piece
            sums_ref[...] += jnp.sum(piece * weight.astype(F32), axis=1, keepdims=True)

    @pl.when(at == pl.num_programs(0) - 1)
    def _():
        router_ref[...] = rows_ref[:EXPERTS, :]
        mixture_ref[...] = rows_ref[EXPERTS : EXPERTS + 1, :]
        qg_ref[...] = rows_ref[EXPERTS + 1 : EXPERTS + 2, :]
        kg_ref[...] = rows_ref[EXPERTS + 2 : EXPERTS + 3, :]
        attention_ref[...] = jnp.transpose(sums_ref[...], (1, 0))[:1, :] / gain_ref[...]


def finish_attention(packed, weights, width, sharers):
    parts, tall, total = packed.shape
    shard = tall - SMALL
    head = pl.BlockSpec((shard, HD), lambda c: (0, c // sharers))
    own = pl.BlockSpec((shard, width), lambda c: (0, c))
    whole = lambda c: (0, 0)
    return pl.pallas_call(
        functools.partial(finish_attention_kernel, sharers),
        out_shape=(
            jax.ShapeDtypeStruct((shard, width * parts), F32),
            jax.ShapeDtypeStruct((shard, HK * HD), F32),
            jax.ShapeDtypeStruct((shard, HK * HD), F32),
            jax.ShapeDtypeStruct((shard, width * parts), F32),
            jax.ShapeDtypeStruct((EXPERTS, shard), F32),
        )
        + (jax.ShapeDtypeStruct((1, shard), F32),) * 4,
        grid_spec=pltpu.PrefetchScalarGridSpec(
            num_scalar_prefetch=0,
            grid=(parts,),
            in_specs=[
                pl.BlockSpec((1, shard, total), lambda c: (c, 0, 0)),
                pl.BlockSpec((1, SMALL, total), lambda c: (c, shard // SMALL, 0)),
                own,
                head,
                head,
                pl.BlockSpec((1, shard), whole),
            ],
            out_specs=(
                own,
                head,
                head,
                own,
                pl.BlockSpec((EXPERTS, shard), whole),
            )
            + (pl.BlockSpec((1, shard), whole),) * 4,
            scratch_shapes=[pltpu.VMEM((SMALL, shard), F32), pltpu.VMEM((shard, PAD), F32)],
        ),
        cost_estimate=pl.CostEstimate(flops=0, bytes_accessed=packed.size // 16, transcendentals=0),
        name="finish_attention",
    )(packed, packed, *weights)


def per_device(
    tokens,
    positions,
    expert_ids,
    cotangent,
    attention_gain,
    query_weight,
    key_weight,
    value_weight,
    output_weight,
    query_gain,
    key_gain,
    mixture_gain,
    router_weight,
    gate_weight,
    up_weight,
    down_weight,
):
    parts, owners = lax.axis_size("ctx"), lax.axis_size("group")
    here, group = lax.axis_index("ctx"), lax.axis_index("group")
    rows = tokens.shape[1]
    length = rows * parts
    shard = query_weight.shape[0]
    width = HQ * HD // parts
    experts = EXPERTS // parts
    sharers = parts // HK
    key_head = here // sharers
    share = 2 * HD // sharers
    share_at = (here % sharers) * share

    gather_group = lambda v: lax.all_gather(v, "group", axis=0, tiled=True)

    def columns(array, start, count):
        return lax.dynamic_slice_in_dim(array, start, count, 1)

    spread = lambda vector: jnp.pad(vector, (0, shard - vector.shape[0]))
    gain_rows = jnp.concatenate(
        [
            attention_gain,
            mixture_gain,
            spread(query_gain),
            spread(key_gain),
            jnp.zeros((12 * shard,), BF16),
        ]
    ).reshape(16, shard)
    comm = lambda plan, number, name, micros, **transfers: comm_call(
        plan, number, name, parts, owners, micros, **transfers
    )
    def expert_pack(number, at):
        return jnp.concatenate(
            [
                lax.dynamic_index_in_dim(w, at * experts + number, 0, keepdims=False)
                for w in (up_weight, down_weight)
            ],
            axis=1,
        )

    packs = [expert_pack(number, here) for number in range(experts)]
    gain_rows = after(gain_rows, *packs)

    def cut(start, count):
        return lambda ref: ref.at[:, pl.ds(pl.multiple_of(start(), count), count)]

    place = lambda: lax.axis_index("ctx")
    key_cut = cut(lambda: place() // sharers * HD, HD)
    own_cut = cut(lambda: place() * width, width)

    def gate_item(number):
        return (gate_weight, lambda ref: ref.at[place() * experts + number], (shard, F))


    inputs_all, positions_all, gain_rows, router, wquery, wkey, wvalue, wout = comm(
        plan_gather,
        0,
        "gather_tokens",
        45,
        gather=(tokens[0], jnp.broadcast_to(positions, (8, rows))),
        group_gather=(
            (gain_rows, lambda ref: ref, (16, shard)),
            (router_weight, lambda ref: ref, (shard, EXPERTS)),
            (query_weight, own_cut, (shard, width)),
            (key_weight, key_cut, (shard, HD)),
            (value_weight, key_cut, (shard, HD)),
            (output_weight, own_cut, (shard, width)),
        ),
    )
    packs = [gather_group(after(pack, positions_all)) for pack in packs]
    wqkv = jnp.concatenate([wquery, wkey, wvalue], axis=1)

    gain_rows = gain_rows.reshape(owners, 16, shard).astype(F32)
    attention_gains, mixture_gains = gain_rows[:, 0].reshape(D), gain_rows[:, 1].reshape(D)
    query_gains = gain_rows[:, 2, : HD // owners].reshape(1, HD)
    key_gains = gain_rows[:, 3, : HD // owners].reshape(1, HD)

    positions_all = positions_all.reshape(parts, 8, rows)[:, 0].reshape(length)
    doc_start = (jnp.arange(length, dtype=jnp.int32) - positions_all)[:, None]
    inputs = tokens[0].astype(F32)
    unused, attn_factor = rms_parts(inputs, attention_gains)
    normed_all = rms_parts(inputs_all.astype(F32), attention_gains)[0].astype(BF16)
    qkv_raw = dot(normed_all, wqkv)
    tables = (qkv_raw, doc_start, rope_tables(positions_all), query_gains, key_gains)
    mixed_low = attend(*tables)
    attn_out, upstream_all, first_gate = comm(
        plan_scatter,
        1,
        "scatter_attention",
        50,
        scatter=((mixed_low, wout),),
        gather=(cotangent[0],),
        group_gather=(gate_item(0),),
    )
    hidden = inputs + attn_out
    moe_normed, moe_factor = rms_parts(hidden, mixture_gains)
    moe_low = moe_normed.astype(BF16)
    logits = dot(moe_low, router)
    onehot = (
        expert_ids[0][:, :, None] == jnp.arange(EXPERTS, dtype=jnp.int32)[None, None, :]
    ).astype(F32)
    chosen = jnp.sum(onehot * logits[:, None, :], axis=-1)
    expo = jnp.exp(chosen - jnp.max(chosen, axis=-1, keepdims=True))
    gates = expo / jnp.sum(expo, axis=-1, keepdims=True)
    combine = jnp.sum(gates[:, :, None] * onehot, axis=1)
    moe_all, combine_all, *gates_all = comm(
        plan_gather,
        2,
        "gather_mixture",
        45,
        gather=(moe_low, jnp.pad(combine, ((0, 0), (0, PAD - EXPERTS)))),
        group_gather=[gate_item(number) for number in range(1, experts)],
    )
    gates_all = [first_gate, *gates_all]
    combine_all = columns(combine_all, here * experts, experts)

    def expert_forward(number, weights, gate_all):
        up_all = dot(moe_all, weights[1])
        sigmoid = lax.logistic(gate_all)
        act_low = (gate_all * sigmoid * up_all).astype(BF16)
        weighted = (combine_all[:, number : number + 1] * act_low.astype(F32)).astype(BF16)
        return gate_all, up_all, act_low, weighted

    def expert_back(number, gate_all, up_all, act_low, weights):
        back_all = dot(upstream_all, weights[2])
        sigmoid = lax.logistic(gate_all)
        combine_grad = jnp.sum(act_low.astype(F32) * back_all, axis=-1, keepdims=True)
        act_grad = combine_all[:, number : number + 1] * back_all
        gate_grad = (act_grad * up_all * sigmoid * (1.0 + gate_all * (1.0 - sigmoid))).astype(BF16)
        up_grad = (act_grad * gate_all * sigmoid).astype(BF16)
        return combine_grad, gate_grad, up_grad

    def weight_grad(left, right):
        return dot_tn(left, right).astype(BF16)

    split = lambda number, pack: (gates_all[number], pack[:, :F], pack[:, F:])
    weights = split(0, packs[0])
    gate_all = dot(moe_all, weights[0])
    gate_all, up_all, act_low, weighted = expert_forward(0, weights, gate_all)
    combine_grads, layer_terms, moe_terms, gathered = [], [], [], []
    last_grads = [weight_grad(upstream_all, weighted)]
    for number in range(1, experts):
        half = F // 2
        down_sums = [
            GroupSum(last_grads[0][:, :half], owners, group, False),
            GroupSum(last_grads[0][:, half:], owners, group, True),
        ]
        gate_all, up_all = after((gate_all, up_all), *send_all(down_sums))
        combine_grad, gate_grad, up_grad = expert_back(
            number - 1, gate_all, up_all, act_low, weights
        )
        combine_grads.append(combine_grad)
        layer_terms.append((weighted, weights[2]))
        moe_terms += [(gate_grad, weights[0]), (up_grad, weights[1])]
        grads = weight_grad(moe_all, gate_grad), weight_grad(moe_all, up_grad)
        layer_part = dot_nt(weighted, weights[2])
        add_all(down_sums, layer_part, *grads)
        sent = send_all(down_sums) if down_sums[0].order else []
        other_sums = [
            GroupSum(after(grads[0], *sent), owners, group, False),
            GroupSum(after(grads[1], *sent), owners, group, True),
        ]
        weights = split(number, after(packs[number], *send_all(other_sums)))
        gate_all = dot(moe_all, weights[0])
        add_all(down_sums, gate_all)
        finish_all(down_sums)
        down = jnp.concatenate([one.held[0] for one in down_sums], axis=1)
        weights = (weights[0], after(weights[1], down), weights[2])
        gate_all, up_all, act_low, weighted = expert_forward(number, weights, gate_all)
        last_grads = [weight_grad(upstream_all, weighted)]
        gathered.append([down.reshape(2, shard // 2, F), other_sums])
    combine_grad, gate_grad, up_grad = expert_back(
        experts - 1, gate_all, up_all, act_low, weights
    )
    combine_grads.append(combine_grad)
    layer_terms.append((weighted, weights[2]))
    moe_terms += [(gate_grad, weights[0]), (up_grad, weights[1])]
    for pieces in gathered:
        add_all(pieces[1], gate_grad, up_grad)
        if pieces[1][0].order:
            gate_grad, up_grad = after((gate_grad, up_grad), *send_all(pieces[1]))
    last_grads += [weight_grad(moe_all, gate_grad), weight_grad(moe_all, up_grad)]
    for pieces in gathered:
        add_all(pieces[1], *last_grads)
        finish_all(pieces[1])
        pieces[1] = jnp.stack([one.held[0] for one in pieces[1]])
        last_grads = list(after(last_grads, pieces[1]))
    half = F // 2
    last_sums = [
        GroupSum([last_grads[0][:, :half], last_grads[1]], owners, group, False),
        GroupSum([last_grads[0][:, half:], last_grads[2]], owners, group, True),
    ]
    moe_terms = after(moe_terms, *send_all(last_sums))
    moe_part = sum(dot_nt(left, right) for left, right in moe_terms[:2])
    layer_part = sum(dot_nt(left, right) for left, right in layer_terms)
    for left, right in moe_terms[2:]:
        moe_part = moe_part + dot_nt(left, right)
    moe_part_low = moe_part.astype(BF16)
    add_all(last_sums, moe_part_low)
    if last_sums[0].order:
        moe_part_low = after(moe_part_low, *send_all(last_sums))
    combine_grad = jnp.concatenate(combine_grads, axis=1)
    high = combine_grad.astype(BF16).astype(F32)
    low = combine_grad - high
    at = jnp.arange(PAD, dtype=jnp.int32)[None, :]
    small = sum(
        jnp.where(at == here * experts + number, high[:, number : number + 1], 0.0)
        + jnp.where(at == EXPERTS + here * experts + number, low[:, number : number + 1], 0.0)
        for number in range(experts)
    ).astype(BF16)
    moe_sum, small_sum = comm(
        plan_scatter, 3, "scatter_mixture", 60, scatter=((moe_part_low,), (small,))
    )
    add_all(last_sums, moe_sum)
    finish_all(last_sums)
    ends = [one.held[0] for one in last_sums]
    down = jnp.concatenate([end[:, :half] for end in ends], axis=1)
    gathered.append([jnp.stack([down] + [end[:, half:] for end in ends])])
    unfold = lambda piece: lax.all_gather(piece, "ctx").reshape(parts, -1, shard, F)
    expert_packs = [[unfold(piece) for piece in pieces] for pieces in gathered]

    dcombine = small_sum[:, :EXPERTS] + small_sum[:, EXPERTS : 2 * EXPERTS]
    gates_grad = jnp.sum(onehot * dcombine[:, None, :], axis=-1)
    chosen_grad = gates * (gates_grad - jnp.sum(gates * gates_grad, axis=-1, keepdims=True))
    logit_grad_low = jnp.sum(chosen_grad[:, :, None] * onehot, axis=1).astype(BF16)
    router_partial = dot_tn(moe_low, logit_grad_low)
    moe_grad = moe_sum + dot_nt(logit_grad_low, router)
    hidden_part, mixture_terms = rms_back(hidden, moe_factor, mixture_gains, moe_grad)
    mixture_partial = jnp.sum(mixture_terms, axis=0)
    hidden_grad = cotangent[0].astype(F32) + hidden_part

    (attn_grad_all,) = comm(
        plan_gather,
        4,
        "gather_attention",
        45,
        gather=(
            after(hidden_grad.astype(BF16), *(pack[0] for pack in expert_packs[:-1])),
        ),
    )
    mixed_grad = dot(attn_grad_all, wout).astype(BF16)
    output_partial = weight_grad(attn_grad_all, mixed_low)
    output_sums = [
        GroupSum(output_partial[:, : width // 2], owners, group, False),
        GroupSum(output_partial[:, width // 2 :], owners, group, True),
    ]
    mixed_grad = after(mixed_grad, *send_all(output_sums))
    query_low, kv_part, query_terms, key_terms = attend_back(*tables, mixed_grad)
    step = 1
    while step < sharers:
        kv_part = kv_part + lax.ppermute(kv_part, "ctx", [(i, i ^ step) for i in range(parts)])
        step *= 2
    kv_low = columns(kv_part.astype(BF16), share_at, share)
    qkv_low = jnp.concatenate([query_low, kv_low], axis=1)
    wqkv_share = jnp.concatenate(
        [wqkv[:, :width], columns(wqkv[:, width:], share_at, share)], axis=1
    )
    def head_column(terms):
        spread = terms.reshape(owners, HD // owners)
        return jnp.pad(spread, ((0, 0), (0, shard - HD // owners))).reshape(D, 1)

    add_all(output_sums, qkv_low)
    qkv_tied = qkv_low
    if output_sums[0].order:
        qkv_tied = after(qkv_low, *send_all(output_sums))
    spare = next(n for n in range(EXPERTS + 8, 1024) if (width + share + n) % 256 == 0)
    grad_extras = jnp.concatenate(
        [
            router_partial,
            mixture_partial[:, None],
            head_column(query_terms),
            head_column(key_terms),
        ],
        axis=1,
    )
    grad_extras = jnp.pad(grad_extras, ((0, 0), (width + share, spare - EXPERTS - 3)))
    qkv_wide = jnp.pad(qkv_tied, ((0, 0), (0, spare)))
    qkv_partial = (dot_tn(normed_all, qkv_wide) + grad_extras).astype(BF16)
    layer_sum, qkv_piece = comm(
        plan_scatter,
        6,
        "scatter_grads",
        60,
        scatter=((layer_part.astype(BF16),),),
        group_scatter=(after(qkv_partial, *(pack[-1] for pack in expert_packs[:-1])),),
    )
    layer_out = (hidden + layer_sum).astype(BF16)[None]
    add_all(output_sums, qkv_piece)
    finish_all(output_sums)
    wide = jnp.concatenate(
        [one.held[0] for one in output_sums] + [qkv_piece[:, : width + share]], axis=1
    )
    low_rows = jnp.pad(
        qkv_piece[:, width + share : width + share + EXPERTS + 3].T,
        ((0, SMALL - EXPERTS - 3), (0, wide.shape[1] - shard)),
    )
    attn_piece = jnp.concatenate([wide, low_rows], axis=0)
    attn_grads = lax.all_gather(attn_piece, "ctx")
    (normed_grad,) = comm(
        plan_scatter,
        5,
        "scatter_normed",
        60,
        scatter=((after(qkv_low, attn_piece), wqkv_share),),
    )
    input_part, unused = rms_back(inputs, attn_factor, attention_gains, normed_grad)
    tokens_grad = (hidden_grad + input_part).astype(BF16)[None]
    query_grad, key_grad, value_grad, output_grad, router_grad, *gain_grads = finish_attention(
        attn_grads,
        (query_weight, key_weight, value_weight, attention_gain.astype(F32).reshape(1, shard)),
        width,
        sharers,
    )
    finished = ()
    for number in range(experts):
        finished = widen(expert_packs[number], number, experts, finished)
    whole = lambda v: v.reshape(EXPERTS, shard, F)
    return (
        layer_out,
        tokens_grad,
        gain_grads[0].reshape(shard),
        query_grad,
        key_grad,
        value_grad,
        output_grad,
        gain_grads[2][0, : HD // owners],
        gain_grads[3][0, : HD // owners],
        gain_grads[1].reshape(shard),
        router_grad.T,
        whole(finished[1]),
        whole(finished[2]),
        whole(finished[0]),
    )


def solution(mesh):
    return jax.shard_map(
        per_device,
        mesh=mesh,
        in_specs=(
            P("group", "ctx", None),
            P("group", "ctx"),
            P("group", "ctx", None),
            P("group", "ctx", None),
            P("group"),
            P("group", None),
            P("group", None),
            P("group", None),
            P("group", None),
            P("group"),
            P("group"),
            P("group"),
            P("group", None),
            P(None, "group", None),
            P(None, "group", None),
            P(None, "group", None),
        ),
        out_specs=(
            P("group", "ctx", None),
            P("group", "ctx", None),
            P("group"),
            P("group", None),
            P("group", None),
            P("group", None),
            P("group", None),
            P("group"),
            P("group"),
            P("group"),
            P("group", None),
            P(None, "group", None),
            P(None, "group", None),
            P(None, "group", None),
        ),
        check_vma=False,
    )
```

```python
import functools

import jax
import jax.numpy as jnp
from jax import lax
from jax.experimental import pallas as pl
from jax.experimental.pallas import tpu as pltpu
from jax.sharding import PartitionSpec as P

D = 2048
HQ = 32
HK = 4
HD = 128
F = 768
TOPK = 8
EXPERTS = 16
PAD = 128
SMALL = 32

EPS = 1e-06
ROPE_BASE = 1000000.0
FLOOR = -1e30
F32 = jnp.float32
BF16 = jnp.bfloat16


def rms_parts(values, gains):
    factor = lax.rsqrt(jnp.mean(values * values, axis=-1, keepdims=True) + EPS)
    return (values * factor * gains, factor)


def rms_back(values, factor, gains, gradient):
    weighted = gradient * gains
    inner = jnp.mean(weighted * values, axis=-1, keepdims=True)
    grad_values = factor * weighted - values * (factor * factor * factor) * inner
    return (grad_values, gradient * values * factor)


def dot(left, right):
    return jnp.dot(left, right, preferred_element_type=F32)


def dot_nt(left, right):
    return lax.dot_general(left, right, (((1,), (1,)), ((), ())), preferred_element_type=F32)


def dot_tn(left, right):
    return lax.dot_general(left, right, (((0,), (0,)), ((), ())), preferred_element_type=F32)


def rope_tables(position_row):
    frequency = ROPE_BASE ** (-2.0 * jnp.arange(HD // 2, dtype=F32) / HD)
    angles = position_row.astype(F32)[:, None] * frequency[None, :]
    cosine, sine = jnp.cos(angles), jnp.sin(angles)
    return jnp.concatenate([cosine, cosine, -sine, sine], axis=-1)


def turn(values):
    return pltpu.roll(values, HD // 2, 1)


def normed_rope(raw, gains, cosine, sine):
    normed, factor = rms_parts(raw, gains)
    return (normed * cosine + turn(normed) * sine, factor)


def softmax_weights(query, key_ref, doc_start, number):
    rows = query.shape[0]
    scale = HD**-0.5 * 1.4426950408889634
    parts = []
    if number:
        columns = number * rows
        key_index = lax.broadcasted_iota(jnp.int32, (rows, columns), 1)
        scores = dot_nt(query, key_ref[:columns, :]) * scale
        parts.append(jnp.where(key_index >= doc_start, scores, FLOOR))
    row_index = lax.broadcasted_iota(jnp.int32, (rows, rows), 0)
    key_index = lax.broadcasted_iota(jnp.int32, (rows, rows), 1)
    allowed = (key_index <= row_index) & (key_index >= doc_start - number * rows)
    scores = dot_nt(query, key_ref[number * rows : (number + 1) * rows, :]) * scale
    parts.append(jnp.where(allowed, scores, FLOOR))
    masked = jnp.concatenate(parts, axis=1) if number else parts[0]
    weights = jnp.exp2(masked - jnp.max(masked, axis=-1, keepdims=True))
    return weights, 1.0 / jnp.sum(weights, axis=-1, keepdims=True)


def attend_kernel(
    block, q_ref, kv_ref, doc_ref, cos_ref, sin_ref, qg_ref, kg_ref, out_ref, key_ref, val_ref
):
    @pl.when(pl.program_id(0) == 0)
    def _():
        key, unused = normed_rope(kv_ref[:, :HD], kg_ref[...], cos_ref[...], sin_ref[...])
        key_ref[...] = key.astype(BF16)
        val_ref[...] = kv_ref[:, HD:].astype(BF16)

    for number in range(kv_ref.shape[0] // block):
        rows = pl.ds(number * block, block)
        query, unused = normed_rope(q_ref[rows, :], qg_ref[...], cos_ref[rows, :], sin_ref[rows, :])
        weights, share = softmax_weights(query.astype(BF16), key_ref, doc_ref[rows, :], number)
        mixed = dot(weights.astype(BF16), val_ref[: (number + 1) * block, :])
        out_ref[rows, :] = (mixed * share).astype(BF16)


def attend_back_kernel(
    block,
    q_ref,
    kv_ref,
    doc_ref,
    cos_ref,
    sin_ref,
    qg_ref,
    kg_ref,
    dm_ref,
    dq_ref,
    dkv_ref,
    qt_ref,
    kt_ref,
    key_ref,
    val_ref,
    dk_ref,
    dv_ref,
):
    head = pl.program_id(0)
    scaling = HD**-0.5

    @pl.when(head == 0)
    def _():
        key, unused = normed_rope(kv_ref[:, :HD], kg_ref[...], cos_ref[...], sin_ref[...])
        key_ref[...] = key.astype(BF16)
        val_ref[...] = kv_ref[:, HD:].astype(BF16)
        dk_ref[...] = jnp.zeros_like(dk_ref)
        dv_ref[...] = jnp.zeros_like(dv_ref)
        qt_ref[...] = jnp.zeros_like(qt_ref)

    for number in range(kv_ref.shape[0] // block):
        rows = pl.ds(number * block, block)
        columns = (number + 1) * block
        cosine, sine = cos_ref[rows, :], sin_ref[rows, :]
        raw = q_ref[rows, :]
        query, factor = normed_rope(raw, qg_ref[...], cosine, sine)
        query = query.astype(BF16)
        key, value = key_ref[:columns, :], val_ref[:columns, :]
        upstream = dm_ref[rows, :]
        weights, share = softmax_weights(query, key_ref, doc_ref[rows, :], number)
        probs = weights * share
        prob_grad = dot_nt(upstream, value)
        delta = jnp.sum(probs * prob_grad, axis=-1, keepdims=True)
        score_grad = (probs * (prob_grad - delta)).astype(BF16)
        dk_ref[:columns, :] += dot_tn(score_grad, query)
        dv_ref[:columns, :] += dot_tn(probs.astype(BF16), upstream)
        rotated = dot(score_grad, key) * scaling
        query_grad = rotated * cosine - turn(rotated) * sine
        raw_grad, terms = rms_back(raw, factor, qg_ref[...], query_grad)
        dq_ref[rows, :] = raw_grad.astype(BF16)
        qt_ref[...] += jnp.sum(terms, axis=0, keepdims=True)

    @pl.when(head == pl.num_programs(0) - 1)
    def _():
        raw = kv_ref[:, :HD]
        cosine, sine = cos_ref[...], sin_ref[...]
        unused, factor = rms_parts(raw, kg_ref[...])
        rotated = dk_ref[...] * scaling
        key_grad = rotated * cosine - turn(rotated) * sine
        raw_grad, terms = rms_back(raw, factor, kg_ref[...], key_grad)
        dkv_ref[:, :HD] = raw_grad
        dkv_ref[:, HD:] = dv_ref[...]
        kt_ref[...] = jnp.sum(terms, axis=0, keepdims=True)


def attention_specs(length, heads):
    whole = lambda h: (0, 0)
    return [
        pl.BlockSpec((length, HD), lambda h: (0, h)),
        pl.BlockSpec((length, 2 * HD), lambda h: (0, heads // 2)),
        pl.BlockSpec((length, 1), whole),
        pl.BlockSpec((length, HD), whole),
        pl.BlockSpec((length, HD), lambda h: (0, 1)),
        pl.BlockSpec((1, HD), whole),
        pl.BlockSpec((1, HD), whole),
    ]


def attend(qkv_raw, doc_start, tables, query_gain, key_gain):
    length, width = qkv_raw.shape[0], qkv_raw.shape[1] - 2 * HD
    return pl.pallas_call(
        functools.partial(attend_kernel, 256),
        out_shape=jax.ShapeDtypeStruct((length, width), BF16),
        grid_spec=pltpu.PrefetchScalarGridSpec(
            num_scalar_prefetch=0,
            grid=(width // HD,),
            in_specs=attention_specs(length, width // HD),
            out_specs=pl.BlockSpec((length, HD), lambda h: (0, h)),
            scratch_shapes=[pltpu.VMEM((length, HD), BF16), pltpu.VMEM((length, HD), BF16)],
        ),
        compiler_params=pltpu.CompilerParams(vmem_limit_bytes=40 * 2**20),
        cost_estimate=pl.CostEstimate(
            flops=length * length, bytes_accessed=length * width, transcendentals=0
        ),
        name="attend",
    )(qkv_raw, qkv_raw, doc_start, tables, tables, query_gain, key_gain)


def attend_back(qkv_raw, doc_start, tables, query_gain, key_gain, upstream):
    length, width = qkv_raw.shape[0], qkv_raw.shape[1] - 2 * HD
    whole = lambda h: (0, 0)
    return pl.pallas_call(
        functools.partial(attend_back_kernel, 256),
        out_shape=(
            jax.ShapeDtypeStruct((length, width), BF16),
            jax.ShapeDtypeStruct((length, 2 * HD), F32),
            jax.ShapeDtypeStruct((1, HD), F32),
            jax.ShapeDtypeStruct((1, HD), F32),
        ),
        grid_spec=pltpu.PrefetchScalarGridSpec(
            num_scalar_prefetch=0,
            grid=(width // HD,),
            in_specs=attention_specs(length, width // HD)
            + [pl.BlockSpec((length, HD), lambda h: (0, h))],
            out_specs=(
                pl.BlockSpec((length, HD), lambda h: (0, h)),
                pl.BlockSpec((length, 2 * HD), whole),
                pl.BlockSpec((1, HD), whole),
                pl.BlockSpec((1, HD), whole),
            ),
            scratch_shapes=[
                pltpu.VMEM((length, HD), BF16),
                pltpu.VMEM((length, HD), BF16),
                pltpu.VMEM((length, HD), F32),
                pltpu.VMEM((length, HD), F32),
            ],
        ),
        compiler_params=pltpu.CompilerParams(vmem_limit_bytes=40 * 2**20),
        cost_estimate=pl.CostEstimate(
            flops=length * length, bytes_accessed=length * width, transcendentals=0
        ),
        name="attend_back",
    )(qkv_raw, qkv_raw, doc_start, tables, tables, query_gain, key_gain, upstream)


def ctx_place():
    here = lax.axis_index("ctx")
    return (here // 2, lax.rem(here, 2))


def peer(chip, core):
    return {"ctx": 2 * chip + core}


def greet(chips, owners=1):
    chip, core = ctx_place()
    group = lax.axis_index("group")
    barrier = pltpu.get_barrier_semaphore()
    pl.semaphore_signal(barrier, inc=1, device_id=peer(chip, 1 - core))

    @pl.when(chip > 0)
    def _():
        pl.semaphore_signal(barrier, inc=1, device_id=peer(chip - 1, core))

    @pl.when(chip < chips - 1)
    def _():
        pl.semaphore_signal(barrier, inc=1, device_id=peer(chip + 1, core))

    bits = owners.bit_length() - 1
    for bit in range(bits):
        pl.semaphore_signal(barrier, inc=1, device_id={"group": group ^ (1 << bit)})
    count = 1 + bits + (chip > 0).astype(jnp.int32) + (chip < chips - 1).astype(jnp.int32)
    pl.semaphore_wait(barrier, count)


class Gather:
    def __init__(self, chips, source, target, sems):
        self.chips, self.source, self.target = chips, source, target
        self.up, self.down, self.side, self.near, self.cross, self.local = sems
        self.chip, self.core = ctx_place()
        self.rows = source.shape[0]
        self.chunks = range(chunk_count(self.rows))
        self.piece = self.rows // len(self.chunks)

    def block(self, chip, core, chunk):
        start = (2 * chip + core) * self.rows + chunk * self.piece
        return self.target.at[pl.ds(pl.multiple_of(start, self.piece), self.piece)]

    def hop(self, origin, chunk, sem, arrive, device, own):
        source = self.block(origin, self.core, chunk)
        if own:
            source = self.source.at[pl.ds(chunk * self.piece, self.piece)]
        return pltpu.make_async_remote_copy(
            src_ref=source,
            dst_ref=self.block(origin, self.core, chunk),
            send_sem=sem.at[origin, chunk],
            recv_sem=arrive.at[origin, chunk],
            device_id=device,
        )

    def to_up(self, origin, chunk, own=False):
        return self.hop(origin, chunk, self.up, self.near, peer(self.chip + 1, self.core), own)

    def to_down(self, origin, chunk, own=False):
        return self.hop(origin, chunk, self.down, self.near, peer(self.chip - 1, self.core), own)

    def to_side(self, origin, chunk, own=False):
        return self.hop(origin, chunk, self.side, self.cross, peer(self.chip, 1 - self.core), own)

    def mine(self):
        start = pl.multiple_of((2 * self.chip + self.core) * self.rows, self.rows)
        return pltpu.make_async_copy(
            self.source, self.target.at[pl.ds(start, self.rows)], self.local
        )

    def start(self):
        for chunk in self.chunks:

            @pl.when(self.chip < self.chips - 1)
            def _():
                self.to_up(self.chip, chunk, True).start()

            @pl.when(self.chip > 0)
            def _():
                self.to_down(self.chip, chunk, True).start()

        for chunk in self.chunks:
            self.to_side(self.chip, chunk, True).start()
        self.mine().start()

    def step(self, distance):
        below, above = self.chip - distance, self.chip + distance
        for chunk in self.chunks:

            @pl.when(below >= 0)
            def _():
                self.to_up(below, chunk).wait_recv()

                @pl.when(self.chip < self.chips - 1)
                def _():
                    self.to_up(below, chunk).start()

                self.to_side(below, chunk).start()

            @pl.when(above < self.chips)
            def _():
                self.to_down(above, chunk).wait_recv()

                @pl.when(self.chip > 0)
                def _():
                    self.to_down(above, chunk).start()

                self.to_side(above, chunk).start()

    def finish(self):
        self.mine().wait()
        for origin in range(self.chips):
            for chunk in self.chunks:
                pltpu.make_async_remote_copy(
                    src_ref=self.source.at[pl.ds(chunk * self.piece, self.piece)],
                    dst_ref=self.block(origin, 1 - self.core, chunk),
                    send_sem=self.side.at[origin, chunk],
                    recv_sem=self.cross.at[origin, chunk],
                    device_id=peer(self.chip, 1 - self.core),
                ).wait_recv()
                self.to_side(origin, chunk).wait_send()

                @pl.when((origin <= self.chip) & (self.chip < self.chips - 1))
                def _():
                    self.to_up(origin, chunk).wait_send()

                @pl.when((origin >= self.chip) & (self.chip > 0))
                def _():
                    self.to_down(origin, chunk).wait_send()


def chunk_count(rows):
    return 4 if rows % 64 == 0 else 1


def gather_sems(chips, rows):
    return [pltpu.SemaphoreType.DMA((chips, chunk_count(rows)))] * 5 + [pltpu.SemaphoreType.DMA]


class Scatter:
    def __init__(self, chips, tile, outs, refs):
        self.chips, self.tile, self.outs = chips, tile, outs
        self.give, self.take, self.send, self.low, self.high, *self.sems = refs
        self.chip, self.core = ctx_place()
        self.rows = outs[0].shape[0]
        self.chunks = range(chunk_count(self.rows))
        self.piece = self.rows // len(self.chunks)

    def part(self, ref, target, chunk):
        return ref.at[target, pl.ds(chunk * self.piece, self.piece)]

    def side(self, target):
        return pltpu.make_async_remote_copy(
            src_ref=self.give.at[target],
            dst_ref=self.take.at[target],
            send_sem=self.sems[0].at[target],
            recv_sem=self.sems[1].at[target],
            device_id=peer(self.chip, 1 - self.core),
        )

    def up(self, target, chunk):
        return pltpu.make_async_remote_copy(
            src_ref=self.part(self.send, target, chunk),
            dst_ref=self.part(self.low, target, chunk),
            send_sem=self.sems[2].at[target, chunk],
            recv_sem=self.sems[3].at[target, chunk],
            device_id=peer(self.chip + 1, self.core),
        )

    def down(self, target, chunk):
        return pltpu.make_async_remote_copy(
            src_ref=self.part(self.send, target, chunk),
            dst_ref=self.part(self.high, target, chunk),
            send_sem=self.sems[2].at[target, chunk],
            recv_sem=self.sems[4].at[target, chunk],
            device_id=peer(self.chip - 1, self.core),
        )

    def order(self):
        last = self.chips - 1
        return sorted(range(self.chips), key=lambda target: min(target, last - target))

    def start(self):
        for target in self.order():
            self.give[target] = self.tile(2 * target + 1 - self.core).astype(BF16)
            self.side(target).start()

    def store(self, value):
        at = 0
        for out in self.outs:
            out[...] = value[:, at : at + out.shape[1]]
            at += out.shape[1]

    def pairs(self):
        last = self.chips - 1
        for target in self.order():
            value = self.tile(2 * target + self.core)
            self.side(target).wait_recv()
            value = value + self.take[target].astype(F32)
            self.send[target] = value.astype(BF16)

            @pl.when(self.chip == target)
            def _():
                self.store(value)

            if target == last:

                @pl.when(self.chip == 0)
                def _():
                    for chunk in self.chunks:
                        self.up(target, chunk).start()

            if target == 0:

                @pl.when(self.chip == last)
                def _():
                    for chunk in self.chunks:
                        self.down(target, chunk).start()

    def add(self, target, chunk, ref):
        mine, theirs = self.part(self.send, target, chunk), self.part(ref, target, chunk)
        mine[...] = (mine[...].astype(F32) + theirs[...].astype(F32)).astype(BF16)

    def upward(self, number):
        target = self.chips - 1 - number

        @pl.when(target > self.chip)
        def _():
            for chunk in self.chunks:

                @pl.when(self.chip > 0)
                def _():
                    self.up(target, chunk).wait_recv()
                    self.add(target, chunk, self.low)

                @pl.when((self.chip > 0) | (number > 0))
                def _():
                    self.up(target, chunk).start()

    def downward(self, number):
        last = self.chips - 1

        @pl.when(number < self.chip)
        def _():
            for chunk in self.chunks:

                @pl.when(self.chip < last)
                def _():
                    self.down(number, chunk).wait_recv()
                    self.add(number, chunk, self.high)

                @pl.when((self.chip < last) | (number > 0))
                def _():
                    self.down(number, chunk).start()

    def step(self, number):
        @pl.when(self.chip < self.chips // 2)
        def _():
            self.upward(number)
            self.downward(number)

        @pl.when(self.chip >= self.chips // 2)
        def _():
            self.downward(number)
            self.upward(number)

    def gain(self, target, chunk, ref):
        theirs = self.part(ref, target, chunk)[...].astype(F32)
        rows, at = pl.ds(chunk * self.piece, self.piece), 0
        for out in self.outs:
            out[rows, :] += theirs[:, at : at + out.shape[1]]
            at += out.shape[1]

    def finish(self):
        for target in range(self.chips):

            @pl.when(self.chip == target)
            def _():
                for chunk in self.chunks:
                    if target > 0:
                        self.up(target, chunk).wait_recv()
                        self.gain(target, chunk, self.low)
                    if target < self.chips - 1:
                        self.down(target, chunk).wait_recv()
                        self.gain(target, chunk, self.high)

        for target in range(self.chips):
            self.side(target).wait_send()

            @pl.when(self.chip != target)
            def _():
                for chunk in self.chunks:
                    self.up(target, chunk).wait_send()


def scatter_scratch(chips, rows, width):
    hops = pltpu.SemaphoreType.DMA((chips, chunk_count(rows)))
    return (
        [pltpu.VMEM((chips, rows, width), BF16)] * 5
        + [pltpu.SemaphoreType.DMA((chips,))] * 2
        + [hops] * 3
    )


def row_block(ref, block, rows):
    return ref[pl.ds(pl.multiple_of(block * rows, rows), rows), :]


class GroupGather:
    def __init__(self, owners, source, target, sems):
        self.owners, self.source, self.target = owners, source, target
        self.sent, self.got, self.local = sems
        self.group = lax.axis_index("group")
        self.rows = source.shape[0]
        self.bits = list(range(owners.bit_length() - 1))
        self.orders = (self.bits, self.bits[::-1])

    def piece(self, mask, half):
        start = (self.group ^ mask) * self.rows + half * (self.rows // 2)
        return self.target.at[pl.ds(pl.multiple_of(start, self.rows // 2), self.rows // 2)]

    def held(self, half, stage):
        masks = [0]
        for bit in self.orders[half][:stage]:
            masks += [mask | 1 << bit for mask in masks]
        return masks

    def hop(self, half, stage, mask):
        bit = self.orders[half][stage]
        source = self.piece(mask, half)
        if mask == 0:
            source = self.source.at[pl.ds(half * (self.rows // 2), self.rows // 2)]
        return pltpu.make_async_remote_copy(
            src_ref=source,
            dst_ref=self.piece(mask, half),
            send_sem=self.sent.at[half, stage * self.owners + mask],
            recv_sem=self.got.at[half, mask | 1 << bit],
            device_id={"group": self.group ^ (1 << bit)},
        )

    def mine(self):
        start = pl.multiple_of(self.group * self.rows, self.rows)
        return pltpu.make_async_copy(
            self.source, self.target.at[pl.ds(start, self.rows)], self.local
        )

    def start(self):
        for half in range(2):
            self.hop(half, 0, 0).start()
        self.mine().start()

    def step(self, stage):
        for half in range(2):
            for mask in self.held(half, stage):
                self.hop(half, stage, mask).wait_recv()
            if stage + 1 < len(self.bits):
                for mask in self.held(half, stage + 1):
                    self.hop(half, stage + 1, mask).start()

    def finish(self):
        self.mine().wait()
        for half in range(2):
            for stage in self.bits:
                for mask in self.held(half, stage):
                    self.hop(half, stage, mask).wait_send()


def group_gather_sems(owners):
    bits = owners.bit_length() - 1
    return [
        pltpu.SemaphoreType.DMA((2, bits * owners)),
        pltpu.SemaphoreType.DMA((2, owners)),
        pltpu.SemaphoreType.DMA,
    ]


class GroupScatter:
    def __init__(self, owners, part, out, refs):
        self.owners, self.part, self.out = owners, part, out
        self.land, (self.sent, self.got) = refs[:-2], refs[-2:]
        self.group = lax.axis_index("group")
        self.bits = list(range(owners.bit_length() - 1))
        self.orders = (self.bits, self.bits[::-1])
        self.rows, self.columns = out.shape[0], out.shape[1] // 2

    def kept(self, half, stage):
        done = self.orders[half][: stage + 1]
        return [r for r in range(self.owners) if not any(r >> bit & 1 for bit in done)]

    def place(self, half, stage, piece):
        if stage == 0:
            start = pl.multiple_of((self.group ^ piece) * self.rows, self.rows)
            return self.part.at[pl.ds(start, self.rows), pl.ds(half * self.columns, self.columns)]
        return self.land[stage - 1].at[half, self.kept(half, stage - 1).index(piece)]

    def hop(self, half, stage, piece):
        bit = self.orders[half][stage]
        at = self.kept(half, stage).index(piece)
        return pltpu.make_async_remote_copy(
            src_ref=self.place(half, stage, piece | 1 << bit),
            dst_ref=self.land[stage].at[half, at],
            send_sem=self.sent.at[half, stage * self.owners + piece],
            recv_sem=self.got.at[half, stage * self.owners + piece],
            device_id={"group": self.group ^ (1 << bit)},
        )

    def begin(self, half, stage):
        for piece in self.kept(half, stage):
            self.hop(half, stage, piece).start()

    def start(self):
        for half in range(2):
            self.begin(half, 0)

    def step(self, stage):
        for half in range(2):
            for piece in self.kept(half, stage):
                self.hop(half, stage, piece).wait_recv()
                mine = self.place(half, stage, piece)
                theirs = self.land[stage].at[half, self.kept(half, stage).index(piece)]
                final = stage + 1 == len(self.bits)
                chunk = min(64, self.rows)

                @pl.loop(0, self.rows // chunk)
                def _(number):
                    rows = pl.ds(pl.multiple_of(number * chunk, chunk), chunk)
                    value = (mine[rows, :].astype(F32) + theirs[rows, :].astype(F32)).astype(BF16)
                    if final:
                        self.out[rows, half * self.columns : (half + 1) * self.columns] = value
                    else:
                        theirs[rows, :] = value

            if stage + 1 < len(self.bits):
                self.begin(half, stage + 1)

    def finish(self):
        for half in range(2):
            for stage in self.bits:
                for piece in self.kept(half, stage):
                    self.hop(half, stage, piece).wait_send()


def group_scatter_scratch(owners, rows, width):
    bits = owners.bit_length() - 1
    return [
        pltpu.VMEM((2, owners >> stage + 1, rows, width // 2), BF16) for stage in range(bits)
    ] + [pltpu.SemaphoreType.DMA((2, bits * owners))] * 2


def comm_kernel(plan, chips, owners, counts, views, *refs):
    refs = list(refs)

    def pop(count):
        taken = refs[:count]
        del refs[:count]
        return taken

    scatter_ins = [pop(count) for count in counts["scatter_ins"]]
    gather_ins = pop(counts["gather"])
    group_gather_ins = [view(ref) for view, ref in zip(views[0], pop(len(views[0])), strict=True)]
    group_scatter_ins = pop(counts["group_scatter"])
    pack_ins = [[view(ref) for view, ref in zip(v, pop(len(v)), strict=True)] for v in views[1]]
    scatter_outs = pop(counts["scatter"])
    gather_outs = pop(counts["gather"])
    group_gather_outs = pop(len(views[0]))
    group_scatter_outs = pop(counts["group_scatter"])
    chained_outs = pop(counts["chained"])
    pack_outs = pop(len(views[1]))
    bits = owners.bit_length() - 1
    transfers = {}
    if scatter_outs:
        rows = scatter_outs[0].shape[0]

        def tile(block):
            values = []
            for left, *weight in scatter_ins:
                value = row_block(left, block, rows)
                values.append(dot_nt(value, weight[0][...]) if weight else value.astype(F32))
            return values[0] if len(values) == 1 else jnp.concatenate(values, axis=1)

        transfers["scatter"] = Scatter(chips, tile, scatter_outs, pop(10))
    transfers["gather"] = [
        Gather(chips, i, o, pop(6)) for i, o in zip(gather_ins, gather_outs, strict=True)
    ]
    transfers["group_gather"] = [
        GroupGather(owners, i, o, pop(3))
        for i, o in zip(group_gather_ins, group_gather_outs, strict=True)
    ]
    transfers["group_scatter"] = [
        GroupScatter(owners, i, o, pop(bits + 2))
        for i, o in zip(group_scatter_ins, group_scatter_outs, strict=True)
    ]
    transfers["chained"] = [
        Gather(chips, group_scatter_outs[i], o, pop(6)) for i, o in enumerate(chained_outs)
    ]
    copies = []
    for sources, target in zip(pack_ins, pack_outs, strict=True):
        sems, at = pop(1)[0], 0
        for number, source in enumerate(sources):
            copies.append(
                pltpu.make_async_copy(
                    source, target.at[:, pl.ds(at, source.shape[1])], sems.at[number]
                )
            )
            at += source.shape[1]
    greet(chips, owners if group_gather_ins or group_scatter_ins else 1)
    for copy in copies:
        copy.start()
    plan(transfers, chips, bits)
    for copy in copies:
        copy.wait()


def comm_call(
    plan,
    number,
    name,
    parts,
    owners,
    micros,
    scatter=(),
    gather=(),
    group_gather=(),
    group_scatter=(),
    chained=0,
    packs=(),
):
    chips = parts // 2
    flat = [array for item in scatter for array in item]
    operands = [*flat, *gather, *(g[0] for g in group_gather), *group_scatter]
    operands += [item[0] for pack in packs for item in pack]
    in_specs = (
        [VMEM] * len(flat)
        + [ANY] * (len(gather) + len(group_gather))
        + [VMEM] * len(group_scatter)
        + [ANY] * sum(len(pack) for pack in packs)
    )
    shapes, out_specs, scratch = [], [], []
    if scatter:
        rows = flat[0].shape[0] // parts
        widths = [item[0].shape[1] if len(item) == 1 else item[1].shape[0] for item in scatter]
        shapes += [jax.ShapeDtypeStruct((rows, width), F32) for width in widths]
        out_specs += [VMEM] * len(widths)
        scratch += scatter_scratch(chips, rows, sum(widths))
    for array in gather:
        shapes.append(jax.ShapeDtypeStruct((parts * array.shape[0], array.shape[1]), array.dtype))
        out_specs.append(ANY)
        scratch += gather_sems(chips, array.shape[0])
    for array, unused, (rows, width) in group_gather:
        shapes.append(jax.ShapeDtypeStruct((owners * rows, width), array.dtype))
        out_specs.append(ANY)
        scratch += group_gather_sems(owners)
    for array in group_scatter:
        rows, width = array.shape[0] // owners, array.shape[1]
        shapes.append(jax.ShapeDtypeStruct((rows, width), BF16))
        out_specs.append(VMEM)
        scratch += group_scatter_scratch(owners, rows, width)
    for array in group_scatter[:chained]:
        rows, width = array.shape[0] // owners, array.shape[1]
        shapes.append(jax.ShapeDtypeStruct((parts * rows, width), BF16))
        out_specs.append(ANY)
        scratch += gather_sems(chips, rows)
    for pack in packs:
        width = sum(item[2][1] for item in pack)
        shapes.append(jax.ShapeDtypeStruct((pack[0][2][0], width), pack[0][0].dtype))
        out_specs.append(ANY)
        scratch.append(pltpu.SemaphoreType.DMA((len(pack),)))
    counts = {
        "scatter_ins": [len(item) for item in scatter],
        "scatter": len(widths) if scatter else 0,
        "gather": len(gather),
        "group_scatter": len(group_scatter),
        "chained": chained,
    }
    views = ([g[1] for g in group_gather], [[item[1] for item in pack] for pack in packs])
    return pl.pallas_call(
        functools.partial(comm_kernel, plan, chips, owners, counts, views),
        out_shape=tuple(shapes),
        in_specs=in_specs,
        out_specs=tuple(out_specs),
        scratch_shapes=scratch,
        compiler_params=comm_params(number),
        cost_estimate=comm_cost(micros),
        name=name,
    )(*operands)


def plan_gather(transfers, chips, bits):
    ends = transfers["group_gather"]
    for one in transfers["gather"] + ends:
        one.start()
    for number in range(1, chips):
        for one in transfers["gather"]:
            one.step(number)
        if number < bits:
            for one in ends:
                one.step(number - 1)
    for number in range(min(bits, chips) - 1, bits):
        for one in ends:
            one.step(number)
    for one in transfers["gather"] + ends:
        one.finish()


def plan_scatter(transfers, chips, bits):
    scatter = transfers["scatter"]
    beside = transfers["group_scatter"] + transfers["group_gather"]
    for one in beside:
        one.start()
    scatter.start()
    scatter.pairs()
    for one in transfers["gather"]:
        one.start()
    for number in range(chips - 1):
        scatter.step(number)
        for one in transfers["gather"]:
            one.step(number + 1)
        if number < bits - 1:
            for one in beside:
                one.step(number)
    scatter.finish()
    for number in range(min(bits, chips) - 1, bits):
        for one in beside:
            one.step(number)
    for one in transfers["gather"] + beside:
        one.finish()


def plan_finish(transfers, chips, bits):
    scatters, chained = transfers["group_scatter"], transfers["chained"]
    for one in transfers["gather"] + scatters:
        one.start()
    for stage in range(bits):
        for one in scatters:
            one.step(stage)
    for one in chained:
        one.start()
    for number in range(1, chips):
        for one in transfers["gather"] + chained:
            one.step(number)
    for one in transfers["gather"] + chained + scatters:
        one.finish()


def plan_group_scatter(transfers, chips, bits):
    scatters, chained = transfers["group_scatter"], transfers["chained"]
    steps = [(one, stage) for one in scatters for stage in range(bits)]
    for one in scatters[:2]:
        one.start()
    waiting = list(scatters[2:])
    hops = []
    for one, stage in steps:
        one.step(stage)
        if stage == 0 and waiting:
            waiting.pop(0).start()
        at = scatters.index(one)
        if hops:
            hops.pop(0)()
        if stage == bits - 1 and at < len(chained):
            chained[at].start()
            hops += [functools.partial(chained[at].step, d) for d in range(1, chips)]
    for hop in hops:
        hop()
    for one in chained + scatters:
        one.finish()


def comm_params(number, limit=48):
    return pltpu.CompilerParams(
        collective_id=number, has_side_effects=True, vmem_limit_bytes=limit * 2**20
    )


def comm_cost(micros):
    return pl.CostEstimate(flops=0, bytes_accessed=int(micros * 3.4e4), transcendentals=0)


ANY = pl.BlockSpec(memory_space=pl.ANY)
VMEM = pl.BlockSpec(memory_space=pltpu.VMEM)


def after(values, *earlier):
    tied = lax.optimization_barrier((values, earlier))[0]
    return tied


class GroupSum:
    def __init__(self, partials, owners, group, flip):
        self.owners, self.group = owners, group
        self.partials = partials if isinstance(partials, list) else [partials]
        self.rows = self.partials[0].shape[0] // owners
        bits = list(range(owners.bit_length() - 1))
        self.order = bits[::-1] if flip else bits
        self.held = {piece: None for piece in range(owners)}

    def piece(self, number):
        if self.held[number] is not None:
            return self.held[number]
        start = (self.group ^ number) * self.rows
        slices = [lax.dynamic_slice_in_dim(p, start, self.rows, 0) for p in self.partials]
        return slices[0] if len(slices) == 1 else jnp.concatenate(slices, axis=1)

    def send(self):
        bit = self.order.pop(0)
        self.keep = [piece for piece in self.held if not piece >> bit & 1]
        self.sent = jnp.stack([self.piece(piece | 1 << bit) for piece in self.keep])
        pairs = [(i, i ^ 1 << bit) for i in range(self.owners)]
        self.got = lax.ppermute(self.sent, "group", pairs)
        return self.sent

    def add(self, *earlier):
        got = after(self.got, *earlier)
        self.held = {
            piece: (self.piece(piece).astype(F32) + got[at].astype(F32)).astype(BF16)
            for at, piece in enumerate(self.keep)
        }


def finish_all(sums):
    for one in sums:
        while one.order:
            one.send()
            one.add()


def send_all(sums):
    return [one.send() for one in sums]


def add_all(sums, *earlier):
    for one in sums:
        one.add(*earlier)


def widen_kernel(counts, *refs):
    sources, targets = refs[: len(counts)], refs[-sum(counts) :]
    at = 0
    for source, count in zip(sources, counts, strict=True):
        for number in range(count):
            targets[at][0, 0] = source[0, number].astype(F32)
            at += 1


def widen(packs, number, experts, previous=()):
    parts, unused, shard, width = packs[0].shape
    counts = [pack.shape[1] for pack in packs]
    total = sum(counts)
    shape = jax.ShapeDtypeStruct((parts, experts, shard, width), F32)
    block = pl.BlockSpec((1, 1, shard // 2, width), lambda c, h: (c, number, h, 0))
    return pl.pallas_call(
        functools.partial(widen_kernel, counts),
        out_shape=(shape,) * total,
        grid=(parts, 2),
        in_specs=[
            pl.BlockSpec((1, count, shard // 2, width), lambda c, h: (c, 0, h, 0))
            for count in counts
        ]
        + [ANY] * len(previous),
        out_specs=(block,) * total,
        input_output_aliases={len(packs) + i: i for i in range(len(previous))},
        cost_estimate=pl.CostEstimate(
            flops=0, bytes_accessed=sum(p.size for p in packs) // 16, transcendentals=0
        ),
        name="widen",
    )(*packs, *previous)


def finish_attention_kernel(
    sharers,
    packed_ref,
    small_ref,
    query_ref,
    key_ref,
    value_ref,
    gain_ref,
    q_ref,
    k_ref,
    v_ref,
    o_ref,
    router_ref,
    attention_ref,
    mixture_ref,
    qg_ref,
    kg_ref,
    rows_ref,
    sums_ref,
):
    shard, width = o_ref.shape
    share = 2 * HD // sharers
    at = pl.program_id(0)
    o_ref[...] = packed_ref[0, :, :width].astype(F32)
    query = packed_ref[0, :, width : 2 * width].astype(F32)
    q_ref[...] = query

    @pl.when(at == 0)
    def _():
        rows_ref[...] = jnp.zeros_like(rows_ref)
        sums_ref[...] = jnp.zeros_like(sums_ref)

    rows_ref[...] += small_ref[0, :, :shard].astype(F32)
    sums_ref[...] += jnp.sum(query * query_ref[...].astype(F32), axis=1, keepdims=True)
    for number in range(sharers):

        @pl.when(lax.rem(at, sharers) == number)
        def _():
            piece = packed_ref[0, :, 2 * width : 2 * width + share].astype(F32)
            start = number * share
            if start < HD:
                weight = key_ref[:, start : start + share]
                k_ref[:, start : start + share] = piece
            else:
                weight = value_ref[:, start - HD : start - HD + share]
                v_ref[:, start - HD : start - HD + share] = piece
            sums_ref[...] += jnp.sum(piece * weight.astype(F32), axis=1, keepdims=True)

    @pl.when(at == pl.num_programs(0) - 1)
    def _():
        router_ref[...] = rows_ref[:EXPERTS, :]
        mixture_ref[...] = rows_ref[EXPERTS : EXPERTS + 1, :]
        qg_ref[...] = rows_ref[EXPERTS + 1 : EXPERTS + 2, :]
        kg_ref[...] = rows_ref[EXPERTS + 2 : EXPERTS + 3, :]
        attention_ref[...] = jnp.transpose(sums_ref[...], (1, 0))[:1, :] / gain_ref[...]


def finish_attention(packed, weights, width, sharers):
    parts, tall, total = packed.shape
    shard = tall - SMALL
    head = pl.BlockSpec((shard, HD), lambda c: (0, c // sharers))
    own = pl.BlockSpec((shard, width), lambda c: (0, c))
    whole = lambda c: (0, 0)
    return pl.pallas_call(
        functools.partial(finish_attention_kernel, sharers),
        out_shape=(
            jax.ShapeDtypeStruct((shard, width * parts), F32),
            jax.ShapeDtypeStruct((shard, HK * HD), F32),
            jax.ShapeDtypeStruct((shard, HK * HD), F32),
            jax.ShapeDtypeStruct((shard, width * parts), F32),
            jax.ShapeDtypeStruct((EXPERTS, shard), F32),
        )
        + (jax.ShapeDtypeStruct((1, shard), F32),) * 4,
        grid_spec=pltpu.PrefetchScalarGridSpec(
            num_scalar_prefetch=0,
            grid=(parts,),
            in_specs=[
                pl.BlockSpec((1, shard, total), lambda c: (c, 0, 0)),
                pl.BlockSpec((1, SMALL, total), lambda c: (c, shard // SMALL, 0)),
                own,
                head,
                head,
                pl.BlockSpec((1, shard), whole),
            ],
            out_specs=(
                own,
                head,
                head,
                own,
                pl.BlockSpec((EXPERTS, shard), whole),
            )
            + (pl.BlockSpec((1, shard), whole),) * 4,
            scratch_shapes=[pltpu.VMEM((SMALL, shard), F32), pltpu.VMEM((shard, PAD), F32)],
        ),
        cost_estimate=pl.CostEstimate(flops=0, bytes_accessed=packed.size // 16, transcendentals=0),
        name="finish_attention",
    )(packed, packed, *weights)


def per_device(
    tokens,
    positions,
    expert_ids,
    cotangent,
    attention_gain,
    query_weight,
    key_weight,
    value_weight,
    output_weight,
    query_gain,
    key_gain,
    mixture_gain,
    router_weight,
    gate_weight,
    up_weight,
    down_weight,
):
    parts, owners = lax.axis_size("ctx"), lax.axis_size("group")
    here, group = lax.axis_index("ctx"), lax.axis_index("group")
    rows = tokens.shape[1]
    length = rows * parts
    shard = query_weight.shape[0]
    width = HQ * HD // parts
    experts = EXPERTS // parts
    sharers = parts // HK
    key_head = here // sharers
    share = 2 * HD // sharers
    share_at = (here % sharers) * share

    gather_group = lambda v: lax.all_gather(v, "group", axis=0, tiled=True)

    def columns(array, start, count):
        return lax.dynamic_slice_in_dim(array, start, count, 1)

    spread = lambda vector: jnp.pad(vector, (0, shard - vector.shape[0]))
    gain_rows = jnp.concatenate(
        [
            attention_gain,
            mixture_gain,
            spread(query_gain),
            spread(key_gain),
            jnp.zeros((12 * shard,), BF16),
        ]
    ).reshape(16, shard)
    comm = lambda plan, number, name, micros, **transfers: comm_call(
        plan, number, name, parts, owners, micros, **transfers
    )
    def expert_pack(number, at):
        return jnp.concatenate(
            [
                lax.dynamic_index_in_dim(w, at * experts + number, 0, keepdims=False)
                for w in (up_weight, down_weight)
            ],
            axis=1,
        )

    packs = [expert_pack(number, here) for number in range(experts)]
    gain_rows = after(gain_rows, *packs)

    def cut(start, count):
        return lambda ref: ref.at[:, pl.ds(pl.multiple_of(start(), count), count)]

    place = lambda: lax.axis_index("ctx")
    key_cut = cut(lambda: place() // sharers * HD, HD)
    own_cut = cut(lambda: place() * width, width)

    def gate_item(number):
        return (gate_weight, lambda ref: ref.at[place() * experts + number], (shard, F))


    inputs_all, positions_all, gain_rows, router, wquery, wkey, wvalue, wout = comm(
        plan_gather,
        0,
        "gather_tokens",
        45,
        gather=(tokens[0], jnp.broadcast_to(positions, (8, rows))),
        group_gather=(
            (gain_rows, lambda ref: ref, (16, shard)),
            (router_weight, lambda ref: ref, (shard, EXPERTS)),
            (query_weight, own_cut, (shard, width)),
            (key_weight, key_cut, (shard, HD)),
            (value_weight, key_cut, (shard, HD)),
            (output_weight, own_cut, (shard, width)),
        ),
    )
    packs = [gather_group(after(pack, positions_all)) for pack in packs]
    wqkv = jnp.concatenate([wquery, wkey, wvalue], axis=1)

    gain_rows = gain_rows.reshape(owners, 16, shard).astype(F32)
    attention_gains, mixture_gains = gain_rows[:, 0].reshape(D), gain_rows[:, 1].reshape(D)
    query_gains = gain_rows[:, 2, : HD // owners].reshape(1, HD)
    key_gains = gain_rows[:, 3, : HD // owners].reshape(1, HD)

    positions_all = positions_all.reshape(parts, 8, rows)[:, 0].reshape(length)
    doc_start = (jnp.arange(length, dtype=jnp.int32) - positions_all)[:, None]
    inputs = tokens[0].astype(F32)
    unused, attn_factor = rms_parts(inputs, attention_gains)
    normed_all = rms_parts(inputs_all.astype(F32), attention_gains)[0].astype(BF16)
    qkv_raw = dot(normed_all, wqkv)
    tables = (qkv_raw, doc_start, rope_tables(positions_all), query_gains, key_gains)
    mixed_low = attend(*tables)
    attn_out, upstream_all, first_gate = comm(
        plan_scatter,
        1,
        "scatter_attention",
        50,
        scatter=((mixed_low, wout),),
        gather=(cotangent[0],),
        group_gather=(gate_item(0),),
    )
    hidden = inputs + attn_out
    moe_normed, moe_factor = rms_parts(hidden, mixture_gains)
    moe_low = moe_normed.astype(BF16)
    logits = dot(moe_low, router)
    onehot = (
        expert_ids[0][:, :, None] == jnp.arange(EXPERTS, dtype=jnp.int32)[None, None, :]
    ).astype(F32)
    chosen = jnp.sum(onehot * logits[:, None, :], axis=-1)
    expo = jnp.exp(chosen - jnp.max(chosen, axis=-1, keepdims=True))
    gates = expo / jnp.sum(expo, axis=-1, keepdims=True)
    combine = jnp.sum(gates[:, :, None] * onehot, axis=1)
    moe_all, combine_all, *gates_all = comm(
        plan_gather,
        2,
        "gather_mixture",
        45,
        gather=(moe_low, jnp.pad(combine, ((0, 0), (0, PAD - EXPERTS)))),
        group_gather=[gate_item(number) for number in range(1, experts)],
    )
    gates_all = [first_gate, *gates_all]
    combine_all = columns(combine_all, here * experts, experts)

    def expert_forward(number, weights, gate_all):
        up_all = dot(moe_all, weights[1])
        sigmoid = lax.logistic(gate_all)
        act_low = (gate_all * sigmoid * up_all).astype(BF16)
        weighted = (combine_all[:, number : number + 1] * act_low.astype(F32)).astype(BF16)
        return gate_all, up_all, act_low, weighted

    def expert_back(number, gate_all, up_all, act_low, weights):
        back_all = dot(upstream_all, weights[2])
        sigmoid = lax.logistic(gate_all)
        combine_grad = jnp.sum(act_low.astype(F32) * back_all, axis=-1, keepdims=True)
        act_grad = combine_all[:, number : number + 1] * back_all
        gate_grad = (act_grad * up_all * sigmoid * (1.0 + gate_all * (1.0 - sigmoid))).astype(BF16)
        up_grad = (act_grad * gate_all * sigmoid).astype(BF16)
        return combine_grad, gate_grad, up_grad

    def weight_grad(left, right):
        return dot_tn(left, right).astype(BF16)

    split = lambda number, pack: (gates_all[number], pack[:, :F], pack[:, F:])
    weights = split(0, packs[0])
    gate_all = dot(moe_all, weights[0])
    gate_all, up_all, act_low, weighted = expert_forward(0, weights, gate_all)
    combine_grads, layer_terms, moe_terms, gathered = [], [], [], []
    last_grads = [weight_grad(upstream_all, weighted)]
    for number in range(1, experts):
        half = F // 2
        down_sums = [
            GroupSum(last_grads[0][:, :half], owners, group, False),
            GroupSum(last_grads[0][:, half:], owners, group, True),
        ]
        gate_all, up_all = after((gate_all, up_all), *send_all(down_sums))
        combine_grad, gate_grad, up_grad = expert_back(
            number - 1, gate_all, up_all, act_low, weights
        )
        combine_grads.append(combine_grad)
        layer_terms.append((weighted, weights[2]))
        moe_terms += [(gate_grad, weights[0]), (up_grad, weights[1])]
        grads = weight_grad(moe_all, gate_grad), weight_grad(moe_all, up_grad)
        layer_part = dot_nt(weighted, weights[2])
        add_all(down_sums, layer_part, *grads)
        sent = send_all(down_sums) if down_sums[0].order else []
        other_sums = [
            GroupSum(after(grads[0], *sent), owners, group, False),
            GroupSum(after(grads[1], *sent), owners, group, True),
        ]
        weights = split(number, after(packs[number], *send_all(other_sums)))
        gate_all = dot(moe_all, weights[0])
        add_all(down_sums, gate_all)
        finish_all(down_sums)
        down = jnp.concatenate([one.held[0] for one in down_sums], axis=1)
        weights = (weights[0], after(weights[1], down), weights[2])
        gate_all, up_all, act_low, weighted = expert_forward(number, weights, gate_all)
        last_grads = [weight_grad(upstream_all, weighted)]
        gathered.append([down.reshape(2, shard // 2, F), other_sums])
    combine_grad, gate_grad, up_grad = expert_back(
        experts - 1, gate_all, up_all, act_low, weights
    )
    combine_grads.append(combine_grad)
    layer_terms.append((weighted, weights[2]))
    moe_terms += [(gate_grad, weights[0]), (up_grad, weights[1])]
    for pieces in gathered:
        add_all(pieces[1], gate_grad, up_grad)
        if pieces[1][0].order:
            gate_grad, up_grad = after((gate_grad, up_grad), *send_all(pieces[1]))
    last_grads += [weight_grad(moe_all, gate_grad), weight_grad(moe_all, up_grad)]
    for pieces in gathered:
        add_all(pieces[1], *last_grads)
        finish_all(pieces[1])
        pieces[1] = jnp.stack([one.held[0] for one in pieces[1]])
        last_grads = list(after(last_grads, pieces[1]))
    half = F // 2
    last_sums = [
        GroupSum([last_grads[0][:, :half], last_grads[1]], owners, group, False),
        GroupSum([last_grads[0][:, half:], last_grads[2]], owners, group, True),
    ]
    moe_terms = after(moe_terms, *send_all(last_sums))
    moe_part = sum(dot_nt(left, right) for left, right in moe_terms[:2])
    layer_part = sum(dot_nt(left, right) for left, right in layer_terms)
    for left, right in moe_terms[2:]:
        moe_part = moe_part + dot_nt(left, right)
    moe_part_low = moe_part.astype(BF16)
    add_all(last_sums, moe_part_low)
    if last_sums[0].order:
        moe_part_low = after(moe_part_low, *send_all(last_sums))
    combine_grad = jnp.concatenate(combine_grads, axis=1)
    high = combine_grad.astype(BF16).astype(F32)
    low = combine_grad - high
    at = jnp.arange(PAD, dtype=jnp.int32)[None, :]
    small = sum(
        jnp.where(at == here * experts + number, high[:, number : number + 1], 0.0)
        + jnp.where(at == EXPERTS + here * experts + number, low[:, number : number + 1], 0.0)
        for number in range(experts)
    ).astype(BF16)
    moe_sum, small_sum = comm(
        plan_scatter, 3, "scatter_mixture", 60, scatter=((moe_part_low,), (small,))
    )
    add_all(last_sums, moe_sum)
    finish_all(last_sums)
    ends = [one.held[0] for one in last_sums]
    down = jnp.concatenate([end[:, :half] for end in ends], axis=1)
    gathered.append([jnp.stack([down] + [end[:, half:] for end in ends])])
    unfold = lambda piece: lax.all_gather(piece, "ctx").reshape(parts, -1, shard, F)
    expert_packs = [[unfold(piece) for piece in pieces] for pieces in gathered]

    dcombine = small_sum[:, :EXPERTS] + small_sum[:, EXPERTS : 2 * EXPERTS]
    gates_grad = jnp.sum(onehot * dcombine[:, None, :], axis=-1)
    chosen_grad = gates * (gates_grad - jnp.sum(gates * gates_grad, axis=-1, keepdims=True))
    logit_grad_low = jnp.sum(chosen_grad[:, :, None] * onehot, axis=1).astype(BF16)
    router_partial = dot_tn(moe_low, logit_grad_low)
    moe_grad = moe_sum + dot_nt(logit_grad_low, router)
    hidden_part, mixture_terms = rms_back(hidden, moe_factor, mixture_gains, moe_grad)
    mixture_partial = jnp.sum(mixture_terms, axis=0)
    hidden_grad = cotangent[0].astype(F32) + hidden_part

    (attn_grad_all,) = comm(
        plan_gather,
        4,
        "gather_attention",
        45,
        gather=(
            after(hidden_grad.astype(BF16), *(pack[0] for pack in expert_packs[:-1])),
        ),
    )
    mixed_grad = dot(attn_grad_all, wout).astype(BF16)
    output_partial = weight_grad(attn_grad_all, mixed_low)
    output_sums = [
        GroupSum(output_partial[:, : width // 2], owners, group, False),
        GroupSum(output_partial[:, width // 2 :], owners, group, True),
    ]
    mixed_grad = after(mixed_grad, *send_all(output_sums))
    query_low, kv_part, query_terms, key_terms = attend_back(*tables, mixed_grad)
    step = 1
    while step < sharers:
        kv_part = kv_part + lax.ppermute(kv_part, "ctx", [(i, i ^ step) for i in range(parts)])
        step *= 2
    kv_low = columns(kv_part.astype(BF16), share_at, share)
    qkv_low = jnp.concatenate([query_low, kv_low], axis=1)
    wqkv_share = jnp.concatenate(
        [wqkv[:, :width], columns(wqkv[:, width:], share_at, share)], axis=1
    )
    def head_column(terms):
        spread = terms.reshape(owners, HD // owners)
        return jnp.pad(spread, ((0, 0), (0, shard - HD // owners))).reshape(D, 1)

    add_all(output_sums, qkv_low)
    qkv_tied = qkv_low
    if output_sums[0].order:
        qkv_tied = after(qkv_low, *send_all(output_sums))
    spare = next(n for n in range(EXPERTS + 8, 1024) if (width + share + n) % 256 == 0)
    grad_extras = jnp.concatenate(
        [
            router_partial,
            mixture_partial[:, None],
            head_column(query_terms),
            head_column(key_terms),
        ],
        axis=1,
    )
    grad_extras = jnp.pad(grad_extras, ((0, 0), (width + share, spare - EXPERTS - 3)))
    qkv_wide = jnp.pad(qkv_tied, ((0, 0), (0, spare)))
    qkv_partial = (dot_tn(normed_all, qkv_wide) + grad_extras).astype(BF16)
    layer_sum, qkv_piece = comm(
        plan_scatter,
        6,
        "scatter_grads",
        60,
        scatter=((layer_part.astype(BF16),),),
        group_scatter=(after(qkv_partial, *(pack[-1] for pack in expert_packs[:-1])),),
    )
    layer_out = (hidden + layer_sum).astype(BF16)[None]
    add_all(output_sums, qkv_piece)
    finish_all(output_sums)
    wide = jnp.concatenate(
        [one.held[0] for one in output_sums] + [qkv_piece[:, : width + share]], axis=1
    )
    low_rows = jnp.pad(
        qkv_piece[:, width + share : width + share + EXPERTS + 3].T,
        ((0, SMALL - EXPERTS - 3), (0, wide.shape[1] - shard)),
    )
    attn_piece = jnp.concatenate([wide, low_rows], axis=0)
    attn_grads = lax.all_gather(attn_piece, "ctx")
    finished = ()
    for number in range(experts):
        finished = widen(expert_packs[number], number, experts, finished)
    (normed_grad,) = comm(
        plan_scatter,
        5,
        "scatter_normed",
        60,
        scatter=((after(qkv_low, attn_piece, *finished), wqkv_share),),
    )
    input_part, unused = rms_back(inputs, attn_factor, attention_gains, normed_grad)
    tokens_grad = (hidden_grad + input_part).astype(BF16)[None]
    query_grad, key_grad, value_grad, output_grad, router_grad, *gain_grads = finish_attention(
        attn_grads,
        (query_weight, key_weight, value_weight, attention_gain.astype(F32).reshape(1, shard)),
        width,
        sharers,
    )
    whole = lambda v: v.reshape(EXPERTS, shard, F)
    return (
        layer_out,
        tokens_grad,
        gain_grads[0].reshape(shard),
        query_grad,
        key_grad,
        value_grad,
        output_grad,
        gain_grads[2][0, : HD // owners],
        gain_grads[3][0, : HD // owners],
        gain_grads[1].reshape(shard),
        router_grad.T,
        whole(finished[1]),
        whole(finished[2]),
        whole(finished[0]),
    )


def solution(mesh):
    return jax.shard_map(
        per_device,
        mesh=mesh,
        in_specs=(
            P("group", "ctx", None),
            P("group", "ctx"),
            P("group", "ctx", None),
            P("group", "ctx", None),
            P("group"),
            P("group", None),
            P("group", None),
            P("group", None),
            P("group", None),
            P("group"),
            P("group"),
            P("group"),
            P("group", None),
            P(None, "group", None),
            P(None, "group", None),
            P(None, "group", None),
        ),
        out_specs=(
            P("group", "ctx", None),
            P("group", "ctx", None),
            P("group"),
            P("group", None),
            P("group", None),
            P("group", None),
            P("group", None),
            P("group"),
            P("group"),
            P("group"),
            P("group", None),
            P(None, "group", None),
            P(None, "group", None),
            P(None, "group", None),
        ),
        check_vma=False,
    )
```
